32 devices in a mesh: dp: 16 (over z, x, core), head: 2 (over y).
Axes of the slice: x: 2, y: 2, z: 4, core: 2. Of those that a mesh axis runs over, the one named last changes fastest.
Arguments:
- layer_input: bfloat16 [16384, 1152], P(('dp', 'head')), may hold values from -6 to 6
- seq_lengths: int32 [16, 4], P('dp'), may hold values from 0 to 1024, as said below
- input_gain: float32 [1152], replicated, may hold values from -0.4 to 0.4
- query_weight: bfloat16 [1152, 1024], P(None, 'head'), may hold values from -0.1875 to 0.1875
- key_weight: bfloat16 [1152, 256], replicated, may hold values from -0.1875 to 0.1875
- value_weight: bfloat16 [1152, 256], replicated, may hold values from -0.1875 to 0.1875
- query_gain: float32 [256], replicated, may hold values from -0.4 to 0.4
- key_gain: float32 [256], replicated, may hold values from -0.4 to 0.4
- output_weight: bfloat16 [1152, 1024], P(None, 'head'), may hold values from -0.1875 to 0.1875
- post_attn_gain: float32 [1152], replicated, may hold values from -0.4 to 0.4
- pre_ffn_gain: float32 [1152], replicated, may hold values from -0.4 to 0.4
- gate_weight: bfloat16 [1152, 6912], P(None, 'head'), may hold values from -0.1875 to 0.1875
- up_weight: bfloat16 [1152, 6912], P(None, 'head'), may hold values from -0.1875 to 0.1875
- down_weight: bfloat16 [1152, 6912], P(None, 'head'), may hold values from -0.078125 to 0.078125
- post_ffn_gain: float32 [1152], replicated, may hold values from -0.4 to 0.4
- out_cotangent: bfloat16 [16384, 1152], P(('dp', 'head')), may hold values from -6 to 6
Outputs:
- layer_output: bfloat16 [16384, 1152], P(('dp', 'head'))
- input_grad: bfloat16 [16384, 1152], P(('dp', 'head'))
- input_gain_grad: float32 [1152], P('dp')
- query_weight_grad: float32 [1152, 1024], P('dp', 'head')
- key_weight_grad: float32 [1152, 256], P('dp')
- value_weight_grad: float32 [1152, 256], P('dp')
- query_gain_grad: float32 [256], P('dp')
- key_gain_grad: float32 [256], P('dp')
- output_weight_grad: float32 [1152, 1024], P('dp', 'head')
- post_attn_gain_grad: float32 [1152], P('dp')
- pre_ffn_gain_grad: float32 [1152], P('dp')
- gate_weight_grad: float32 [1152, 6912], P('dp', 'head')
- up_weight_grad: float32 [1152, 6912], P('dp', 'head')
- down_weight_grad: float32 [1152, 6912], P('dp', 'head')
- post_ffn_gain_grad: float32 [1152], P('dp')
The draws below stay inside these ranges and needn't reach their ends.
Inputs may be any that keep to these rules, and one draw needn't show every extreme that they name: `seq_lengths`: row b lists bucket b's sequences in order, packed from its first token; they sum to at most 1024 and the rest of the bucket is padding; a length may be 0. In every draw some bucket holds a single sequence of 1024 tokens.
All inputs are finite; a program needn't handle non-finite values.
Results may differ from the reference program's by a relative error of at most 0.023.
Values may be sent and summed in bfloat16 or wider, within the bound.
No kernel may reach another device: no remote copies, remote signals or barrier semaphores. Data moves between devices by JAX's collectives and lax.ppermute only.
A program may use at most 256 MiB of HBM per device.

```python
import jax
import jax.numpy as jnp
from jax import lax

D = 1152
HQ = 4
HD = 256
FF = 6912
SEQS = 4
BUCKET = 1024
BUCKETS = 16
TOKENS = 16384
N_DP = 16
N_HEAD = 2


def draw_seq_lengths(key, part):
    key_list = jax.random.split(key, 3)
    exponent = jax.random.randint(key_list[0], (BUCKETS, SEQS), 0, 4)
    divisor = jnp.power(2, exponent).astype(jnp.int32)
    longest = BUCKET // divisor
    shorten = jax.random.randint(key_list[1], (BUCKETS, SEQS), 0, BUCKET // (2 * divisor) + 1)
    wanted = (longest - shorten).astype(jnp.int32)
    before = (jnp.cumsum(wanted, axis=1) - wanted).astype(jnp.int32)
    room = jnp.maximum(BUCKET - before, 0)
    taken = jnp.minimum(wanted, room)
    full_bucket = jax.random.randint(key_list[2], (), 0, BUCKETS)
    single = jnp.where(jnp.arange(SEQS) == 0, BUCKET, 0)
    chosen = jnp.arange(BUCKETS)[:, None] == full_bucket
    return jnp.where(chosen, single[None, :], taken).astype(jnp.int32)


def strengthened(drawn, own_key, source, target, shards_of, factor):
    def block_of(dim):
        return (jnp.arange(drawn.shape[dim]) // (drawn.shape[dim] // shards_of)).reshape((-1,) + (1,) * (drawn.ndim - 1 - dim))

    first = jax.random.permutation(own_key, shards_of)[block_of(target)]
    other_side = (block_of(target) + shards_of // 2) % shards_of
    return jnp.where((block_of(source) == first) | (block_of(source) == other_side), factor * drawn, drawn)


def block_scale(key, shape, cuts, smallest, top_value):
    def one(dim, shards_of):
        draws = jax.random.uniform(jax.random.fold_in(jax.random.fold_in(key, 6), dim), (shards_of,), jnp.float32, smallest / len(cuts), top_value / len(cuts))
        return jnp.repeat(jnp.exp(draws), shape[dim] // shards_of).reshape((-1,) + (1,) * (len(shape) - dim - 1))

    loudness = one(*cuts[0])
    for cut in cuts[1:]:
        loudness = loudness * one(*cut)
    return loudness


def gaussian(stream_key, extent, deviation, most, cuts=(), kind=jnp.bfloat16):
    drawn = deviation * jax.random.normal(stream_key, extent, jnp.float32)
    if cuts:
        drawn = drawn * block_scale(stream_key, extent, cuts, -0.22, 0.18)
    return jnp.clip(drawn, -most, most).astype(kind)


def gaussian_with(rng, extent, deviation, bound, cuts, heavy, kind=jnp.bfloat16):
    values = deviation * jax.random.normal(rng, extent, jnp.float32)
    if cuts:
        values = values * block_scale(rng, extent, cuts, -0.22, 0.18)
    return jnp.clip(strengthened(values, jax.random.fold_in(rng, 3), *heavy), -bound, bound).astype(kind)


def setup_inputs(seed: int = 0) -> dict:
    arg_keys = jax.random.split(jax.random.key(seed), 17)
    layer_input = gaussian_with(arg_keys[0], (TOKENS, D), 1.0, 6.0, ((0, 32),), (0, 1, 32, 2.75))
    seq_lengths = draw_seq_lengths(jax.random.fold_in(arg_keys[16], 71), 0)
    input_gain = jnp.clip(jax.random.uniform(arg_keys[2], (D,), jnp.float32, -0.4, 0.4), -0.4, 0.4)
    query_weight = gaussian(arg_keys[3], (D, HQ * HD), D ** -0.5, 0.1875, ((1, 2),))
    key_weight = gaussian(arg_keys[4], (D, HD), D ** -0.5, 0.1875)
    value_weight = gaussian(arg_keys[5], (D, HD), D ** -0.5, 0.1875)
    query_gain = jnp.clip(jax.random.uniform(arg_keys[6], (HD,), jnp.float32, -0.4, 0.4), -0.4, 0.4)
    key_gain = jnp.clip(jax.random.uniform(arg_keys[7], (HD,), jnp.float32, -0.4, 0.4), -0.4, 0.4)
    output_weight = gaussian(arg_keys[8], (D, HQ * HD), (HQ * HD) ** -0.5, 0.1875, ((1, 2),))
    post_attn_gain = jnp.clip(jax.random.uniform(arg_keys[9], (D,), jnp.float32, -0.4, 0.4), -0.4, 0.4)
    pre_ffn_gain = jnp.clip(jax.random.uniform(arg_keys[10], (D,), jnp.float32, -0.4, 0.4), -0.4, 0.4)
    gate_weight = gaussian(arg_keys[11], (D, FF), D ** -0.5, 0.1875, ((1, 2),))
    up_weight = gaussian(arg_keys[12], (D, FF), D ** -0.5, 0.1875, ((1, 2),))
    down_weight = gaussian(arg_keys[13], (D, FF), FF ** -0.5, 0.078125, ((1, 2),))
    post_ffn_gain = jnp.clip(jax.random.uniform(arg_keys[14], (D,), jnp.float32, -0.4, 0.4), -0.4, 0.4)
    out_cotangent = gaussian_with(arg_keys[15], (TOKENS, D), 1.0, 6.0, ((0, 32),), (0, 1, 32, 2.75))
    return dict(layer_input=layer_input, seq_lengths=seq_lengths, input_gain=input_gain, query_weight=query_weight, key_weight=key_weight, value_weight=value_weight, query_gain=query_gain, key_gain=key_gain, output_weight=output_weight, post_attn_gain=post_attn_gain, pre_ffn_gain=pre_ffn_gain, gate_weight=gate_weight, up_weight=up_weight, down_weight=down_weight, post_ffn_gain=post_ffn_gain, out_cotangent=out_cotangent)


EPSILON = 1e-06
ROPE_BASE = 1000000.0
NEG_FILL = -1e+30

@jax.custom_vjp
def low(v):
    return lax.optimization_barrier(v.astype(jnp.bfloat16)).astype(jnp.float32)

@jax.custom_vjp
def low_back(v):
    return v

def low_keep(v):
    return (low(v), None)

def low_pass(kept, grad):
    return (grad,)

def back_keep(v):
    return (v, None)

def back_low(kept, grad):
    return (low(grad),)
low.defvjp(low_keep, low_pass)
low_back.defvjp(back_keep, back_low)

def matmul(left, right):
    return jnp.dot(left, right, precision=lax.Precision.HIGHEST, preferred_element_type=jnp.float32)

def normed(values, gain_vec):
    return values * lax.rsqrt(lax.optimization_barrier(jnp.mean(values * values, axis=-1, keepdims=True)) + EPSILON) * (1.0 + gain_vec)

def rotary(values, cosine, sine_table):
    half_width = values.shape[-1] // 2
    first_half = values[..., :half_width]
    second_half = values[..., half_width:]
    return jnp.concatenate([first_half * cosine - second_half * sine_table, second_half * cosine + first_half * sine_table], axis=-1)

def angle_tables(position, head_dim):
    frequency = ROPE_BASE ** (-2.0 * jnp.arange(head_dim // 2, dtype=jnp.float32) / head_dim)
    angle_grid = position.astype(jnp.float32)[:, None] * frequency[None, :]
    return (jnp.cos(angle_grid), jnp.sin(angle_grid))

def seq_tables(bucket_lens, bucket_rows):
    bucket_lens = bucket_lens.astype(jnp.int32)
    slot_total = bucket_lens.shape[0]
    seq_ends = jnp.cumsum(bucket_lens).astype(jnp.int32)
    token_ids = jnp.arange(bucket_rows, dtype=jnp.int32)
    segment = lax.optimization_barrier(jnp.sum((seq_ends[None, :] <= token_ids[:, None]).astype(jnp.int32), axis=1)).astype(jnp.int32)
    slot_ids = jnp.arange(slot_total, dtype=jnp.int32)
    seq_begin = lax.optimization_barrier(jnp.sum(jnp.where(slot_ids[None, :] < segment[:, None], bucket_lens[None, :], 0), axis=1)).astype(jnp.int32)
    position = (token_ids - seq_begin).astype(jnp.int32)
    visible = (token_ids[None, :] == token_ids[:, None]) | (token_ids[None, :] < token_ids[:, None]) & (segment[None, :] == segment[:, None]) & (segment[:, None] < slot_total)
    return (position, visible)

def layer(input_f32, weights, cosine, sine_table, visible):
    in_gain, w_query, w_key, w_value, gain_query, gain_key, w_output, gain_post_attn, gain_pre_ffn, w_gate, w_up, w_down, gain_post_ffn = weights
    normed_in = low(normed(input_f32, in_gain))
    q_raw = low_back(matmul(normed_in, w_query))
    k_raw = matmul(normed_in, w_key)
    v_raw = matmul(normed_in, w_value)
    queries = low(rotary(normed(q_raw.reshape(BUCKET, HQ, HD), gain_query), cosine[:, None, :], sine_table[:, None, :]))
    per_group = HQ // N_HEAD
    pieces = []
    for group_idx in range(N_HEAD):
        key_g = low(rotary(normed(low_back(k_raw), gain_key), cosine, sine_table))
        val_g = low(low_back(v_raw))
        query_group = queries[:, group_idx * per_group:(group_idx + 1) * per_group]
        scores = low_back(jnp.einsum('qhd,kd->hqk', query_group, key_g, precision=lax.Precision.HIGHEST) * HD ** (-0.5))
        scores = jnp.where(visible[None], scores, NEG_FILL)
        row_max = lax.optimization_barrier(jnp.max(scores, axis=-1, keepdims=True))
        exp_scores = jnp.exp(scores - row_max)
        prob_low = low(exp_scores / lax.optimization_barrier(jnp.sum(exp_scores, axis=-1, keepdims=True)))
        pieces.append(jnp.einsum('hqk,kd->qhd', prob_low, val_g, precision=lax.Precision.HIGHEST))
    attn_out = low(low_back(jnp.concatenate(pieces, axis=1).reshape(BUCKET, HQ * HD)))
    attn_proj = low_back(jnp.einsum('tc,dc->td', attn_out, w_output, precision=lax.Precision.HIGHEST))
    hidden_state = input_f32 + normed(attn_proj, gain_post_attn)
    ffn_in = low(normed(hidden_state, gain_pre_ffn))
    gate_pre = low_back(matmul(ffn_in, w_gate))
    up_pre = low_back(matmul(ffn_in, w_up))
    hidden = low(jax.nn.gelu(gate_pre, approximate=True) * up_pre)
    ffn_proj = low_back(jnp.einsum('tf,df->td', hidden, w_down, precision=lax.Precision.HIGHEST))
    return hidden_state + normed(ffn_proj, gain_post_ffn)

def reference(layer_input, seq_lengths, input_gain, query_weight, key_weight, value_weight, query_gain, key_gain, output_weight, post_attn_gain, pre_ffn_gain, gate_weight, up_weight, down_weight, post_ffn_gain, out_cotangent):
    params = (input_gain.astype(jnp.float32), query_weight.astype(jnp.float32), key_weight.astype(jnp.float32), value_weight.astype(jnp.float32), query_gain.astype(jnp.float32), key_gain.astype(jnp.float32), output_weight.astype(jnp.float32), post_attn_gain.astype(jnp.float32), pre_ffn_gain.astype(jnp.float32), gate_weight.astype(jnp.float32), up_weight.astype(jnp.float32), down_weight.astype(jnp.float32), post_ffn_gain.astype(jnp.float32))
    scan_items = (layer_input.reshape(N_DP, BUCKET, D), out_cotangent.reshape(N_DP, BUCKET, D), seq_lengths)

    def bucket_step(grad_sums, bucket_item):
        bucket_in, bucket_cot, bucket_lens = bucket_item
        position, visible = seq_tables(bucket_lens, BUCKET)
        cosine, sine_table = angle_tables(position, HD)

        def forward(input_f32, *weights):
            return layer(input_f32, weights, cosine, sine_table, visible)
        result, pullback = jax.vjp(forward, bucket_in.astype(jnp.float32), *params)
        gradients = pullback(bucket_cot.astype(jnp.float32))
        grad_sums = tuple((running + fresh for running, fresh in zip(grad_sums, gradients[1:])))
        return (grad_sums, (result.astype(jnp.bfloat16), gradients[0].astype(jnp.bfloat16)))
    zero_grads = tuple((jnp.zeros_like(weight_arr) for weight_arr in params))
    grad_sums, (outputs, input_grads) = lax.scan(bucket_step, zero_grads, scan_items)
    return (outputs.reshape(TOKENS, D), input_grads.reshape(TOKENS, D), grad_sums[0], grad_sums[1], grad_sums[2], grad_sums[3], grad_sums[4], grad_sums[5], grad_sums[6], grad_sums[7], grad_sums[8], grad_sums[9], grad_sums[10], grad_sums[11], grad_sums[12])
```

```python
import jax
import jax.numpy as jnp
from jax import lax
from jax.sharding import PartitionSpec as P

HD = 256
EPSILON = 1e-06
ROPE_BASE = 1000000.0
NEG_FILL = -1e30
LOW = jnp.bfloat16
F32 = jnp.float32


def normed(values, gain_vec):
    return (
        values
        * lax.rsqrt(jnp.mean(values * values, axis=-1, keepdims=True) + EPSILON)
        * (1.0 + gain_vec)
    )


def rotary(values, cosine, sine_table):
    half_width = values.shape[-1] // 2
    first_half = values[..., :half_width]
    second_half = values[..., half_width:]
    return jnp.concatenate(
        [
            first_half * cosine - second_half * sine_table,
            second_half * cosine + first_half * sine_table,
        ],
        axis=-1,
    )


def angle_tables(position, head_dim):
    frequency = ROPE_BASE ** (-2.0 * jnp.arange(head_dim // 2, dtype=F32) / head_dim)
    angle_grid = position.astype(F32)[:, None] * frequency[None, :]
    return (jnp.cos(angle_grid), jnp.sin(angle_grid))


def seq_tables(bucket_lens, token_ids):
    seq_ends = jnp.cumsum(bucket_lens)
    segment = jnp.sum((seq_ends[None, :] <= token_ids[:, None]).astype(jnp.int32), axis=1)
    slot_ids = jnp.arange(bucket_lens.shape[0], dtype=jnp.int32)
    seq_begin = jnp.sum(
        jnp.where(slot_ids[None, :] < segment[:, None], bucket_lens[None, :], 0), axis=1
    )
    return segment, token_ids - seq_begin


def gelu_gate(gate_pre, up_pre):
    return jax.nn.gelu(gate_pre, approximate=True) * up_pre


def dot(left, right):
    return jnp.dot(left, right, preferred_element_type=F32)


def row_dot(left, right):
    return jnp.einsum("tc,dc->td", left, right, preferred_element_type=F32)


def col_dot(left, right):
    return jnp.einsum("td,tc->dc", left, right, preferred_element_type=F32)


def swap_head(value):
    return lax.ppermute(value, "head", [(0, 1), (1, 0)])


def pair(axis_size, bit):
    return [(i, i ^ (1 << bit)) for i in range(axis_size)]


def scatter_bits(parts, bits, axis_size, index, low=LOW):
    count = axis_size.bit_length() - 1
    rows = parts[0].shape[0] // axis_size
    parts = [p.reshape((2,) * count + (rows,) + p.shape[1:]) for p in parts]
    left = list(range(count - 1, -1, -1))

    def take(p, dim, which):
        return lax.dynamic_index_in_dim(p, which, axis=dim, keepdims=False)

    for bit in bits:
        dim = left.index(bit)
        mine = (index >> bit) & 1
        send = sum(take(p, dim, 1 - mine).astype(F32) for p in parts).astype(low)
        got = lax.ppermute(send, "dp", pair(axis_size, bit))
        parts = [take(p, dim, mine) for p in parts] + [got]
        left.remove(bit)
    return parts


def finish(parts):
    return sum(p.astype(F32) for p in parts)


def on_device(
    layer_input,
    seq_lengths,
    input_gain,
    query_weight,
    key_weight,
    value_weight,
    query_gain,
    key_gain,
    output_weight,
    post_attn_gain,
    pre_ffn_gain,
    gate_weight,
    up_weight,
    down_weight,
    post_ffn_gain,
    out_cotangent,
):
    rows = layer_input.shape[0]
    dp_size = lax.axis_size("dp")
    bit_count = dp_size.bit_length() - 1
    dp_index = lax.axis_index("dp")
    head_index = lax.axis_index("head")
    core = dp_index & 1
    core_pairs = pair(dp_size, 0)
    slot_total = seq_lengths.shape[1]
    width = query_weight.shape[1]
    head_total = 2 * width // HD
    score_scale = HD ** (-0.5)

    def fetch_columns(weight):
        mine = lax.dynamic_slice_in_dim(weight, core * HD, HD, axis=1)
        first = swap_head(mine)
        second = lax.ppermute(first, "dp", core_pairs)
        return first, second

    query_first, query_second = fetch_columns(query_weight)
    output_first, output_second = fetch_columns(output_weight)

    own_ids = head_index * rows + jnp.arange(rows, dtype=jnp.int32)
    before_ids = jnp.where(head_index > 0, jnp.arange(rows, dtype=jnp.int32), -1)
    segment, position = seq_tables(seq_lengths[0], own_ids)
    before_segment, _ = seq_tables(seq_lengths[0], before_ids)
    before_segment = jnp.where(head_index > 0, before_segment, -1)
    key_ids = jnp.concatenate([before_ids, own_ids])
    key_segment = jnp.concatenate([before_segment, segment])
    visible = (key_ids[None, :] == own_ids[:, None]) | (
        (key_ids[None, :] < own_ids[:, None])
        & (key_segment[None, :] == segment[:, None])
        & (segment[:, None] < slot_total)
    )
    cosine, sine_table = angle_tables(position, HD)

    input_f32 = layer_input.astype(F32)
    normed_local, input_pull = jax.vjp(normed, input_f32, input_gain)
    normed_in = normed_local.astype(LOW)
    k_raw = dot(normed_in, key_weight)
    v_raw = dot(normed_in, value_weight)

    def query_path(raw_in, gain_vec):
        return rotary(normed(raw_in, gain_vec), cosine[:, None, :], sine_table[:, None, :])

    def key_path(raw_in, gain_vec):
        return rotary(normed(raw_in, gain_vec), cosine, sine_table)

    k_rot, key_pull = jax.vjp(key_path, k_raw, key_gain)
    kv_own = jnp.concatenate([k_rot.astype(LOW), v_raw.astype(LOW)], axis=1)
    kv_before = lax.ppermute(kv_own, "head", [(0, 1)])
    kv_all = jnp.concatenate([kv_before, kv_own], axis=0)
    k_low = kv_all[:, :HD]
    v_low = kv_all[:, HD:]

    q_raw = jnp.concatenate(
        [dot(normed_in, query_weight), dot(normed_in, query_first), dot(normed_in, query_second)],
        axis=1,
    )
    q_rot, query_pull = jax.vjp(query_path, q_raw.reshape(rows, head_total, HD), query_gain)
    q_low = q_rot.astype(LOW)

    scores = jnp.einsum("qhd,kd->hqk", q_low, k_low, preferred_element_type=F32) * score_scale
    scores = jnp.where(visible[None], scores, NEG_FILL)
    row_max = jnp.max(scores, axis=-1, keepdims=True)
    exp_scores = jnp.exp(scores - row_max)
    row_total = jnp.sum(exp_scores, axis=-1, keepdims=True)
    prob_low = (exp_scores / row_total).astype(LOW)
    log_total = row_max + jnp.log(row_total)
    attn_out = (
        jnp.einsum("hqk,kd->qhd", prob_low, v_low, preferred_element_type=F32)
        .reshape(rows, head_total * HD)
        .astype(LOW)
    )
    attn_proj = (
        row_dot(attn_out[:, :width], output_weight)
        + row_dot(attn_out[:, width : width + HD], output_first)
        + row_dot(attn_out[:, width + HD :], output_second)
    )
    attn_branch, post_attn_pull = jax.vjp(normed, attn_proj, post_attn_gain)
    hidden_state = input_f32 + attn_branch
    ffn_local, pre_ffn_pull = jax.vjp(normed, hidden_state, pre_ffn_gain)
    grad_out = out_cotangent.astype(F32)

    own_in = ffn_local.astype(LOW)
    other_in = swap_head(own_in)

    def up_part(ffn_in):
        gate_pre = dot(ffn_in, gate_weight)
        up_pre = dot(ffn_in, up_weight)
        hidden_f32 = gelu_gate(gate_pre, up_pre)
        return gate_pre.astype(LOW), up_pre.astype(LOW), hidden_f32.astype(LOW)

    own_gate, own_up, own_hidden = up_part(own_in)
    other_gate, other_up, other_hidden = up_part(other_in)
    other_proj = swap_head(row_dot(other_hidden, down_weight).astype(LOW))
    ffn_proj = row_dot(own_hidden, down_weight) + other_proj.astype(F32)
    ffn_branch, post_ffn_pull = jax.vjp(normed, ffn_proj, post_ffn_gain)
    layer_output = (hidden_state + ffn_branch).astype(LOW)
    ffn_grad_local, grad_post_ffn = post_ffn_pull(grad_out)
    own_fgrad = ffn_grad_local.astype(LOW)
    other_fgrad = swap_head(own_fgrad)

    def back_part(fgrad, gate_low, up_low):
        hidden_grad = dot(fgrad, down_weight)
        _, pull = jax.vjp(gelu_gate, gate_low.astype(F32), up_low.astype(F32))
        gate_grad, up_grad = pull(hidden_grad)
        return gate_grad.astype(LOW), up_grad.astype(LOW)

    own_ggrad, own_ugrad = back_part(own_fgrad, own_gate, own_up)
    other_ggrad, other_ugrad = back_part(other_fgrad, other_gate, other_up)
    other_zgrad = swap_head(
        (row_dot(other_ggrad, gate_weight) + row_dot(other_ugrad, up_weight)).astype(LOW)
    )
    own_zgrad = row_dot(own_ggrad, gate_weight) + row_dot(own_ugrad, up_weight)

    def weight_grad(left_own, left_other, right_own, right_other):
        left = jnp.concatenate([left_own, left_other], axis=0)
        right = jnp.concatenate([right_own, right_other], axis=0)
        return col_dot(left, right).astype(LOW)

    grad_down = weight_grad(own_fgrad, other_fgrad, own_hidden, other_hidden)
    grad_gate = weight_grad(own_in, other_in, own_ggrad, other_ggrad)
    grad_up = weight_grad(own_in, other_in, own_ugrad, other_ugrad)

    ffn_in_grad = own_zgrad + other_zgrad.astype(F32)
    state_grad_norm, grad_pre_ffn = pre_ffn_pull(ffn_in_grad)
    state_grad = grad_out + state_grad_norm
    attn_grad_local, grad_post_attn = post_attn_pull(state_grad)
    attn_grad = attn_grad_local.astype(LOW)

    heads_grad = jnp.concatenate(
        [dot(attn_grad, output_weight), dot(attn_grad, output_first), dot(attn_grad, output_second)],
        axis=1,
    )
    heads_grad = heads_grad.reshape(rows, head_total, HD).astype(LOW)
    scores = jnp.einsum("qhd,kd->hqk", q_low, k_low, preferred_element_type=F32) * score_scale
    scores = jnp.where(visible[None], scores, NEG_FILL)
    prob_f32 = jnp.exp(scores - log_total)
    prob_low = prob_f32.astype(LOW)
    prob_grad = jnp.einsum("qhd,kd->hqk", heads_grad, v_low, preferred_element_type=F32)
    row_delta = jnp.sum(prob_f32 * prob_grad, axis=-1, keepdims=True)
    score_grad = (prob_f32 * (prob_grad - row_delta)).astype(LOW)
    q_grad = jnp.einsum("hqk,kd->qhd", score_grad, k_low, preferred_element_type=F32) * score_scale
    k_grad = jnp.einsum("hqk,qhd->kd", score_grad, q_low, preferred_element_type=F32) * score_scale
    v_grad = jnp.einsum("hqk,qhd->kd", prob_low, heads_grad, preferred_element_type=F32)
    kv_grad = jnp.concatenate([k_grad, v_grad], axis=1)
    kv_back = lax.ppermute(kv_grad[:rows].astype(LOW), "head", [(1, 0)])
    kv_grad = kv_grad[rows:] + kv_back.astype(F32)
    query_raw_grad, grad_query_gain = query_pull(q_grad)
    key_raw_grad, grad_key_gain = key_pull(kv_grad[:, :HD])
    query_grad_low = query_raw_grad.reshape(rows, head_total * HD).astype(LOW)
    key_grad_low = key_raw_grad.astype(LOW)
    value_grad_low = kv_grad[:, HD:].astype(LOW)

    def in_order(two_heads):
        first, second = two_heads[:, :HD], two_heads[:, HD:]
        return jnp.where(
            core == 0,
            jnp.concatenate([first, second], axis=1),
            jnp.concatenate([second, first], axis=1),
        )

    def split_grad(left, right_heads, transposed):
        kept = right_heads[:, :width]
        sent = in_order(right_heads[:, width:])
        return col_dot(left, kept).astype(LOW), col_dot(left, sent).astype(LOW)

    output_kept, output_sent = split_grad(attn_grad, attn_out, False)
    query_kept, query_sent = split_grad(normed_in, query_grad_low, False)
    grad_kv = col_dot(normed_in, jnp.concatenate([key_grad_low, value_grad_low], axis=1)).astype(LOW)

    normed_grad = (
        row_dot(query_grad_low[:, :width], query_weight)
        + row_dot(query_grad_low[:, width : width + HD], query_first)
        + row_dot(query_grad_low[:, width + HD :], query_second)
        + row_dot(key_grad_low, key_weight)
        + row_dot(value_grad_low, value_weight)
    )
    input_grad_norm, grad_in_gain = input_pull(normed_grad)
    input_grad = (state_grad + input_grad_norm).astype(LOW)

    order = list(range(bit_count))

    def reduce_weight(grad):
        return finish(scatter_bits([grad], order, dp_size, dp_index))

    def reduce_split(kept, sent):
        return reduce_weight(kept.astype(F32) + swap_head(sent).astype(F32))

    down_part = reduce_weight(grad_down)
    gate_part = reduce_weight(grad_gate)
    up_part_out = reduce_weight(grad_up)
    output_part = reduce_split(output_kept, output_sent)
    query_part = reduce_split(query_kept, query_sent)

    gains = [grad_in_gain, grad_post_attn, grad_pre_ffn, grad_post_ffn, grad_query_gain, grad_key_gain]
    gains = [g.reshape(dp_size, -1) for g in gains]
    gain_widths = [g.shape[1] for g in gains]
    packed = jnp.concatenate(gains, axis=1)
    packed = finish(scatter_bits([packed], order, dp_size, dp_index, F32)).reshape(-1)
    kv_sum = reduce_weight(grad_kv)
    kv_sum = kv_sum + swap_head(kv_sum)
    packed = packed + swap_head(packed)
    pieces = []
    start = 0
    for gain_width in gain_widths:
        pieces.append(packed[start : start + gain_width])
        start += gain_width
    return (
        layer_output,
        input_grad,
        pieces[0],
        query_part,
        kv_sum[:, :HD],
        kv_sum[:, HD:],
        pieces[4],
        pieces[5],
        output_part,
        pieces[1],
        pieces[2],
        gate_part,
        up_part_out,
        down_part,
        pieces[3],
    )


def solution(mesh):
    placed = (
        P(("dp", "head"), None),
        P("dp", None),
        P(),
        P(None, "head"),
        P(),
        P(),
        P(),
        P(),
        P(None, "head"),
        P(),
        P(),
        P(None, "head"),
        P(None, "head"),
        P(None, "head"),
        P(),
        P(("dp", "head"), None),
    )
    return jax.shard_map(
        on_device,
        mesh=mesh,
        in_specs=placed,
        out_specs=(
            P(("dp", "head"), None),
            P(("dp", "head"), None),
            P("dp"),
            P("dp", "head"),
            P("dp", None),
            P("dp", None),
            P("dp"),
            P("dp"),
            P("dp", "head"),
            P("dp"),
            P("dp"),
            P("dp", "head"),
            P("dp", "head"),
            P("dp", "head"),
            P("dp"),
        ),
        check_vma=False,
    )
```

```python
import jax
import jax.numpy as jnp
import numpy as np
from jax import lax
from jax.experimental import pallas as pl
from jax.experimental.pallas import tpu as pltpu
from jax.sharding import PartitionSpec as P

HD = 256
EPSILON = 1e-06
ROPE_BASE = 1000000.0
NEG_FILL = -1e30
LOW = jnp.bfloat16
F32 = jnp.float32
ROOT = 0.7978845608028654
CUBIC = 0.044715
SCALE = HD ** (-0.5)
VMEM_BESIDE = 38 << 20
VMEM_BYTES = 60 << 20


def shape(*dims, dtype=LOW):
    return jax.ShapeDtypeStruct(dims, dtype)


def contract(left, right, dims):
    return lax.dot_general(left, right, (dims, ((), ())), preferred_element_type=F32)


def rms_scale(values):
    return lax.rsqrt(jnp.mean(values * values, axis=-1, keepdims=True) + EPSILON)


def rms_back(values, gain, cotangent):
    scale = rms_scale(values)
    unit = values * scale
    scaled = cotangent * (1.0 + gain)
    back = scale * (scaled - unit * jnp.mean(scaled * unit, axis=-1, keepdims=True))
    return back, jnp.sum(cotangent * unit, axis=0, keepdims=True)


def turn(values, cosine, sine):
    half = HD // 2
    first, second = values[:, :half], values[:, half:]
    return jnp.concatenate([first * cosine - second * sine, second * cosine + first * sine], axis=1)


def turn_back(values, cosine, sine):
    return turn(values, cosine, -sine)


def add_to(ref, value, first):
    @pl.when(first)
    def _():
        ref[...] = value

    @pl.when(jnp.logical_not(first))
    def _():
        ref[...] += value


def run(body, name, grid, inputs, outputs, scratch=(), scalars=(), aliases=None, flops=0, vmem=VMEM_BESIDE, hbm=True):
    def spec(array, block):
        if block is None:
            dims = tuple(array.shape)
            return pl.BlockSpec(dims, lambda *_: (0,) * len(dims))
        if block == "any":
            return pl.BlockSpec(memory_space=pl.ANY)
        if block == "vmem":
            return pl.BlockSpec(memory_space=pltpu.VMEM)
        return pl.BlockSpec(*block)

    arrays = [a for a, _ in inputs]
    out_shape = [o for o, _ in outputs]
    if hbm:
        arrays = [
            a if b == "vmem" else pltpu.with_memory_space_constraint(a, pltpu.HBM)
            for a, b in inputs
        ]
    moved = sum(a.size * a.dtype.itemsize for a, _ in inputs)
    moved += sum(int(np.prod(o.shape)) * o.dtype.itemsize for o in out_shape)
    return pl.pallas_call(
        body,
        grid_spec=pltpu.PrefetchScalarGridSpec(
            num_scalar_prefetch=len(scalars),
            grid=grid,
            in_specs=[spec(a, b) for a, b in inputs],
            out_specs=[spec(o, b) for o, b in outputs],
            scratch_shapes=list(scratch),
        ),
        out_shape=[pltpu.HBM(o.shape, o.dtype) for o in out_shape] if hbm else out_shape,
        input_output_aliases={} if aliases is None else aliases,
        compiler_params=pltpu.CompilerParams(vmem_limit_bytes=vmem),
        cost_estimate=pl.CostEstimate(flops=flops, transcendentals=0, bytes_accessed=moved),
        name=name,
    )(*scalars, *arrays)


def column_tile(units):
    for tile in (1152, 1024, 768, 512, 384, 256, 128):
        if units % tile == 0:
            return tile
    return units


def row_tile(rows, most):
    tile = most
    while rows % tile:
        tile //= 2
    return tile


def keys_body(x, gain, key_w, value_w, key_gain, cosine, sine, xn_out, kv_out, raw_out):
    values = x[...].astype(F32)
    xn = (values * rms_scale(values) * (1.0 + gain[...])).astype(LOW)
    xn_out[...] = xn
    raw = contract(xn, key_w[...], ((1,), (0,)))
    raw_out[...] = raw
    unit = raw * rms_scale(raw) * (1.0 + key_gain[...])
    kv_out[:, :HD] = turn(unit, cosine[...], sine[...]).astype(LOW)
    kv_out[:, HD:] = contract(xn, value_w[...], ((1,), (0,))).astype(LOW)


def project_keys(x, gain, key_w, value_w, key_gain, cosine, sine):
    rows, dim = x.shape
    tile = row_tile(rows, 128)
    by_row = lambda width: ((tile, width), lambda i: (i, 0))
    return run(
        keys_body,
        "project_keys",
        (rows // tile,),
        [
            (x, by_row(dim)),
            (gain, None),
            (key_w, None),
            (value_w, None),
            (key_gain, None),
            (cosine, by_row(HD // 2)),
            (sine, by_row(HD // 2)),
        ],
        [
            (shape(rows, dim), by_row(dim)),
            (shape(rows, 2 * HD), by_row(2 * HD)),
            (shape(rows, HD, dtype=F32), by_row(HD)),
        ],
        flops=4 * rows * dim * HD,
    )


def queries_body(xn, own_w, first_w, second_w, gain, cosine, sine, q_out, raw_out):
    values = xn[...]
    start = 0
    for weight in (own_w, first_w, second_w):
        raw_all = contract(values, weight[...], ((1,), (0,)))
        for at in range(0, weight.shape[1], HD):
            raw = raw_all[:, at : at + HD]
            unit = raw * rms_scale(raw) * (1.0 + gain[...])
            raw_out[:, start : start + HD] = raw
            q_out[:, start : start + HD] = turn(unit, cosine[...], sine[...]).astype(LOW)
            start += HD


def project_queries(xn, heads_w, gain, cosine, sine):
    rows, dim = xn.shape
    width = sum(w.shape[1] for w in heads_w)
    tile = row_tile(rows, 128)
    by_row = lambda size: ((tile, size), lambda i: (i, 0))
    return run(
        queries_body,
        "project_queries",
        (rows // tile,),
        [(xn, by_row(dim))]
        + [(w, None) for w in heads_w]
        + [(gain, None), (cosine, by_row(HD // 2)), (sine, by_row(HD // 2))],
        [(shape(rows, width), by_row(width)), (shape(rows, width, dtype=F32), by_row(width))],
        flops=2 * rows * dim * width,
    )


def attend_body(slots, meta, q, before, own, o_out, p_out, bias):
    block, keys = bias.shape
    rows = keys // 2

    @pl.when(pl.program_id(1) == 0)
    def _():
        second = meta[0]
        first_row = second * rows + pl.program_id(0) * block
        query = first_row + lax.broadcasted_iota(jnp.int32, (block, keys), 0)
        column = lax.broadcasted_iota(jnp.int32, (block, keys), 1)
        is_own = column >= rows
        key = jnp.where(is_own, column + (second - 1) * rows, column)
        ends = jnp.int32(0)
        query_segment = jnp.zeros((block, keys), jnp.int32)
        key_segment = jnp.zeros((block, keys), jnp.int32)
        for s in range(slots):
            ends = ends + meta[1 + s]
            query_segment += (query >= ends).astype(jnp.int32)
            key_segment += (key >= ends).astype(jnp.int32)
        known = is_own | (column < second * rows)
        seen = (key < query) & (query_segment == key_segment) & (query_segment < slots) & known
        seen = seen | (is_own & (key == query))
        bias[...] = jnp.where(seen, 0.0, NEG_FILL)

    scores = jnp.concatenate(
        [
            contract(q[...], before[:, :HD], ((1,), (1,))),
            contract(q[...], own[:, :HD], ((1,), (1,))),
        ],
        axis=1,
    )
    scores = jnp.where(bias[...] < 0.0, NEG_FILL, scores * SCALE)
    exps = jnp.exp(scores - jnp.max(scores, axis=1, keepdims=True))
    probs = (exps * (1.0 / jnp.sum(exps, axis=1, keepdims=True))).astype(LOW)
    p_out[...] = probs
    out = contract(probs[:, :rows], before[:, HD:], ((1,), (0,)))
    out += contract(probs[:, rows:], own[:, HD:], ((1,), (0,)))
    o_out[...] = out.astype(LOW)


def attend(meta, q, before, own):
    rows, width = q.shape
    heads = width // HD
    block = row_tile(rows, 256)
    blocks = rows // block
    slots = meta.shape[0] - 1
    head_block = ((block, HD), lambda i, h, m: (i, h))
    return run(
        lambda *refs: attend_body(slots, *refs),
        "attend",
        (blocks, heads),
        [(q, head_block), (before, None), (own, None)],
        [
            (shape(rows, width), head_block),
            (shape(heads * rows, 2 * rows), ((block, 2 * rows), lambda i, h, m: (h * blocks + i, 0))),
        ],
        scratch=[pltpu.VMEM((block, 2 * rows), F32)],
        scalars=[meta],
        flops=8 * rows * rows * width,
    )


def merge_body(o, own_w, first_w, second_w, x, post_gain, pre_gain, a_out, state_out, z_out):
    start = 0
    total = None
    for weight in (own_w, first_w, second_w):
        width = weight.shape[1]
        part = contract(o[:, start : start + width], weight[...], ((1,), (1,)))
        total = part if total is None else total + part
        start += width
    a_out[...] = total.astype(a_out.dtype)
    state = x[...].astype(F32) + total * rms_scale(total) * (1.0 + post_gain[...])
    state_out[...] = state.astype(state_out.dtype)
    z_out[...] = (state * rms_scale(state) * (1.0 + pre_gain[...])).astype(LOW)


def merge_heads(o, heads_w, x, post_gain, pre_gain):
    rows, dim = x.shape
    width = o.shape[1]
    tile = row_tile(rows, 128)
    by_row = lambda size: ((tile, size), lambda i: (i, 0))
    return run(
        merge_body,
        "merge_heads",
        (rows // tile,),
        [(o, by_row(width))]
        + [(w, None) for w in heads_w]
        + [(x, by_row(dim)), (post_gain, None), (pre_gain, None)],
        [
            (shape(rows, dim), by_row(dim)),
            (shape(rows, dim), by_row(dim)),
            (shape(rows, dim), by_row(dim)),
        ],
        flops=2 * rows * dim * width,
    )


def ffn_forward_body(z, gate_w, up_w, down_w, *rest):
    hid_out, act_out, slope_out, f_out, acc = rest[-5:]
    step, last = pl.program_id(0), pl.num_programs(0) - 1
    tile = hid_out.shape[1]
    here = pl.ds(pl.multiple_of(step * tile, 128), tile)
    gate = contract(z[...], gate_w[:, here], ((1,), (0,)))
    up = contract(z[...], up_w[:, here], ((1,), (0,)))
    square = gate * gate
    tanh = jnp.tanh(ROOT * gate * (1.0 + CUBIC * square))
    half = 0.5 * (1.0 + tanh)
    act = gate * half
    slope = half + 0.5 * gate * (1.0 - tanh * tanh) * (ROOT * (1.0 + 3.0 * CUBIC * square))
    hid = (act * up).astype(LOW)
    hid_out[...] = hid
    act_out[...] = act.astype(LOW)
    slope_out[...] = (slope * up).astype(LOW)
    add_to(acc, contract(hid, down_w[:, here], ((1,), (1,))), step == 0)

    @pl.when(step == last)
    def _():
        f_out[...] = acc[...].astype(f_out.dtype)


def ffn_forward(z, z_block, rows, weights, block, total, kept, out_dtype):
    dim, units = weights[0].shape
    tile = column_tile(units)
    inner = ((rows, tile), lambda j: (block, j))
    extra = [] if kept is None else list(kept)
    return run(
        ffn_forward_body,
        "ffn_forward",
        (units // tile,),
        [(z, ((rows, dim), lambda j: (z_block, 0)))]
        + [(w, "vmem") for w in weights]
        + [(k, "any") for k in extra],
        [(shape(total, units), inner)] * 3 + [(shape(rows, dim, dtype=out_dtype), None)],
        scratch=[pltpu.VMEM((rows, dim), F32)],
        aliases={4 + i: i for i in range(len(extra))},
        flops=6 * rows * dim * units,
    )


def ffn_end_body(f_own, f_other, state, cotangent, gain, *rest):
    out, df_out, gain_out = rest[-3:]
    f = f_own[...] + f_other[...].astype(F32)
    out[...] = (state[...].astype(F32) + f * rms_scale(f) * (1.0 + gain[...])).astype(LOW)
    df, gain_grad = rms_back(f, gain[...], cotangent[...].astype(F32))
    df_out[...] = df.astype(LOW)
    add_to(gain_out, gain_grad, pl.program_id(0) == 0)


def ffn_end(f_own, f_other, state, cotangent, gain, chunk, out):
    rows, dim = f_own.shape
    tile = row_tile(rows, 128)
    steps = rows // tile
    here = ((tile, dim), lambda i: (i, 0))
    there = ((tile, dim), lambda i: (chunk * steps + i, 0))
    extra = [] if out is None else [out]
    return run(
        ffn_end_body,
        "ffn_end",
        (steps,),
        [(f_own, here), (f_other, here), (state, there), (cotangent, there), (gain, None)]
        + [(e, "any") for e in extra],
        [(shape(*state.shape), there), (shape(rows, dim), here), (shape(1, dim, dtype=F32), None)],
        aliases={5: 0} if extra else None,
    )


def ffn_backward_body(pieces, *refs):
    dfs = refs[:pieces]
    act, slope, gate_w, up_w, down_w = refs[pieces : pieces + 5]
    dgate_out, dup_out, dz_out, acc, df = refs[-5:]
    step, last = pl.program_id(0), pl.num_programs(0) - 1

    @pl.when(step == 0)
    def _():
        at = 0
        for piece in dfs:
            df[at : at + piece.shape[0]] = piece[...]
            at += piece.shape[0]

    tile = dup_out.shape[1]
    here = pl.ds(pl.multiple_of(step * tile, 128), tile)
    dhid = contract(df[...], down_w[:, here], ((1,), (0,)))
    dup = (dhid * act[...].astype(F32)).astype(LOW)
    dgate = (dhid * slope[...].astype(F32)).astype(LOW)
    dup_out[...] = dup
    dgate_out[...] = dgate
    part = contract(dgate, gate_w[:, here], ((1,), (1,)))
    part += contract(dup, up_w[:, here], ((1,), (1,)))
    add_to(acc, part, step == 0)

    @pl.when(step == last)
    def _():
        dz_out[...] = acc[...].astype(dz_out.dtype)


def ffn_backward(dfs, act, slope, weights, block, made, out_dtype):
    rows = sum(d.shape[0] for d in dfs)
    total, units = act.shape
    dim = dfs[0].shape[1]
    tile = column_tile(units)
    inner = ((rows, tile), lambda j: (block, j))
    extra = [] if made is None else list(made)
    return run(
        lambda *refs: ffn_backward_body(len(dfs), *refs),
        "ffn_backward",
        (units // tile,),
        [(d, None) for d in dfs]
        + [(act, inner), (slope, inner)]
        + [(w, "vmem") for w in weights]
        + [(e, "any") for e in extra],
        [(shape(total, units), inner)] * 2 + [(shape(rows, dim, dtype=out_dtype), None)],
        scratch=[pltpu.VMEM((rows, dim), F32), pltpu.VMEM((rows, dim), LOW)],
        aliases={len(dfs) + 5 + i: i for i in range(len(extra))},
        flops=6 * rows * dim * units,
    )


def weight_grad_body(sides, core, *refs):
    *inputs, send, keep = refs
    groups, rows, _ = keep.shape
    first = core[0] == 0

    def write(lefts, right):
        at = 0
        total = None
        for left in lefts:
            size = left.shape[0]
            part = contract(left[...], right[at : at + size], ((0,), (0,)))
            total = part if total is None else total + part
            at += size
        for i in range(groups):
            even = total[2 * i * rows : (2 * i + 1) * rows].astype(LOW)
            odd = total[(2 * i + 1) * rows : (2 * i + 2) * rows].astype(LOW)
            send[i] = jnp.where(first, odd, even)
            keep[i] = jnp.where(first, even, odd)

    at = 0
    for side, count in enumerate(sides):
        lefts, right = inputs[at : at + count], inputs[at + count]
        at += count + 1
        if len(sides) == 1:
            write(lefts, right)
        else:
            mine = (pl.program_id(0) % len(sides)) == side
            pl.when(mine)(lambda lefts=lefts, right=right: write(lefts, right))


def weight_grad(
    pairs, core, axis_size, start, stop, tile=None, columns_of=None, vmem=VMEM_BYTES
):
    dim = pairs[0][0][0].shape[1]
    columns = stop - start
    rows = dim // axis_size
    groups = axis_size // 2
    tile = column_tile(columns) if tile is None else tile
    blocks = columns // tile
    if columns_of is None:
        columns_of = lambda j, c: j + start // tile
    if rows % 8:
        full = []
        for j in range(blocks):
            lefts, right = pairs[j % len(pairs)]
            left = jnp.concatenate(lefts, axis=0)
            at = columns_of(j, core) * tile
            here = lax.dynamic_slice_in_dim(right, at, tile, axis=1)
            full.append(contract(left, here, ((0,), (0,))).astype(LOW))
        full = jnp.concatenate(full, axis=1).reshape(groups, 2, rows, columns)
        return (
            lax.dynamic_index_in_dim(full, 1 - core, axis=1, keepdims=False),
            lax.dynamic_index_in_dim(full, core, axis=1, keepdims=False),
        )
    inputs = []
    for lefts, right in pairs:
        inputs += [(left, None) for left in lefts]
        inputs.append((right, ((right.shape[0], tile), lambda j, c: (0, columns_of(j, c[0])))))
    out = (shape(groups, rows, columns), ((groups, rows, tile), lambda j, c: (0, 0, j)))
    sides = [len(lefts) for lefts, _ in pairs]
    return run(
        lambda *refs: weight_grad_body(sides, *refs),
        "weight_grad",
        (blocks,),
        inputs,
        [out, out],
        scalars=[core.reshape(1)],
        flops=2 * pairs[0][1].shape[0] * dim * columns,
        vmem=vmem,
    )


def state_back_body(
    dz_own, dz_first, dz_second, state, a, cotangent, pre_gain, post_gain, own_w, first_w, second_w,
    dh_out, da_out, do_out, pre_out, post_out,
):
    first = pl.program_id(0) == 0
    early = pl.program_id(0) < pl.num_programs(0) // 2
    dz = dz_own[...] + jnp.where(early, dz_first[...], dz_second[...]).astype(F32)
    back, pre_grad = rms_back(state[...].astype(F32), pre_gain[...], dz)
    dh = cotangent[...].astype(F32) + back
    dh_out[...] = dh.astype(dh_out.dtype)
    da, post_grad = rms_back(a[...].astype(F32), post_gain[...], dh)
    da = da.astype(LOW)
    da_out[...] = da
    add_to(pre_out, pre_grad, first)
    add_to(post_out, post_grad, first)
    at = 0
    for weight in (own_w, first_w, second_w):
        width = weight.shape[1]
        do_out[:, at : at + width] = contract(da, weight[...], ((1,), (0,))).astype(LOW)
        at += width


def state_back(dz_own, dz_other, state, a, cotangent, pre_gain, post_gain, heads_w):
    rows, dim = state.shape
    width = sum(w.shape[1] for w in heads_w)
    tile = row_tile(rows, 128)
    steps = rows // tile
    by_row = lambda size: ((tile, size), lambda i: (i, 0))
    return run(
        state_back_body,
        "state_back",
        (rows // tile,),
        [
            (dz_own, by_row(dim)),
            (dz_other[0], ((tile, dim), lambda i: (jnp.minimum(i, steps // 2 - 1), 0))),
            (dz_other[1], ((tile, dim), lambda i: (jnp.maximum(i - steps // 2, 0), 0))),
        ]
        + [(v, by_row(dim)) for v in (state, a, cotangent)]
        + [(v, None) for v in (pre_gain, post_gain, *heads_w)],
        [
            (shape(rows, dim), by_row(dim)),
            (shape(rows, dim), by_row(dim)),
            (shape(rows, width), by_row(width)),
            (shape(1, dim, dtype=F32), None),
            (shape(1, dim, dtype=F32), None),
        ],
        vmem=VMEM_BYTES,
        flops=2 * rows * dim * width,
    )


def attend_back_body(
    p, do, q, raw, before, own, gain, cosine, sine, dq_out, before_out, own_out, gain_out, acc
):
    head, part = pl.program_id(0), pl.program_id(1)
    first = (head == 0) & (part == 0)
    last = (head == pl.num_programs(0) - 1) & (part == pl.num_programs(1) - 1)
    rows = before.shape[0]
    dp = jnp.concatenate(
        [
            contract(do[...], before[:, HD:], ((1,), (1,))),
            contract(do[...], own[:, HD:], ((1,), (1,))),
        ],
        axis=1,
    )
    probs = p[...].astype(F32)
    weighted = probs * dp
    ds = (weighted - probs * jnp.sum(weighted, axis=1, keepdims=True)).astype(LOW)
    dq = contract(ds[:, :rows], before[:, :HD], ((1,), (0,)))
    dq += contract(ds[:, rows:], own[:, :HD], ((1,), (0,)))
    dk = contract(ds, q[...], ((0,), (0,))) * SCALE
    dv = contract(p[...], do[...], ((0,), (0,)))
    add_to(acc, jnp.concatenate([dk, dv], axis=1), first)
    back = turn_back(dq * SCALE, cosine[...], sine[...])
    dq_raw, gain_grad = rms_back(raw[...], gain[...], back)
    dq_out[...] = dq_raw.astype(LOW)
    add_to(gain_out, gain_grad, first)

    @pl.when(last)
    def _():
        before_out[...] = acc[:rows].astype(LOW)
        own_out[...] = acc[rows:]


def attend_back(p, do, q, raw, before, own, gain, cosine, sine):
    rows, width = q.shape
    heads = width // HD
    block = row_tile(rows, 256)
    blocks = rows // block
    head_block = ((block, HD), lambda h, i: (i, h))
    table = ((block, HD // 2), lambda h, i: (i, 0))
    return run(
        attend_back_body,
        "attend_back",
        (heads, blocks),
        [
            (p, ((block, 2 * rows), lambda h, i: (h * blocks + i, 0))),
            (do, head_block),
            (q, head_block),
            (raw, head_block),
            (before, None),
            (own, None),
            (gain, None),
            (cosine, table),
            (sine, table),
        ],
        [
            (shape(rows, width), head_block),
            (shape(rows, 2 * HD), None),
            (shape(rows, 2 * HD, dtype=F32), None),
            (shape(1, HD, dtype=F32), None),
        ],
        scratch=[pltpu.VMEM((2 * rows, 2 * HD), F32)],
        vmem=VMEM_BYTES,
        flops=16 * rows * rows * width,
    )


def input_back_body(
    dq, dkv_own, dkv_other, raw, cosine, sine, x, dh, key_gain, in_gain,
    own_w, first_w, second_w, key_w, value_w,
    grad_out, dkv_out, key_gain_out, in_gain_out,
):
    first = pl.program_id(0) == 0
    dkv = dkv_own[...] + dkv_other[...].astype(F32)
    back = turn_back(dkv[:, :HD], cosine[...], sine[...])
    dk, key_grad = rms_back(raw[...], key_gain[...], back)
    dk = dk.astype(LOW)
    dv = dkv[:, HD:].astype(LOW)
    dkv_out[:, :HD] = dk
    dkv_out[:, HD:] = dv
    add_to(key_gain_out, key_grad, first)
    dxn = contract(dk, key_w[...], ((1,), (1,))) + contract(dv, value_w[...], ((1,), (1,)))
    at = 0
    for weight in (own_w, first_w, second_w):
        width = weight.shape[1]
        dxn += contract(dq[:, at : at + width], weight[...], ((1,), (1,)))
        at += width
    dx, in_grad = rms_back(x[...].astype(F32), in_gain[...], dxn)
    grad_out[...] = (dh[...].astype(F32) + dx).astype(LOW)
    add_to(in_gain_out, in_grad, first)


def input_back(dq, dkv_own, dkv_other, raw, cosine, sine, x, dh, key_gain, in_gain, weights):
    rows, dim = x.shape
    width = dq.shape[1]
    tile = row_tile(rows, 128)
    by_row = lambda size: ((tile, size), lambda i: (i, 0))
    return run(
        input_back_body,
        "input_back",
        (rows // tile,),
        [(v, by_row(v.shape[1])) for v in (dq, dkv_own, dkv_other, raw, cosine, sine, x, dh)]
        + [(v, None) for v in (key_gain, in_gain, *weights)],
        [
            (shape(rows, dim), by_row(dim)),
            (shape(rows, 2 * HD), by_row(2 * HD)),
            (shape(1, HD, dtype=F32), None),
            (shape(1, dim, dtype=F32), None),
        ],
        vmem=VMEM_BYTES,
        flops=2 * rows * dim * (width + 2 * HD),
    )


def swap_head(value):
    return lax.ppermute(value, "head", [(0, 1), (1, 0)])


def pair(axis_size, bit):
    return [(i, i ^ (1 << bit)) for i in range(axis_size)]


def tie(*values):
    return lax.optimization_barrier(values)


def sum_parts(parts, choice, columns, dtype):
    total = None
    for array, own, at in parts:
        value = array.reshape((2,) * len(own) + array.shape[-2:])
        if columns != array.shape[-1]:
            value = value[..., at : at + columns]
        left = list(own)
        for bit in own:
            if bit in choice:
                value = lax.dynamic_index_in_dim(value, choice[bit], left.index(bit), False)
                left.remove(bit)
        value = value.astype(F32)
        total = value if total is None else total + value
    return total.astype(dtype)


class Scatter:
    def __init__(self, size, index, order, bits, parts, columns, out=None, low=LOW):
        self.size, self.index, self.order, self.low = size, index, list(order), low
        self.bits, self.parts, self.columns, self.out = list(bits), list(parts), columns, out
        self.gone, self.loaded, self.flying, self.cuts = [], out is not None, False, None
        if out is None:
            self.load()
        else:
            self.drop()

    def value(self, bit):
        return (self.index >> bit) & 1

    def drop(self):
        bit = self.order[0]
        if bit == "head":
            self.columns //= 2
        else:
            self.bits.remove(bit)
            self.gone.append(bit)

    def load(self):
        if not self.order:
            return
        bit = self.order[0]
        choice = {b: self.value(b) for b in self.gone}
        parts, columns = self.parts, self.columns
        if bit == "head":
            columns //= 2
            parts = [(p, own, at + columns) for p, own, at in parts]
        else:
            choice[bit] = 1 - self.value(bit)
        self.out = sum_parts(parts, choice, columns, self.low)
        self.loaded = True
        self.drop()

    def go(self):
        bit = self.order.pop(0)
        if bit == "head":
            self.got = swap_head(self.out)
        else:
            self.got = lax.ppermute(self.out, "dp", pair(self.size, bit))
        self.loaded, self.flying = False, True
        return self

    def take(self):
        self.parts = self.parts + [(self.got, list(self.bits), 0)]
        self.flying = False
        return self

    def land(self):
        self.take().load()
        return self

    def finish(self):
        if self.flying:
            self.take()
        while self.order:
            if not self.loaded:
                self.load()
            self.go().take()
        choice = {b: self.value(b) for b in self.gone}
        return sum_parts(self.parts, choice, self.columns, F32)


def load_body(*refs):
    count = (len(refs) - 1) // 2
    sems = refs[-1]
    copies = [
        pltpu.make_async_copy(source, target, sems.at[i])
        for i, (source, target) in enumerate(zip(refs[:count], refs[count : 2 * count]))
    ]
    for copy in copies:
        copy.start()
    for copy in copies:
        copy.wait()


def load_weights(weights):
    return pl.pallas_call(
        load_body,
        in_specs=[pl.BlockSpec(memory_space=pl.ANY)] * len(weights),
        out_specs=[pl.BlockSpec(memory_space=pltpu.VMEM)] * len(weights),
        out_shape=[pltpu.VMEM(w.shape, w.dtype) for w in weights],
        scratch_shapes=[pltpu.SemaphoreType.DMA((len(weights),))],
        compiler_params=pltpu.CompilerParams(vmem_limit_bytes=VMEM_BESIDE),
        name="load_weights",
    )(*weights)


def angle_tables(lengths, head_index, rows):
    ids = head_index * rows + jnp.arange(rows, dtype=jnp.int32)
    begin = jnp.zeros_like(ids)
    end = jnp.int32(0)
    for s in range(lengths.shape[0]):
        end = end + lengths[s]
        begin = jnp.where(ids >= end, end, begin)
    frequency = np.power(ROPE_BASE, -2.0 * np.arange(HD // 2) / HD).astype(np.float32)
    grid = (ids - begin).astype(F32)[:, None] * frequency[None, :]
    return jnp.cos(grid), jnp.sin(grid)


def on_device(
    layer_input,
    seq_lengths,
    input_gain,
    query_weight,
    key_weight,
    value_weight,
    query_gain,
    key_gain,
    output_weight,
    post_attn_gain,
    pre_ffn_gain,
    gate_weight,
    up_weight,
    down_weight,
    post_ffn_gain,
    out_cotangent,
):
    rows = layer_input.shape[0]
    dp_size = lax.axis_size("dp")
    bit_count = dp_size.bit_length() - 1
    dp_index = lax.axis_index("dp")
    head_index = lax.axis_index("head")
    core = dp_index & 1
    core_pairs = pair(dp_size, 0)
    width = query_weight.shape[1]
    in_gain, q_gain, k_gain, post_gain, pre_gain, end_gain = (
        g.reshape(1, -1)
        for g in (input_gain, query_gain, key_gain, post_attn_gain, pre_ffn_gain, post_ffn_gain)
    )

    query_mine = lax.dynamic_slice_in_dim(query_weight, core * HD, HD, axis=1)
    output_mine = lax.dynamic_slice_in_dim(output_weight, core * HD, HD, axis=1)
    query_mine, output_mine, layer_input, seq_lengths = tie(
        query_mine, output_mine, layer_input, seq_lengths
    )
    query_first = swap_head(query_mine)
    query_second = lax.ppermute(query_first, "dp", core_pairs)

    cosine, sine = angle_tables(seq_lengths[0], head_index, rows)
    meta = jnp.concatenate([head_index.reshape(1).astype(jnp.int32), seq_lengths[0]])
    xn, kv_own, k_raw = project_keys(
        layer_input, in_gain, key_weight, value_weight, k_gain, cosine, sine
    )
    kv_before = lax.ppermute(kv_own, "head", [(0, 1)])
    *weights, kv_own = tie(gate_weight, up_weight, down_weight, kv_own)
    weights = load_weights(weights)
    xn_in, *weights = tie(xn, *weights)
    weights = [pltpu.with_memory_space_constraint(w, pltpu.VMEM) for w in weights]
    kv_before, output_mine = tie(kv_before, output_mine)
    output_first = swap_head(output_mine)
    query_w = (query_weight, query_first, query_second)

    q_low, q_raw = project_queries(xn_in, query_w, q_gain, cosine, sine)
    q_low, output_first = tie(q_low, output_first)
    output_second = lax.ppermute(output_first, "dp", core_pairs)
    output_w = (output_weight, output_first, output_second)
    attn_out, probs = attend(meta, q_low, kv_before, kv_own)
    attn_proj, state, z_all = merge_heads(attn_out, output_w, layer_input, post_gain, pre_gain)

    half = rows // 2
    total = 2 * rows
    z_other = [swap_head(z_all[:half]), swap_head(z_all[half:])]
    *kept, f_own0 = ffn_forward(z_all, 0, half, weights, 0, total, None, F32)
    z_in, f_own0 = tie(z_other[0], f_own0)
    *kept, f_send0 = ffn_forward(z_in, 0, half, weights, 2, total, kept, LOW)
    z_in, f_send0 = tie(z_other[1], f_send0)
    *kept, f_send1 = ffn_forward(z_in, 0, half, weights, 3, total, kept, LOW)
    f_got0 = swap_head(f_send0)
    z_in, f_send1 = tie(z_all, f_send1)
    f_got1 = swap_head(f_send1)
    *kept, f_own1 = ffn_forward(z_in, 1, half, weights, 1, total, kept, F32)
    hid, act, slope = kept
    f_got0, f_own0, f_own1 = tie(f_got0, f_own0, f_own1)
    layer_output, df_own0, end_grad0 = ffn_end(
        f_own0, f_got0, state, out_cotangent, end_gain, 0, None
    )
    df_other0 = swap_head(df_own0)
    layer_output, df_own1, end_grad1 = ffn_end(
        f_own1, f_got1, state, out_cotangent, end_gain, 1, layer_output
    )
    df_other1 = swap_head(df_own1)
    df_own = [df_own0, df_own1]
    *made, own_zgrad = ffn_backward(df_own, act, slope, weights, 0, None, F32)
    df_other0, df_other1, own_zgrad = tie(df_other0, df_other1, own_zgrad)
    df_other = [df_other0, df_other1]
    units = hid.shape[1]
    order = list(range(bit_count))
    rest = order[1:]
    leading = rest[::-1]
    third = units // 3

    def start(pairs, first, last, route=order, **options):
        send, keep = weight_grad(pairs, core, dp_size, first, last, **options)
        columns = last - first
        return Scatter(
            dp_size, dp_index, route, order[::-1], [(keep, leading, 0)], columns, send
        )

    def cut(whole, at, columns, route=rest):
        parts = [(p, own, at) for p, own, _ in whole.parts]
        return Scatter(dp_size, dp_index, route, leading, parts, columns)

    def phase(values, end=(), go=(), now=()):
        count = len(values)
        done = list(end) + list(now)
        tied = list(tie(*values, *[s.got for s in done], *[s.out for s in go]))
        for s in go[::-1]:
            s.out = tied.pop()
        for s in done[::-1]:
            s.got = tied.pop()
            s.take()
        for s in go:
            s.go()
        for s in list(now) + [s for s in end if s.cuts is None]:
            s.load()
        if now:
            tied = list(tie(*tied, *[s.out for s in now]))
            for s in now[::-1]:
                s.out = tied.pop()
                s.go()
        return tied

    df_all = df_own + df_other
    down_a = start([(df_all, hid)], 0, 2 * third, vmem=VMEM_BESIDE)
    (hid,) = phase([hid], go=[down_a])
    down_b = start([(df_all, hid)], 2 * third, units, vmem=VMEM_BESIDE)
    down_a.cuts = down_b.cuts = 1
    (df_other0,) = phase([df_other0], end=[down_a], go=[down_b])
    d1 = cut(down_a, 0, third)
    (df_other0,) = phase([df_other0], go=[d1])
    *made, other_send = ffn_backward([df_other0, df_other1], act, slope, weights, 1, made, LOW)
    d2 = cut(down_a, third, third)
    dgate, dup = made
    other_send, dgate = phase([other_send, dgate], end=[down_b, d1], go=[d2])
    other_half = [swap_head(other_send[:half])]
    z_both = [z_all] + z_other
    gate_s = start([(z_both, dgate)], 0, units)
    d3 = cut(down_b, 0, third)
    other_half[0], other_send, dup = phase(
        [other_half[0], other_send, dup], end=[d2], go=[d3, gate_s, d1]
    )
    other_half.append(swap_head(other_send[half:]))
    up_s = start([(z_both, dup)], 0, units)
    gate_s.cuts = up_s.cuts = 1
    own_zgrad, other_half[0], other_half[1] = phase(
        [own_zgrad, other_half[0], other_half[1]], end=[gate_s, d1, d3], go=[up_s, d2]
    )
    g1 = cut(gate_s, 0, 2 * third)
    (own_zgrad,) = phase([own_zgrad], go=[g1])
    g2 = cut(gate_s, 2 * third, third)
    other_zgrad = other_half

    state_grad, attn_grad, heads_grad, pre_grad, post_grad = state_back(
        own_zgrad, other_zgrad, state, attn_proj, out_cotangent, pre_gain, post_gain, output_w
    )
    dq, kv_back_send, kv_grad, q_gain_grad = attend_back(
        probs, heads_grad, q_low, q_raw, kv_before, kv_own, q_gain, cosine, sine
    )
    kv_back = lax.ppermute(kv_back_send, "head", [(1, 0)])

    own_heads = width // HD

    def head_block(j, c):
        j = j // 2
        there = own_heads + ((j - own_heads) ^ c)
        return jnp.where(j < own_heads, j, there)

    heads_s = start(
        [([attn_grad], attn_out), ([xn], dq)],
        0,
        4 * width,
        [order[0], "head"] + rest,
        tile=HD,
        columns_of=head_block,
    )
    dq, kv_grad, kv_back = phase(
        [dq, kv_grad, kv_back], end=[up_s, g1, d2], go=[heads_s, g2, d3, d1]
    )
    u1, u2, u3 = (cut(up_s, third * i, third) for i in range(3))
    input_grad, dkv, k_gain_grad, in_gain_grad = input_back(
        dq, kv_grad, kv_back, k_raw, cosine, sine, layer_input, state_grad, k_gain, in_gain,
        query_w + (key_weight, value_weight),
    )
    kv_s = start([([xn], dkv)], 0, 2 * HD)
    gains = [in_gain_grad, post_grad, pre_grad, end_grad0 + end_grad1, q_gain_grad, k_gain_grad]
    gains = [g.reshape(dp_size, 1, -1) for g in gains]
    widths = [g.shape[2] for g in gains]
    packed = jnp.concatenate(gains, axis=2)
    packed = jnp.pad(packed, ((0, 0), (0, 0), (0, -packed.shape[2] % 128)))
    gains_s = Scatter(
        dp_size, dp_index, order, order[::-1], [(packed, order[::-1], 0)], packed.shape[2], low=F32
    )
    (packed,) = phase([packed], end=[g2, d3, d1], go=[u1, kv_s, d2, g1], now=[heads_s])
    (packed,) = phase([packed], end=[u1, d2, g1], go=[g2, d3], now=[heads_s, kv_s])
    (packed,) = phase([packed], end=[g2, d3], go=[u2, u1, g1], now=[heads_s, kv_s])
    (packed,) = phase([packed], end=[u1, g1], go=[u3, g2], now=[heads_s, kv_s, u2])
    (packed,) = phase([packed], end=[g2], go=[u1], now=[u3, u2])
    down_part = jnp.concatenate([d1.finish(), d2.finish(), d3.finish()], axis=1)
    gate_part = jnp.concatenate([g1.finish(), g2.finish()], axis=1)
    up_part = jnp.concatenate([u1.finish(), u2.finish(), u3.finish()], axis=1)
    heads_part = heads_s.finish()
    query_part = jnp.concatenate([heads_part[:, HD : 2 * HD], heads_part[:, 3 * HD :]], axis=1)
    output_part = jnp.concatenate([heads_part[:, :HD], heads_part[:, 2 * HD : 3 * HD]], axis=1)
    kv_sum = kv_s.finish()
    kv_sum = kv_sum + swap_head(kv_sum)
    packed = gains_s.finish().reshape(-1)
    packed = packed + swap_head(packed)
    pieces = []
    at = 0
    for size in widths:
        pieces.append(packed[at : at + size])
        at += size
    return (
        layer_output,
        input_grad,
        pieces[0],
        query_part,
        kv_sum[:, :HD],
        kv_sum[:, HD:],
        pieces[4],
        pieces[5],
        output_part,
        pieces[1],
        pieces[2],
        gate_part,
        up_part,
        down_part,
        pieces[3],
    )


def solution(mesh):
    placed = (
        P(("dp", "head"), None),
        P("dp", None),
        P(),
        P(None, "head"),
        P(),
        P(),
        P(),
        P(),
        P(None, "head"),
        P(),
        P(),
        P(None, "head"),
        P(None, "head"),
        P(None, "head"),
        P(),
        P(("dp", "head"), None),
    )
    return jax.shard_map(
        on_device,
        mesh=mesh,
        in_specs=placed,
        out_specs=(
            P(("dp", "head"), None),
            P(("dp", "head"), None),
            P("dp"),
            P("dp", "head"),
            P("dp", None),
            P("dp", None),
            P("dp"),
            P("dp"),
            P("dp", "head"),
            P("dp"),
            P("dp"),
            P("dp", "head"),
            P("dp", "head"),
            P("dp", "head"),
            P("dp"),
        ),
        check_vma=False,
    )
```

```python
import jax
import jax.numpy as jnp
import numpy as np
from jax import lax
from jax.experimental import pallas as pl
from jax.experimental.pallas import tpu as pltpu
from jax.sharding import PartitionSpec as P

HD = 256
EPSILON = 1e-06
ROPE_BASE = 1000000.0
NEG_FILL = -1e30
LOW = jnp.bfloat16
F32 = jnp.float32
ROOT = 0.7978845608028654
CUBIC = 0.044715
SCALE = HD ** (-0.5)
VMEM_BESIDE = 30 << 20
VMEM_BYTES = 60 << 20


def shape(*dims, dtype=LOW):
    return jax.ShapeDtypeStruct(dims, dtype)


def contract(left, right, dims):
    return lax.dot_general(left, right, (dims, ((), ())), preferred_element_type=F32)


def rms_scale(values):
    return lax.rsqrt(jnp.mean(values * values, axis=-1, keepdims=True) + EPSILON)


def rms_back(values, gain, cotangent):
    scale = rms_scale(values)
    unit = values * scale
    scaled = cotangent * (1.0 + gain)
    back = scale * (scaled - unit * jnp.mean(scaled * unit, axis=-1, keepdims=True))
    return back, jnp.sum(cotangent * unit, axis=0, keepdims=True)


def turn(values, cosine, sine):
    half = HD // 2
    first, second = values[:, :half], values[:, half:]
    return jnp.concatenate([first * cosine - second * sine, second * cosine + first * sine], axis=1)


def turn_back(values, cosine, sine):
    return turn(values, cosine, -sine)


def add_to(ref, value, first):
    @pl.when(first)
    def _():
        ref[...] = value

    @pl.when(jnp.logical_not(first))
    def _():
        ref[...] += value


def run(body, name, grid, inputs, outputs, scratch=(), scalars=(), aliases=None, flops=0, vmem=VMEM_BESIDE, hbm=True):
    def spec(array, block):
        if block is None:
            dims = tuple(array.shape)
            return pl.BlockSpec(dims, lambda *_: (0,) * len(dims))
        if block == "any":
            return pl.BlockSpec(memory_space=pl.ANY)
        if block == "vmem":
            return pl.BlockSpec(memory_space=pltpu.VMEM)
        return pl.BlockSpec(*block)

    arrays = [a for a, _ in inputs]
    out_shape = [o for o, _ in outputs]
    if hbm:
        arrays = [
            a if b == "vmem" else pltpu.with_memory_space_constraint(a, pltpu.HBM)
            for a, b in inputs
        ]
    moved = sum(a.size * a.dtype.itemsize for a, _ in inputs)
    moved += sum(int(np.prod(o.shape)) * o.dtype.itemsize for o in out_shape)
    return pl.pallas_call(
        body,
        grid_spec=pltpu.PrefetchScalarGridSpec(
            num_scalar_prefetch=len(scalars),
            grid=grid,
            in_specs=[spec(a, b) for a, b in inputs],
            out_specs=[spec(o, b) for o, b in outputs],
            scratch_shapes=list(scratch),
        ),
        out_shape=[pltpu.HBM(o.shape, o.dtype) for o in out_shape] if hbm else out_shape,
        input_output_aliases={} if aliases is None else aliases,
        compiler_params=pltpu.CompilerParams(vmem_limit_bytes=vmem),
        cost_estimate=pl.CostEstimate(flops=flops, transcendentals=0, bytes_accessed=moved),
        name=name,
    )(*scalars, *arrays)


def column_tile(units):
    for tile in (1152, 1024, 768, 512, 384, 256, 128):
        if units % tile == 0:
            return tile
    return units


def row_tile(rows, most):
    tile = most
    while rows % tile:
        tile //= 2
    return tile


def keys_body(x, gain, key_w, value_w, key_gain, cosine, sine, xn_out, kv_out, raw_out):
    values = x[...].astype(F32)
    xn = (values * rms_scale(values) * (1.0 + gain[...])).astype(LOW)
    xn_out[...] = xn
    raw = contract(xn, key_w[...], ((1,), (0,)))
    raw_out[...] = raw
    unit = raw * rms_scale(raw) * (1.0 + key_gain[...])
    kv_out[:, :HD] = turn(unit, cosine[...], sine[...]).astype(LOW)
    kv_out[:, HD:] = contract(xn, value_w[...], ((1,), (0,))).astype(LOW)


def project_keys(x, gain, key_w, value_w, key_gain, cosine, sine):
    rows, dim = x.shape
    tile = row_tile(rows, 256)
    by_row = lambda width: ((tile, width), lambda i: (i, 0))
    return run(
        keys_body,
        "project_keys",
        (rows // tile,),
        [
            (x, by_row(dim)),
            (gain, None),
            (key_w, None),
            (value_w, None),
            (key_gain, None),
            (cosine, by_row(HD // 2)),
            (sine, by_row(HD // 2)),
        ],
        [
            (shape(rows, dim), by_row(dim)),
            (shape(rows, 2 * HD), by_row(2 * HD)),
            (shape(rows, HD, dtype=F32), by_row(HD)),
        ],
        flops=4 * rows * dim * HD,
    )


def queries_body(xn, own_w, first_w, second_w, gain, cosine, sine, q_out, raw_out):
    values = xn[...]
    start = 0
    for weight in (own_w, first_w, second_w):
        raw_all = contract(values, weight[...], ((1,), (0,)))
        for at in range(0, weight.shape[1], HD):
            raw = raw_all[:, at : at + HD]
            unit = raw * rms_scale(raw) * (1.0 + gain[...])
            raw_out[:, start : start + HD] = raw
            q_out[:, start : start + HD] = turn(unit, cosine[...], sine[...]).astype(LOW)
            start += HD


def project_queries(xn, heads_w, gain, cosine, sine):
    rows, dim = xn.shape
    width = sum(w.shape[1] for w in heads_w)
    tile = row_tile(rows, 256)
    by_row = lambda size: ((tile, size), lambda i: (i, 0))
    return run(
        queries_body,
        "project_queries",
        (rows // tile,),
        [(xn, by_row(dim))]
        + [(w, None) for w in heads_w]
        + [(gain, None), (cosine, by_row(HD // 2)), (sine, by_row(HD // 2))],
        [(shape(rows, width), by_row(width)), (shape(rows, width, dtype=F32), by_row(width))],
        flops=2 * rows * dim * width,
    )


def attend_body(slots, meta, q, before, own, o_out, p_out, bias):
    block, keys = bias.shape
    rows = keys // 2

    @pl.when(pl.program_id(1) == 0)
    def _():
        second = meta[0]
        first_row = second * rows + pl.program_id(0) * block
        query = first_row + lax.broadcasted_iota(jnp.int32, (block, keys), 0)
        column = lax.broadcasted_iota(jnp.int32, (block, keys), 1)
        is_own = column >= rows
        key = jnp.where(is_own, column + (second - 1) * rows, column)
        ends = jnp.int32(0)
        query_segment = jnp.zeros((block, keys), jnp.int32)
        key_segment = jnp.zeros((block, keys), jnp.int32)
        for s in range(slots):
            ends = ends + meta[1 + s]
            query_segment += (query >= ends).astype(jnp.int32)
            key_segment += (key >= ends).astype(jnp.int32)
        known = is_own | (column < second * rows)
        seen = (key < query) & (query_segment == key_segment) & (query_segment < slots) & known
        seen = seen | (is_own & (key == query))
        bias[...] = jnp.where(seen, 0.0, NEG_FILL)

    scaled = q[...] * LOW(SCALE)
    scores = jnp.concatenate(
        [
            contract(scaled, before[:, :HD], ((1,), (1,))),
            contract(scaled, own[:, :HD], ((1,), (1,))),
        ],
        axis=1,
    )
    scores = scores + bias[...]
    exps = jnp.exp(scores - jnp.max(scores, axis=1, keepdims=True))
    probs = (exps * (1.0 / jnp.sum(exps, axis=1, keepdims=True))).astype(LOW)
    p_out[...] = probs
    out = contract(probs[:, :rows], before[:, HD:], ((1,), (0,)))
    out += contract(probs[:, rows:], own[:, HD:], ((1,), (0,)))
    o_out[...] = out.astype(LOW)


def attend(meta, q, before, own):
    rows, width = q.shape
    heads = width // HD
    block = row_tile(rows, 256)
    blocks = rows // block
    slots = meta.shape[0] - 1
    head_block = ((block, HD), lambda i, h, m: (i, h))
    return run(
        lambda *refs: attend_body(slots, *refs),
        "attend",
        (blocks, heads),
        [(q, head_block), (before, None), (own, None)],
        [
            (shape(rows, width), head_block),
            (shape(heads * rows, 2 * rows), ((block, 2 * rows), lambda i, h, m: (h * blocks + i, 0))),
        ],
        scratch=[pltpu.VMEM((block, 2 * rows), F32)],
        scalars=[meta],
        flops=8 * rows * rows * width,
    )


def merge_body(o, own_w, first_w, second_w, x, post_gain, pre_gain, a_out, state_out, first_out, second_out):
    start = 0
    total = None
    for weight in (own_w, first_w, second_w):
        width = weight.shape[1]
        part = contract(o[:, start : start + width], weight[...], ((1,), (1,)))
        total = part if total is None else total + part
        start += width
    a_out[...] = total.astype(a_out.dtype)
    state = x[...].astype(F32) + total * rms_scale(total) * (1.0 + post_gain[...])
    state_out[...] = state.astype(state_out.dtype)
    z = (state * rms_scale(state) * (1.0 + pre_gain[...])).astype(LOW)
    early = pl.program_id(0) < pl.num_programs(0) // 2

    @pl.when(early)
    def _():
        first_out[...] = z

    @pl.when(jnp.logical_not(early))
    def _():
        second_out[...] = z


def merge_heads(o, heads_w, x, post_gain, pre_gain):
    rows, dim = x.shape
    width = o.shape[1]
    tile = row_tile(rows, 256)
    by_row = lambda size: ((tile, size), lambda i: (i, 0))
    half = rows // tile // 2
    return run(
        merge_body,
        "merge_heads",
        (rows // tile,),
        [(o, by_row(width))]
        + [(w, None) for w in heads_w]
        + [(x, by_row(dim)), (post_gain, None), (pre_gain, None)],
        [
            (shape(rows, dim), by_row(dim)),
            (shape(rows, dim), by_row(dim)),
            (shape(rows // 2, dim), ((tile, dim), lambda i: (jnp.minimum(i, half - 1), 0))),
            (shape(rows // 2, dim), ((tile, dim), lambda i: (jnp.maximum(i - half, 0), 0))),
        ],
        flops=2 * rows * dim * width,
    )


def ffn_forward_body(z, gate_w, up_w, down_w, *rest):
    hid_out, act_out, slope_out, f_out, acc = rest[-5:]
    step, last = pl.program_id(0), pl.num_programs(0) - 1
    tile = hid_out.shape[1]
    here = pl.ds(pl.multiple_of(step * tile, 128), tile)
    gate = contract(z[...], gate_w[:, here], ((1,), (0,)))
    up = contract(z[...], up_w[:, here], ((1,), (0,)))
    square = gate * gate
    tanh = jnp.tanh(ROOT * gate * (1.0 + CUBIC * square))
    half = 0.5 * (1.0 + tanh)
    act = gate * half
    slope = half + 0.5 * gate * (1.0 - tanh * tanh) * (ROOT * (1.0 + 3.0 * CUBIC * square))
    hid = (act * up).astype(LOW)
    hid_out[...] = hid
    act_out[...] = act.astype(LOW)
    slope_out[...] = (slope * up).astype(LOW)
    add_to(acc, contract(hid, down_w[:, here], ((1,), (1,))), step == 0)

    @pl.when(step == last)
    def _():
        f_out[...] = acc[...].astype(f_out.dtype)


def ffn_forward(z, z_block, rows, weights, block, total, kept, out_dtype):
    dim, units = weights[0].shape
    tile = column_tile(units)
    inner = ((rows, tile), lambda j: (block, j))
    extra = [] if kept is None else list(kept)
    return run(
        ffn_forward_body,
        "ffn_forward",
        (units // tile,),
        [(z, ((rows, dim), lambda j: (z_block, 0)))]
        + [(w, "vmem") for w in weights]
        + [(k, "any") for k in extra],
        [(shape(total, units), inner)] * 3 + [(shape(rows, dim, dtype=out_dtype), None)],
        scratch=[pltpu.VMEM((rows, dim), F32)],
        aliases={4 + i: i for i in range(len(extra))},
        flops=6 * rows * dim * units,
    )


def ffn_end_body(f_own, f_other, state, cotangent, gain, *rest):
    out, df_out, gain_out = rest[-3:]
    f = f_own[...] + f_other[...].astype(F32)
    out[...] = (state[...].astype(F32) + f * rms_scale(f) * (1.0 + gain[...])).astype(LOW)
    df, gain_grad = rms_back(f, gain[...], cotangent[...].astype(F32))
    df_out[...] = df.astype(LOW)
    add_to(gain_out, gain_grad, pl.program_id(0) == 0)


def ffn_end(f_own, f_other, state, cotangent, gain, chunk, out):
    rows, dim = f_own.shape
    tile = row_tile(rows, 128)
    steps = rows // tile
    here = ((tile, dim), lambda i: (i, 0))
    there = ((tile, dim), lambda i: (chunk * steps + i, 0))
    extra = [] if out is None else [out]
    return run(
        ffn_end_body,
        "ffn_end",
        (steps,),
        [(f_own, here), (f_other, here), (state, there), (cotangent, there), (gain, None)]
        + [(e, "any") for e in extra],
        [(shape(*state.shape), there), (shape(rows, dim), here), (shape(1, dim, dtype=F32), None)],
        aliases={5: 0} if extra else None,
    )


def ffn_backward_body(pieces, splits, *refs):
    dfs = refs[:pieces]
    act, slope, gate_w, up_w, down_w = refs[pieces : pieces + 5]
    *outs, acc, df = refs[pieces + 5 :]
    dgate_out, dup_out, *dz_outs = outs[-2 - splits :]
    step, last = pl.program_id(0), pl.num_programs(0) - 1

    @pl.when(step == 0)
    def _():
        at = 0
        for piece in dfs:
            df[at : at + piece.shape[0]] = piece[...]
            at += piece.shape[0]

    tile = dup_out.shape[1]
    if gate_w.shape[1] == tile:
        here = slice(None)
    else:
        here = pl.ds(pl.multiple_of(step * tile, 128), tile)
    dhid = contract(df[...], down_w[:, here], ((1,), (0,)))
    dup = (dhid * act[...].astype(F32)).astype(LOW)
    dgate = (dhid * slope[...].astype(F32)).astype(LOW)
    dup_out[...] = dup
    dgate_out[...] = dgate
    part = contract(dgate, gate_w[:, here], ((1,), (1,)))
    part += contract(dup, up_w[:, here], ((1,), (1,)))
    add_to(acc, part, step == 0)

    @pl.when(step == last)
    def _():
        at = 0
        for dz_out in dz_outs:
            size = dz_out.shape[0]
            dz_out[...] = acc[at : at + size].astype(dz_out.dtype)
            at += size


def ffn_backward(dfs, act, slope, weights, block, made, out_dtype, splits, resident):
    rows = sum(d.shape[0] for d in dfs)
    total, units = act.shape
    dim = dfs[0].shape[1]
    tile = column_tile(units)
    inner = ((rows, tile), lambda j: (block, j))
    weight = "vmem" if resident else ((dim, tile), lambda j: (0, j))
    extra = [] if made is None else list(made)
    return run(
        lambda *refs: ffn_backward_body(len(dfs), splits, *refs),
        "ffn_backward",
        (units // tile,),
        [(d, None) for d in dfs]
        + [(act, inner), (slope, inner)]
        + [(w, weight) for w in weights]
        + [(e, "any") for e in extra],
        [(shape(total, units), inner)] * 2
        + [(shape(rows // splits, dim, dtype=out_dtype), None)] * splits,
        scratch=[pltpu.VMEM((rows, dim), F32), pltpu.VMEM((rows, dim), LOW)],
        aliases={len(dfs) + 5 + i: i for i in range(len(extra))},
        flops=6 * rows * dim * units,
        vmem=VMEM_BESIDE if resident else VMEM_BYTES,
    )


def weight_grad_body(sides, core, *refs):
    *inputs, send, keep = refs
    groups, rows, _ = keep.shape
    first = core[0] == 0

    def write(lefts, right):
        at = 0
        total = None
        for left in lefts:
            size = left.shape[0]
            part = contract(left[...], right[at : at + size], ((0,), (0,)))
            total = part if total is None else total + part
            at += size
        for i in range(groups):
            even = total[2 * i * rows : (2 * i + 1) * rows].astype(LOW)
            odd = total[(2 * i + 1) * rows : (2 * i + 2) * rows].astype(LOW)
            send[i] = jnp.where(first, odd, even)
            keep[i] = jnp.where(first, even, odd)

    at = 0
    for side, count in enumerate(sides):
        lefts, right = inputs[at : at + count], inputs[at + count]
        at += count + 1
        if len(sides) == 1:
            write(lefts, right)
        else:
            mine = (pl.program_id(0) % len(sides)) == side
            pl.when(mine)(lambda lefts=lefts, right=right: write(lefts, right))


def weight_grad(
    pairs, core, axis_size, start, stop, tile=None, columns_of=None, vmem=VMEM_BYTES
):
    dim = pairs[0][0][0].shape[1]
    columns = stop - start
    rows = dim // axis_size
    groups = axis_size // 2
    tile = column_tile(columns) if tile is None else tile
    blocks = columns // tile
    if columns_of is None:
        columns_of = lambda j, c: j + start // tile
    if rows % 8:
        full = []
        for j in range(blocks):
            lefts, right = pairs[j % len(pairs)]
            left = jnp.concatenate(lefts, axis=0)
            at = columns_of(j, core) * tile
            here = lax.dynamic_slice_in_dim(right, at, tile, axis=1)
            full.append(contract(left, here, ((0,), (0,))).astype(LOW))
        full = jnp.concatenate(full, axis=1).reshape(groups, 2, rows, columns)
        return (
            lax.dynamic_index_in_dim(full, 1 - core, axis=1, keepdims=False),
            lax.dynamic_index_in_dim(full, core, axis=1, keepdims=False),
        )
    inputs = []
    for lefts, right in pairs:
        inputs += [(left, None) for left in lefts]
        inputs.append((right, ((right.shape[0], tile), lambda j, c: (0, columns_of(j, c[0])))))
    out = (shape(groups, rows, columns), ((groups, rows, tile), lambda j, c: (0, 0, j)))
    sides = [len(lefts) for lefts, _ in pairs]
    return run(
        lambda *refs: weight_grad_body(sides, *refs),
        "weight_grad",
        (blocks,),
        inputs,
        [out, out],
        scalars=[core.reshape(1)],
        flops=2 * pairs[0][1].shape[0] * dim * columns,
        vmem=vmem,
    )


def state_back_body(
    dz_own, dz_first, dz_second, state, a, cotangent, pre_gain, post_gain, own_w, first_w, second_w,
    dh_out, da_out, do_out, pre_out, post_out,
):
    first = pl.program_id(0) == 0
    early = pl.program_id(0) < pl.num_programs(0) // 2
    dz = dz_own[...].astype(F32) + jnp.where(early, dz_first[...], dz_second[...]).astype(F32)
    back, pre_grad = rms_back(state[...].astype(F32), pre_gain[...], dz)
    dh = cotangent[...].astype(F32) + back
    dh_out[...] = dh.astype(dh_out.dtype)
    da, post_grad = rms_back(a[...].astype(F32), post_gain[...], dh)
    da = da.astype(LOW)
    da_out[...] = da
    add_to(pre_out, pre_grad, first)
    add_to(post_out, post_grad, first)
    at = 0
    for weight in (own_w, first_w, second_w):
        width = weight.shape[1]
        do_out[:, at : at + width] = contract(da, weight[...], ((1,), (0,))).astype(LOW)
        at += width


def state_back(dz_own, dz_other, state, a, cotangent, pre_gain, post_gain, heads_w):
    rows, dim = state.shape
    width = sum(w.shape[1] for w in heads_w)
    tile = row_tile(rows, 256)
    steps = rows // tile
    by_row = lambda size: ((tile, size), lambda i: (i, 0))
    return run(
        state_back_body,
        "state_back",
        (rows // tile,),
        [
            (dz_own, by_row(dim)),
            (dz_other[0], ((tile, dim), lambda i: (jnp.minimum(i, steps // 2 - 1), 0))),
            (dz_other[1], ((tile, dim), lambda i: (jnp.maximum(i - steps // 2, 0), 0))),
        ]
        + [(v, by_row(dim)) for v in (state, a, cotangent)]
        + [(v, None) for v in (pre_gain, post_gain, *heads_w)],
        [
            (shape(rows, dim), by_row(dim)),
            (shape(rows, dim), by_row(dim)),
            (shape(rows, width), by_row(width)),
            (shape(1, dim, dtype=F32), None),
            (shape(1, dim, dtype=F32), None),
        ],
        vmem=VMEM_BYTES,
        flops=2 * rows * dim * width,
    )


def attend_back_body(
    p, do, q, raw, before, own, gain, cosine, sine, dq_out, before_out, own_out, gain_out, acc
):
    head, part = pl.program_id(0), pl.program_id(1)
    first = (head == 0) & (part == 0)
    last = (head == pl.num_programs(0) - 1) & (part == pl.num_programs(1) - 1)
    rows = before.shape[0]
    dp = jnp.concatenate(
        [
            contract(do[...], before[:, HD:], ((1,), (1,))),
            contract(do[...], own[:, HD:], ((1,), (1,))),
        ],
        axis=1,
    )
    probs = p[...].astype(F32)
    weighted = probs * dp
    ds = (weighted - probs * jnp.sum(weighted, axis=1, keepdims=True)).astype(LOW)
    dq = contract(ds[:, :rows], before[:, :HD], ((1,), (0,)))
    dq += contract(ds[:, rows:], own[:, :HD], ((1,), (0,)))
    dk = contract(ds, q[...], ((0,), (0,))) * SCALE
    dv = contract(p[...], do[...], ((0,), (0,)))
    add_to(acc, jnp.concatenate([dk, dv], axis=1), first)
    back = turn_back(dq * SCALE, cosine[...], sine[...])
    dq_raw, gain_grad = rms_back(raw[...], gain[...], back)
    dq_out[...] = dq_raw.astype(LOW)
    add_to(gain_out, gain_grad, first)

    @pl.when(last)
    def _():
        before_out[...] = acc[:rows].astype(LOW)
        own_out[...] = acc[rows:]


def attend_back(p, do, q, raw, before, own, gain, cosine, sine):
    rows, width = q.shape
    heads = width // HD
    block = row_tile(rows, 256)
    blocks = rows // block
    head_block = ((block, HD), lambda h, i: (i, h))
    table = ((block, HD // 2), lambda h, i: (i, 0))
    return run(
        attend_back_body,
        "attend_back",
        (heads, blocks),
        [
            (p, ((block, 2 * rows), lambda h, i: (h * blocks + i, 0))),
            (do, head_block),
            (q, head_block),
            (raw, head_block),
            (before, None),
            (own, None),
            (gain, None),
            (cosine, table),
            (sine, table),
        ],
        [
            (shape(rows, width), head_block),
            (shape(rows, 2 * HD), None),
            (shape(rows, 2 * HD, dtype=F32), None),
            (shape(1, HD, dtype=F32), None),
        ],
        scratch=[pltpu.VMEM((2 * rows, 2 * HD), F32)],
        vmem=VMEM_BYTES,
        flops=16 * rows * rows * width,
    )


def input_back_body(
    dq, dkv_own, dkv_other, raw, cosine, sine, x, dh, key_gain, in_gain,
    own_w, first_w, second_w, key_w, value_w,
    grad_out, dkv_out, key_gain_out, in_gain_out,
):
    first = pl.program_id(0) == 0
    dkv = dkv_own[...] + dkv_other[...].astype(F32)
    back = turn_back(dkv[:, :HD], cosine[...], sine[...])
    dk, key_grad = rms_back(raw[...], key_gain[...], back)
    dk = dk.astype(LOW)
    dv = dkv[:, HD:].astype(LOW)
    dkv_out[:, :HD] = dk
    dkv_out[:, HD:] = dv
    add_to(key_gain_out, key_grad, first)
    dxn = contract(dk, key_w[...], ((1,), (1,))) + contract(dv, value_w[...], ((1,), (1,)))
    at = 0
    for weight in (own_w, first_w, second_w):
        width = weight.shape[1]
        dxn += contract(dq[:, at : at + width], weight[...], ((1,), (1,)))
        at += width
    dx, in_grad = rms_back(x[...].astype(F32), in_gain[...], dxn)
    grad_out[...] = (dh[...].astype(F32) + dx).astype(LOW)
    add_to(in_gain_out, in_grad, first)


def input_back(dq, dkv_own, dkv_other, raw, cosine, sine, x, dh, key_gain, in_gain, weights):
    rows, dim = x.shape
    width = dq.shape[1]
    tile = row_tile(rows, 256)
    by_row = lambda size: ((tile, size), lambda i: (i, 0))
    return run(
        input_back_body,
        "input_back",
        (rows // tile,),
        [(v, by_row(v.shape[1])) for v in (dq, dkv_own, dkv_other, raw, cosine, sine, x, dh)]
        + [(v, None) for v in (key_gain, in_gain, *weights)],
        [
            (shape(rows, dim), by_row(dim)),
            (shape(rows, 2 * HD), by_row(2 * HD)),
            (shape(1, HD, dtype=F32), None),
            (shape(1, dim, dtype=F32), None),
        ],
        vmem=VMEM_BYTES,
        flops=2 * rows * dim * (width + 2 * HD),
    )


def swap_head(value):
    return lax.ppermute(value, "head", [(0, 1), (1, 0)])


def pair(axis_size, bit):
    return [(i, i ^ (1 << bit)) for i in range(axis_size)]


def tie(*values):
    return lax.optimization_barrier(values)


def sum_parts(parts, choice, columns, dtype):
    total = None
    for array, own, at in parts:
        rows = array.shape[-2]
        value = lax.dynamic_slice(
            array.reshape((2,) * len(own) + array.shape[-2:]),
            [choice.get(b, 0) for b in own] + [0, at],
            [1 if b in choice else 2 for b in own] + [rows, columns],
        )
        value = value.reshape((2,) * sum(b not in choice for b in own) + (rows, columns))
        value = value.astype(F32)
        total = value if total is None else total + value
    return total.astype(dtype)


class Scatter:
    def __init__(self, size, index, order, bits, parts, columns, out=None, low=LOW):
        self.size, self.index, self.order, self.low = size, index, list(order), low
        self.bits, self.parts, self.columns, self.out = list(bits), list(parts), columns, out
        self.gone, self.loaded, self.flying, self.cuts = [], out is not None, False, None
        if out is None:
            self.load()
        else:
            self.drop()

    def value(self, bit):
        return (self.index >> bit) & 1

    def drop(self):
        bit = self.order[0]
        if bit == "head":
            self.columns //= 2
        else:
            self.bits.remove(bit)
            self.gone.append(bit)

    def load(self):
        if not self.order:
            return
        bit = self.order[0]
        choice = {b: self.value(b) for b in self.gone}
        parts, columns = self.parts, self.columns
        if bit == "head":
            columns //= 2
            parts = [(p, own, at + columns) for p, own, at in parts]
        else:
            choice[bit] = 1 - self.value(bit)
        self.out = sum_parts(parts, choice, columns, self.low)
        self.loaded = True
        self.drop()

    def go(self):
        bit = self.order.pop(0)
        if bit == "head":
            self.got = swap_head(self.out)
        else:
            self.got = lax.ppermute(self.out, "dp", pair(self.size, bit))
        self.loaded, self.flying = False, True
        return self

    def take(self):
        self.parts = self.parts + [(self.got, list(self.bits), 0)]
        self.flying = False
        return self

    def land(self):
        self.take().load()
        return self

    def finish(self):
        if self.flying:
            self.take()
        while self.order:
            if not self.loaded:
                self.load()
            self.go().take()
        choice = {b: self.value(b) for b in self.gone}
        return sum_parts(self.parts, choice, self.columns, F32)


class Joint:
    def __init__(self, items):
        self.items, self.cuts = items, None
        self.join()

    def join(self):
        self.order = self.items[0].order
        if self.order:
            self.out = jnp.concatenate([s.out for s in self.items], axis=-1)

    def load(self):
        for s in self.items:
            if not s.loaded:
                s.load()
        self.join()

    def go(self):
        bit = self.order[0]
        self.got = lax.ppermute(self.out, "dp", pair(self.items[0].size, bit))
        for s in self.items:
            s.order.pop(0)
            s.loaded = False
        return self

    def take(self):
        at = 0
        for s in self.items:
            s.parts = s.parts + [(self.got, list(s.bits), at)]
            at += s.columns
        return self


def load_body(*refs):
    count = (len(refs) - 1) // 2
    sems = refs[-1]
    copies = [
        pltpu.make_async_copy(source, target, sems.at[i])
        for i, (source, target) in enumerate(zip(refs[:count], refs[count : 2 * count]))
    ]
    for copy in copies:
        copy.start()
    for copy in copies:
        copy.wait()


def load_weights(weights):
    return pl.pallas_call(
        load_body,
        in_specs=[pl.BlockSpec(memory_space=pl.ANY)] * len(weights),
        out_specs=[pl.BlockSpec(memory_space=pltpu.VMEM)] * len(weights),
        out_shape=[pltpu.VMEM(w.shape, w.dtype) for w in weights],
        scratch_shapes=[pltpu.SemaphoreType.DMA((len(weights),))],
        compiler_params=pltpu.CompilerParams(vmem_limit_bytes=VMEM_BESIDE),
        name="load_weights",
    )(*weights)


def angle_tables(lengths, head_index, rows):
    ids = head_index * rows + jnp.arange(rows, dtype=jnp.int32)
    begin = jnp.zeros_like(ids)
    end = jnp.int32(0)
    for s in range(lengths.shape[0]):
        end = end + lengths[s]
        begin = jnp.where(ids >= end, end, begin)
    frequency = np.power(ROPE_BASE, -2.0 * np.arange(HD // 2) / HD).astype(np.float32)
    grid = (ids - begin).astype(F32)[:, None] * frequency[None, :]
    return jnp.cos(grid), jnp.sin(grid)


def on_device(
    layer_input,
    seq_lengths,
    input_gain,
    query_weight,
    key_weight,
    value_weight,
    query_gain,
    key_gain,
    output_weight,
    post_attn_gain,
    pre_ffn_gain,
    gate_weight,
    up_weight,
    down_weight,
    post_ffn_gain,
    out_cotangent,
):
    rows = layer_input.shape[0]
    dp_size = lax.axis_size("dp")
    bit_count = dp_size.bit_length() - 1
    dp_index = lax.axis_index("dp")
    head_index = lax.axis_index("head")
    core = dp_index & 1
    core_pairs = pair(dp_size, 0)
    width = query_weight.shape[1]
    in_gain, q_gain, k_gain, post_gain, pre_gain, end_gain = (
        g.reshape(1, -1)
        for g in (input_gain, query_gain, key_gain, post_attn_gain, pre_ffn_gain, post_ffn_gain)
    )

    query_mine = lax.dynamic_slice_in_dim(query_weight, core * HD, HD, axis=1)
    output_mine = lax.dynamic_slice_in_dim(output_weight, core * HD, HD, axis=1)
    query_mine, output_mine, layer_input, seq_lengths = tie(
        query_mine, output_mine, layer_input, seq_lengths
    )
    query_first = swap_head(query_mine)

    cosine, sine = angle_tables(seq_lengths[0], head_index, rows)
    meta = jnp.concatenate([head_index.reshape(1).astype(jnp.int32), seq_lengths[0]])
    xn, kv_own, k_raw = project_keys(
        layer_input, in_gain, key_weight, value_weight, k_gain, cosine, sine
    )
    kv_before = lax.ppermute(kv_own, "head", [(0, 1)])
    query_first, kv_own, *weights = tie(
        query_first, kv_own, gate_weight, up_weight, down_weight
    )
    query_second = lax.ppermute(query_first, "dp", core_pairs)
    weights = load_weights(weights)
    xn_in, kv_before, output_mine, *weights = tie(xn, kv_before, output_mine, *weights)
    output_first = swap_head(output_mine)
    weights = [pltpu.with_memory_space_constraint(w, pltpu.VMEM) for w in weights]
    query_w = (query_weight, query_first, query_second)

    q_low, q_raw = project_queries(xn_in, query_w, q_gain, cosine, sine)
    attn_out, probs = attend(meta, q_low, kv_before, kv_own)
    attn_out, output_first = tie(attn_out, output_first)
    output_second = lax.ppermute(output_first, "dp", core_pairs)
    output_w = (output_weight, output_first, output_second)
    attn_proj, state, *z_own = merge_heads(attn_out, output_w, layer_input, post_gain, pre_gain)

    half = rows // 2
    total = 2 * rows
    z_other = [swap_head(z) for z in z_own]
    *kept, f_own0 = ffn_forward(z_own[0], 0, half, weights, 0, total, None, F32)
    z_in, f_own0 = tie(z_other[0], f_own0)
    *kept, f_send0 = ffn_forward(z_in, 0, half, weights, 2, total, kept, LOW)
    z_in, f_send0 = tie(z_other[1], f_send0)
    *kept, f_send1 = ffn_forward(z_in, 0, half, weights, 3, total, kept, LOW)
    f_got0 = swap_head(f_send0)
    z_in, f_send1 = tie(z_own[1], f_send1)
    f_got1 = swap_head(f_send1)
    *kept, f_own1 = ffn_forward(z_in, 0, half, weights, 1, total, kept, F32)
    hid, act, slope = kept
    f_got0, f_own0, f_own1 = tie(f_got0, f_own0, f_own1)
    layer_output, df_own0, end_grad0 = ffn_end(
        f_own0, f_got0, state, out_cotangent, end_gain, 0, None
    )
    df_other0 = swap_head(df_own0)
    layer_output, df_own1, end_grad1 = ffn_end(
        f_own1, f_got1, state, out_cotangent, end_gain, 1, layer_output
    )
    df_other1 = swap_head(df_own1)
    df_own = [df_own0, df_own1]
    *made, own_zgrad = ffn_backward(df_own, act, slope, weights, 0, None, LOW, 1, True)
    df_other0, df_other1, own_zgrad = tie(df_other0, df_other1, own_zgrad)
    df_other = [df_other0, df_other1]
    units = hid.shape[1]
    order = list(range(bit_count))
    rest = order[1:]
    leading = rest[::-1]
    third = units // 3

    def start(pairs, first, last, route=order, **options):
        send, keep = weight_grad(pairs, core, dp_size, first, last, **options)
        columns = last - first
        return Scatter(
            dp_size, dp_index, route, order[::-1], [(keep, leading, 0)], columns, send
        )

    def cut(whole, at, columns, route=rest):
        parts = [(p, own, at) for p, own, _ in whole.parts]
        return Scatter(dp_size, dp_index, route, leading, parts, columns)

    def later(value, scatter):
        tied = tie(*[p for p, _, _ in scatter.parts], value)
        scatter.parts = [(p, own, at) for p, (_, own, at) in zip(tied, scatter.parts)]

    def phase(values, end=(), go=(), now=(), hold=()):
        count = len(values)
        done = list(end) + list(now) + list(hold)
        tied = list(tie(*values, *[s.got for s in done], *[s.out for s in go]))
        for s in go[::-1]:
            s.out = tied.pop()
        for s in done[::-1]:
            s.got = tied.pop()
            s.take()
        for s in go:
            s.go()
        for s in list(now) + [s for s in end if s.cuts is None]:
            s.load()
        if now:
            tied = list(tie(*tied, *[s.out for s in now]))
            for s in now[::-1]:
                s.out = tied.pop()
                s.go()
        return tied

    df_all = df_own + df_other
    down_a = start([(df_all, hid)], 0, 2 * third, vmem=VMEM_BESIDE)
    (hid,) = phase([hid], go=[down_a])
    down_b = start([(df_all, hid)], 2 * third, units, vmem=VMEM_BESIDE)
    down_a.cuts = down_b.cuts = 1
    (df_other0,) = phase([df_other0], end=[down_a], go=[down_b])
    d1 = cut(down_a, 0, 2 * third)
    (df_other0,) = phase([df_other0], go=[d1])
    *made, dz0, dz1 = ffn_backward(
        [df_other0, df_other1],
        act,
        slope,
        (gate_weight, up_weight, down_weight),
        1,
        made,
        LOW,
        2,
        False,
    )
    dgate, dup = made
    dz0, dz1, dgate = phase([dz0, dz1, dgate], end=[down_b, d1])
    d2 = cut(down_b, 0, third)
    dz0, dz1, dgate = phase([dz0, dz1, dgate], go=[d2])
    other0 = swap_head(dz0)
    z_both = z_own + z_other
    gate_s = start([(z_both, dgate)], 0, units)
    other0, dz1, dup = phase([other0, dz1, dup], end=[d2], go=[gate_s, d1])
    other1 = swap_head(dz1)
    up_s = start([(z_both, dup)], 0, units)
    gate_s.cuts = up_s.cuts = 1
    own_zgrad, other0, other1 = phase(
        [own_zgrad, other0, other1], end=[gate_s], go=[up_s, d2], hold=[d1]
    )
    g1 = cut(gate_s, 0, 2 * third)
    (own_zgrad,) = phase([own_zgrad], go=[g1])
    other_zgrad = [other0, other1]

    state_grad, attn_grad, heads_grad, pre_grad, post_grad = state_back(
        own_zgrad, other_zgrad, state, attn_proj, out_cotangent, pre_gain, post_gain, output_w
    )

    own_heads = width // HD

    def head_block(j, c):
        return jnp.where(j < own_heads, j, own_heads + ((j - own_heads) ^ c))

    def start_heads(left, right):
        route = [order[0], "head"] + rest
        return start([([left], right)], 0, 2 * width, route, tile=HD, columns_of=head_block)

    dq, kv_back_send, kv_grad, q_gain_grad = attend_back(
        probs, heads_grad, q_low, q_raw, kv_before, kv_own, q_gain, cosine, sine
    )
    attn_grad, dq = tie(attn_grad, dq)
    output_s = start_heads(attn_grad, attn_out)
    later(output_s.out, gate_s)
    later(output_s.out, d1)
    d1.load()
    g2 = cut(gate_s, 2 * third, third)
    dq, kv_back_send = phase(
        [dq, kv_back_send], end=[up_s, g1, d2], go=[g2, output_s, d1]
    )
    kv_back = lax.ppermute(kv_back_send, "head", [(1, 0)])
    query_s = start_heads(xn, dq)
    later(query_s.out, up_s)
    u1 = cut(up_s, 0, 2 * third)
    dq, kv_grad, kv_back = phase(
        [dq, kv_grad, kv_back], end=[g2, d1], go=[query_s, u1, g1, d2], now=[output_s]
    )
    input_grad, dkv, k_gain_grad, in_gain_grad = input_back(
        dq, kv_grad, kv_back, k_raw, cosine, sine, layer_input, state_grad, k_gain, in_gain,
        query_w + (key_weight, value_weight),
    )
    kv_s = start([([xn], dkv)], 0, 2 * HD)
    later(kv_s.out, up_s)
    u2 = cut(up_s, 2 * third, third)
    (wait,) = phase(
        [in_gain_grad], end=[u1, d2, output_s], go=[u2, kv_s, g2], now=[query_s, g1]
    )
    gains = [wait, post_grad, pre_grad, end_grad0 + end_grad1, q_gain_grad, k_gain_grad]
    gains = [g.reshape(dp_size, -1) for g in gains]
    widths = [g.shape[1] for g in gains]
    block = layer_input.shape[1] // dp_size
    packed = jnp.concatenate(gains, axis=1)
    packed = jnp.pad(packed, ((0, 0), (0, block * 128 - packed.shape[1])))
    packed = packed.reshape(dp_size // 2, 2, block, 128).astype(LOW)
    packed = jnp.concatenate([packed[:, 0], packed[:, 1]], axis=2)
    gains_s = Scatter(dp_size, dp_index, rest, leading, [(packed, leading, 0)], 256)
    wait, query_s.got, kv_s.got, u2.got, gains_s.out = tie(
        wait, query_s.got, kv_s.got, u2.got, gains_s.out
    )
    for s in (query_s, kv_s, u2):
        s.take().load()
    tail = Joint([output_s, query_s, kv_s, gains_s])
    up_both = Joint([u1, u2])
    (wait,) = phase([wait], end=[g1], go=[tail, up_both], now=[g2])
    (wait,) = phase([wait], end=[g2], now=[tail, up_both])
    (wait,) = phase([wait], end=[up_both], now=[tail])
    (wait,) = phase([wait], end=[tail])
    down_part = jnp.concatenate([d1.finish(), d2.finish()], axis=1)
    gate_part = jnp.concatenate([g1.finish(), g2.finish()], axis=1)
    up_part = jnp.concatenate([u1.finish(), u2.finish()], axis=1)
    output_part = output_s.finish()
    query_part = query_s.finish()
    packed = gains_s.finish()
    pick = lambda which: lax.dynamic_slice_in_dim(packed, which * 128, 128, axis=1)
    packed = pick(core) + lax.ppermute(pick(1 - core), "dp", core_pairs)
    kv_sum = jnp.concatenate([kv_s.finish(), packed], axis=1)
    kv_sum = kv_sum + swap_head(kv_sum)
    packed = kv_sum[:, 2 * HD :].reshape(-1)
    pieces = []
    at = 0
    for size in widths:
        pieces.append(packed[at : at + size])
        at += size
    return (
        layer_output,
        input_grad,
        pieces[0],
        query_part,
        kv_sum[:, :HD],
        kv_sum[:, HD : 2 * HD],
        pieces[4],
        pieces[5],
        output_part,
        pieces[1],
        pieces[2],
        gate_part,
        up_part,
        down_part,
        pieces[3],
    )


def solution(mesh):
    placed = (
        P(("dp", "head"), None),
        P("dp", None),
        P(),
        P(None, "head"),
        P(),
        P(),
        P(),
        P(),
        P(None, "head"),
        P(),
        P(),
        P(None, "head"),
        P(None, "head"),
        P(None, "head"),
        P(),
        P(("dp", "head"), None),
    )
    return jax.shard_map(
        on_device,
        mesh=mesh,
        in_specs=placed,
        out_specs=(
            P(("dp", "head"), None),
            P(("dp", "head"), None),
            P("dp"),
            P("dp", "head"),
            P("dp", None),
            P("dp", None),
            P("dp"),
            P("dp"),
            P("dp", "head"),
            P("dp"),
            P("dp"),
            P("dp", "head"),
            P("dp", "head"),
            P("dp", "head"),
            P("dp"),
        ),
        check_vma=False,
    )
```

```python
import jax
import jax.numpy as jnp
import numpy as np
from jax import lax
from jax.experimental import pallas as pl
from jax.experimental.pallas import tpu as pltpu
from jax.sharding import PartitionSpec as P

HD = 256
EPSILON = 1e-06
ROPE_BASE = 1000000.0
NEG_FILL = -1e30
LOW = jnp.bfloat16
F32 = jnp.float32
ROOT = 0.7978845608028654
CUBIC = 0.044715
SCALE = HD ** (-0.5)
VMEM_BESIDE = 30 << 20
VMEM_BYTES = 60 << 20


def shape(*dims, dtype=LOW):
    return jax.ShapeDtypeStruct(dims, dtype)


def contract(left, right, dims):
    return lax.dot_general(left, right, (dims, ((), ())), preferred_element_type=F32)


def rms_scale(values):
    return lax.rsqrt(jnp.mean(values * values, axis=-1, keepdims=True) + EPSILON)


def rms_back(values, gain, cotangent):
    scale = rms_scale(values)
    unit = values * scale
    scaled = cotangent * (1.0 + gain)
    back = scale * (scaled - unit * jnp.mean(scaled * unit, axis=-1, keepdims=True))
    return back, jnp.sum(cotangent * unit, axis=0, keepdims=True)


def turn(values, cosine, sine):
    half = HD // 2
    first, second = values[:, :half], values[:, half:]
    return jnp.concatenate([first * cosine - second * sine, second * cosine + first * sine], axis=1)


def turn_back(values, cosine, sine):
    return turn(values, cosine, -sine)


def add_to(ref, value, first):
    @pl.when(first)
    def _():
        ref[...] = value

    @pl.when(jnp.logical_not(first))
    def _():
        ref[...] += value


def run(body, name, grid, inputs, outputs, scratch=(), scalars=(), aliases=None, flops=0, vmem=VMEM_BESIDE, hbm=True):
    def spec(array, block):
        if block is None:
            dims = tuple(array.shape)
            return pl.BlockSpec(dims, lambda *_: (0,) * len(dims))
        if block == "any":
            return pl.BlockSpec(memory_space=pl.ANY)
        if block == "vmem":
            return pl.BlockSpec(memory_space=pltpu.VMEM)
        return pl.BlockSpec(*block)

    arrays = [a for a, _ in inputs]
    out_shape = [o for o, _ in outputs]
    if hbm:
        arrays = [
            a if b == "vmem" else pltpu.with_memory_space_constraint(a, pltpu.HBM)
            for a, b in inputs
        ]
    moved = sum(a.size * a.dtype.itemsize for a, _ in inputs)
    moved += sum(int(np.prod(o.shape)) * o.dtype.itemsize for o in out_shape)
    return pl.pallas_call(
        body,
        grid_spec=pltpu.PrefetchScalarGridSpec(
            num_scalar_prefetch=len(scalars),
            grid=grid,
            in_specs=[spec(a, b) for a, b in inputs],
            out_specs=[spec(o, b) for o, b in outputs],
            scratch_shapes=list(scratch),
        ),
        out_shape=[pltpu.HBM(o.shape, o.dtype) for o in out_shape] if hbm else out_shape,
        input_output_aliases={} if aliases is None else aliases,
        compiler_params=pltpu.CompilerParams(vmem_limit_bytes=vmem),
        cost_estimate=pl.CostEstimate(flops=flops, transcendentals=0, bytes_accessed=moved),
        name=name,
    )(*scalars, *arrays)


def column_tile(units):
    for tile in (1152, 1024, 768, 512, 384, 256, 128):
        if units % tile == 0:
            return tile
    return units


def row_tile(rows, most):
    tile = most
    while rows % tile:
        tile //= 2
    return tile


def keys_body(x, gain, key_w, value_w, key_gain, cosine, sine, xn_out, kv_out, raw_out):
    values = x[...].astype(F32)
    xn = (values * rms_scale(values) * (1.0 + gain[...])).astype(LOW)
    xn_out[...] = xn
    raw = contract(xn, key_w[...], ((1,), (0,)))
    raw_out[...] = raw
    unit = raw * rms_scale(raw) * (1.0 + key_gain[...])
    kv_out[:, :HD] = turn(unit, cosine[...], sine[...]).astype(LOW)
    kv_out[:, HD:] = contract(xn, value_w[...], ((1,), (0,))).astype(LOW)


def project_keys(x, gain, key_w, value_w, key_gain, cosine, sine):
    rows, dim = x.shape
    tile = row_tile(rows, 256)
    by_row = lambda width: ((tile, width), lambda i: (i, 0))
    return run(
        keys_body,
        "project_keys",
        (rows // tile,),
        [
            (x, by_row(dim)),
            (gain, None),
            (key_w, None),
            (value_w, None),
            (key_gain, None),
            (cosine, by_row(HD // 2)),
            (sine, by_row(HD // 2)),
        ],
        [
            (shape(rows, dim), by_row(dim)),
            (shape(rows, 2 * HD), by_row(2 * HD)),
            (shape(rows, HD, dtype=F32), by_row(HD)),
        ],
        flops=4 * rows * dim * HD,
    )


def queries_body(xn, own_w, first_w, second_w, gain, cosine, sine, q_out, raw_out):
    values = xn[...]
    start = 0
    for weight in (own_w, first_w, second_w):
        raw_all = contract(values, weight[...], ((1,), (0,)))
        for at in range(0, weight.shape[1], HD):
            raw = raw_all[:, at : at + HD]
            unit = raw * rms_scale(raw) * (1.0 + gain[...])
            raw_out[:, start : start + HD] = raw
            q_out[:, start : start + HD] = turn(unit, cosine[...], sine[...]).astype(LOW)
            start += HD


def project_queries(xn, heads_w, gain, cosine, sine):
    rows, dim = xn.shape
    width = sum(w.shape[1] for w in heads_w)
    tile = row_tile(rows, 256)
    by_row = lambda size: ((tile, size), lambda i: (i, 0))
    return run(
        queries_body,
        "project_queries",
        (rows // tile,),
        [(xn, by_row(dim))]
        + [(w, None) for w in heads_w]
        + [(gain, None), (cosine, by_row(HD // 2)), (sine, by_row(HD // 2))],
        [(shape(rows, width), by_row(width)), (shape(rows, width, dtype=F32), by_row(width))],
        flops=2 * rows * dim * width,
    )


def attend_body(slots, meta, q, before, own, o_out, p_out, bias):
    block, keys = bias.shape
    rows = keys // 2

    @pl.when(pl.program_id(1) == 0)
    def _():
        second = meta[0]
        first_row = second * rows + pl.program_id(0) * block
        query = first_row + lax.broadcasted_iota(jnp.int32, (block, keys), 0)
        column = lax.broadcasted_iota(jnp.int32, (block, keys), 1)
        is_own = column >= rows
        key = jnp.where(is_own, column + (second - 1) * rows, column)
        ends = jnp.int32(0)
        query_segment = jnp.zeros((block, keys), jnp.int32)
        key_segment = jnp.zeros((block, keys), jnp.int32)
        for s in range(slots):
            ends = ends + meta[1 + s]
            query_segment += (query >= ends).astype(jnp.int32)
            key_segment += (key >= ends).astype(jnp.int32)
        known = is_own | (column < second * rows)
        seen = (key < query) & (query_segment == key_segment) & (query_segment < slots) & known
        seen = seen | (is_own & (key == query))
        bias[...] = jnp.where(seen, 0.0, NEG_FILL)

    scaled = q[...] * LOW(SCALE)
    scores = jnp.concatenate(
        [
            contract(scaled, before[:, :HD], ((1,), (1,))),
            contract(scaled, own[:, :HD], ((1,), (1,))),
        ],
        axis=1,
    )
    scores = scores + bias[...]
    exps = jnp.exp(scores - jnp.max(scores, axis=1, keepdims=True))
    probs = (exps * (1.0 / jnp.sum(exps, axis=1, keepdims=True))).astype(LOW)
    p_out[...] = probs
    out = contract(probs[:, :rows], before[:, HD:], ((1,), (0,)))
    out += contract(probs[:, rows:], own[:, HD:], ((1,), (0,)))
    o_out[...] = out.astype(LOW)


def attend(meta, q, before, own):
    rows, width = q.shape
    heads = width // HD
    block = row_tile(rows, 512)
    blocks = rows // block
    slots = meta.shape[0] - 1
    head_block = ((block, HD), lambda i, h, m: (i, h))
    return run(
        lambda *refs: attend_body(slots, *refs),
        "attend",
        (blocks, heads),
        [(q, head_block), (before, None), (own, None)],
        [
            (shape(rows, width), head_block),
            (shape(heads * rows, 2 * rows), ((block, 2 * rows), lambda i, h, m: (h * blocks + i, 0))),
        ],
        scratch=[pltpu.VMEM((block, 2 * rows), F32)],
        scalars=[meta],
        flops=8 * rows * rows * width,
    )


def merge_body(o, own_w, first_w, second_w, x, post_gain, pre_gain, a_out, state_out, first_out, second_out):
    start = 0
    total = None
    for weight in (own_w, first_w, second_w):
        width = weight.shape[1]
        part = contract(o[:, start : start + width], weight[...], ((1,), (1,)))
        total = part if total is None else total + part
        start += width
    a_out[...] = total.astype(a_out.dtype)
    state = x[...].astype(F32) + total * rms_scale(total) * (1.0 + post_gain[...])
    state_out[...] = state.astype(state_out.dtype)
    z = (state * rms_scale(state) * (1.0 + pre_gain[...])).astype(LOW)
    early = pl.program_id(0) < pl.num_programs(0) // 2

    @pl.when(early)
    def _():
        first_out[...] = z

    @pl.when(jnp.logical_not(early))
    def _():
        second_out[...] = z


def merge_heads(o, heads_w, x, post_gain, pre_gain):
    rows, dim = x.shape
    width = o.shape[1]
    tile = row_tile(rows, 256)
    by_row = lambda size: ((tile, size), lambda i: (i, 0))
    half = rows // tile // 2
    return run(
        merge_body,
        "merge_heads",
        (rows // tile,),
        [(o, by_row(width))]
        + [(w, None) for w in heads_w]
        + [(x, by_row(dim)), (post_gain, None), (pre_gain, None)],
        [
            (shape(rows, dim), by_row(dim)),
            (shape(rows, dim), by_row(dim)),
            (shape(rows // 2, dim), ((tile, dim), lambda i: (jnp.minimum(i, half - 1), 0))),
            (shape(rows // 2, dim), ((tile, dim), lambda i: (jnp.maximum(i - half, 0), 0))),
        ],
        flops=2 * rows * dim * width,
    )


def ffn_forward_body(z, gate_w, up_w, down_w, *rest):
    hid_out, act_out, slope_out, f_out, acc = rest[-5:]
    step, last = pl.program_id(0), pl.num_programs(0) - 1
    tile = hid_out.shape[1]
    here = pl.ds(pl.multiple_of(step * tile, 128), tile)
    gate = contract(z[...], gate_w[:, here], ((1,), (0,)))
    up = contract(z[...], up_w[:, here], ((1,), (0,)))
    square = gate * gate
    tanh = jnp.tanh(ROOT * gate * (1.0 + CUBIC * square))
    half = 0.5 * (1.0 + tanh)
    act = gate * half
    slope = half + 0.5 * gate * (1.0 - tanh * tanh) * (ROOT * (1.0 + 3.0 * CUBIC * square))
    hid = (act * up).astype(LOW)
    hid_out[...] = hid
    act_out[...] = act.astype(LOW)
    slope_out[...] = (slope * up).astype(LOW)
    add_to(acc, contract(hid, down_w[:, here], ((1,), (1,))), step == 0)

    @pl.when(step == last)
    def _():
        f_out[...] = acc[...].astype(f_out.dtype)


def ffn_forward(z, z_block, rows, weights, block, total, kept, out_dtype):
    dim, units = weights[0].shape
    tile = column_tile(units)
    inner = ((rows, tile), lambda j: (block, j))
    extra = [] if kept is None else list(kept)
    return run(
        ffn_forward_body,
        "ffn_forward",
        (units // tile,),
        [(z, ((rows, dim), lambda j: (z_block, 0)))]
        + [(w, "vmem") for w in weights]
        + [(k, "any") for k in extra],
        [(shape(total, units), inner)] * 3 + [(shape(rows, dim, dtype=out_dtype), None)],
        scratch=[pltpu.VMEM((rows, dim), F32)],
        aliases={4 + i: i for i in range(len(extra))},
        flops=6 * rows * dim * units,
    )


def ffn_end_body(f_own, f_other, state, cotangent, gain, *rest):
    out, df_out, gain_out = rest[-3:]
    f = f_own[...] + f_other[...].astype(F32)
    out[...] = (state[...].astype(F32) + f * rms_scale(f) * (1.0 + gain[...])).astype(LOW)
    df, gain_grad = rms_back(f, gain[...], cotangent[...].astype(F32))
    df_out[...] = df.astype(LOW)
    add_to(gain_out, gain_grad, pl.program_id(0) == 0)


def ffn_end(f_own, f_other, state, cotangent, gain, chunk, out):
    rows, dim = f_own.shape
    tile = row_tile(rows, 128)
    steps = rows // tile
    here = ((tile, dim), lambda i: (i, 0))
    there = ((tile, dim), lambda i: (chunk * steps + i, 0))
    extra = [] if out is None else [out]
    return run(
        ffn_end_body,
        "ffn_end",
        (steps,),
        [(f_own, here), (f_other, here), (state, there), (cotangent, there), (gain, None)]
        + [(e, "any") for e in extra],
        [(shape(*state.shape), there), (shape(rows, dim), here), (shape(1, dim, dtype=F32), None)],
        aliases={5: 0} if extra else None,
    )


def ffn_backward_body(pieces, splits, *refs):
    dfs = refs[:pieces]
    act, slope, gate_w, up_w, down_w = refs[pieces : pieces + 5]
    *outs, acc, df = refs[pieces + 5 :]
    dgate_out, dup_out, *dz_outs = outs[-2 - splits :]
    step, last = pl.program_id(0), pl.num_programs(0) - 1

    @pl.when(step == 0)
    def _():
        at = 0
        for piece in dfs:
            df[at : at + piece.shape[0]] = piece[...]
            at += piece.shape[0]

    tile = dup_out.shape[1]
    if gate_w.shape[1] == tile:
        here = slice(None)
    else:
        here = pl.ds(pl.multiple_of(step * tile, 128), tile)
    dhid = contract(df[...], down_w[:, here], ((1,), (0,)))
    dup = (dhid * act[...].astype(F32)).astype(LOW)
    dgate = (dhid * slope[...].astype(F32)).astype(LOW)
    dup_out[...] = dup
    dgate_out[...] = dgate
    part = contract(dgate, gate_w[:, here], ((1,), (1,)))
    part += contract(dup, up_w[:, here], ((1,), (1,)))
    add_to(acc, part, step == 0)

    @pl.when(step == last)
    def _():
        at = 0
        for dz_out in dz_outs:
            size = dz_out.shape[0]
            dz_out[...] = acc[at : at + size].astype(dz_out.dtype)
            at += size


def ffn_backward(dfs, act, slope, weights, block, made, out_dtype, splits, resident):
    rows = sum(d.shape[0] for d in dfs)
    total, units = act.shape
    dim = dfs[0].shape[1]
    tile = column_tile(units)
    inner = ((rows, tile), lambda j: (block, j))
    weight = "vmem" if resident else ((dim, tile), lambda j: (0, j))
    extra = [] if made is None else list(made)
    return run(
        lambda *refs: ffn_backward_body(len(dfs), splits, *refs),
        "ffn_backward",
        (units // tile,),
        [(d, None) for d in dfs]
        + [(act, inner), (slope, inner)]
        + [(w, weight) for w in weights]
        + [(e, "any") for e in extra],
        [(shape(total, units), inner)] * 2
        + [(shape(rows // splits, dim, dtype=out_dtype), None)] * splits,
        scratch=[pltpu.VMEM((rows, dim), F32), pltpu.VMEM((rows, dim), LOW)],
        aliases={len(dfs) + 5 + i: i for i in range(len(extra))},
        flops=6 * rows * dim * units,
        vmem=VMEM_BESIDE if resident else VMEM_BYTES,
    )


def weight_grad_body(sides, core, *refs):
    *inputs, send, keep = refs
    groups, rows, _ = keep.shape
    first = core[0] == 0

    def write(lefts, right):
        at = 0
        total = None
        for left in lefts:
            size = left.shape[0]
            part = contract(left[...], right[at : at + size], ((0,), (0,)))
            total = part if total is None else total + part
            at += size
        for i in range(groups):
            even = total[2 * i * rows : (2 * i + 1) * rows].astype(LOW)
            odd = total[(2 * i + 1) * rows : (2 * i + 2) * rows].astype(LOW)
            send[i] = jnp.where(first, odd, even)
            keep[i] = jnp.where(first, even, odd)

    at = 0
    for side, count in enumerate(sides):
        lefts, right = inputs[at : at + count], inputs[at + count]
        at += count + 1
        if len(sides) == 1:
            write(lefts, right)
        else:
            mine = (pl.program_id(0) % len(sides)) == side
            pl.when(mine)(lambda lefts=lefts, right=right: write(lefts, right))


def weight_grad(
    pairs, core, axis_size, start, stop, tile=None, columns_of=None, vmem=VMEM_BYTES
):
    dim = pairs[0][0][0].shape[1]
    columns = stop - start
    rows = dim // axis_size
    groups = axis_size // 2
    tile = column_tile(columns) if tile is None else tile
    blocks = columns // tile
    if columns_of is None:
        columns_of = lambda j, c: j + start // tile
    if rows % 8:
        full = []
        for j in range(blocks):
            lefts, right = pairs[j % len(pairs)]
            left = jnp.concatenate(lefts, axis=0)
            at = columns_of(j, core) * tile
            here = lax.dynamic_slice_in_dim(right, at, tile, axis=1)
            full.append(contract(left, here, ((0,), (0,))).astype(LOW))
        full = jnp.concatenate(full, axis=1).reshape(groups, 2, rows, columns)
        return (
            lax.dynamic_index_in_dim(full, 1 - core, axis=1, keepdims=False),
            lax.dynamic_index_in_dim(full, core, axis=1, keepdims=False),
        )
    inputs = []
    for lefts, right in pairs:
        inputs += [(left, None) for left in lefts]
        inputs.append((right, ((right.shape[0], tile), lambda j, c: (0, columns_of(j, c[0])))))
    out = (shape(groups, rows, columns), ((groups, rows, tile), lambda j, c: (0, 0, j)))
    sides = [len(lefts) for lefts, _ in pairs]
    return run(
        lambda *refs: weight_grad_body(sides, *refs),
        "weight_grad",
        (blocks,),
        inputs,
        [out, out],
        scalars=[core.reshape(1)],
        flops=2 * pairs[0][1].shape[0] * dim * columns,
        vmem=vmem,
    )


def state_back_body(
    dz_own, dz_first, dz_second, state, a, cotangent, pre_gain, post_gain, own_w, first_w, second_w,
    dh_out, da_out, do_out, pre_out, post_out,
):
    first = pl.program_id(0) == 0
    early = pl.program_id(0) < pl.num_programs(0) // 2
    dz = dz_own[...].astype(F32) + jnp.where(early, dz_first[...], dz_second[...]).astype(F32)
    back, pre_grad = rms_back(state[...].astype(F32), pre_gain[...], dz)
    dh = cotangent[...].astype(F32) + back
    dh_out[...] = dh.astype(dh_out.dtype)
    da, post_grad = rms_back(a[...].astype(F32), post_gain[...], dh)
    da = da.astype(LOW)
    da_out[...] = da
    add_to(pre_out, pre_grad, first)
    add_to(post_out, post_grad, first)
    at = 0
    for weight in (own_w, first_w, second_w):
        width = weight.shape[1]
        do_out[:, at : at + width] = contract(da, weight[...], ((1,), (0,))).astype(LOW)
        at += width


def state_back(dz_own, dz_other, state, a, cotangent, pre_gain, post_gain, heads_w):
    rows, dim = state.shape
    width = sum(w.shape[1] for w in heads_w)
    tile = row_tile(rows, 256)
    steps = rows // tile
    by_row = lambda size: ((tile, size), lambda i: (i, 0))
    return run(
        state_back_body,
        "state_back",
        (rows // tile,),
        [
            (dz_own, by_row(dim)),
            (dz_other[0], ((tile, dim), lambda i: (jnp.minimum(i, steps // 2 - 1), 0))),
            (dz_other[1], ((tile, dim), lambda i: (jnp.maximum(i - steps // 2, 0), 0))),
        ]
        + [(v, by_row(dim)) for v in (state, a, cotangent)]
        + [(v, None) for v in (pre_gain, post_gain, *heads_w)],
        [
            (shape(rows, dim), by_row(dim)),
            (shape(rows, dim), by_row(dim)),
            (shape(rows, width), by_row(width)),
            (shape(1, dim, dtype=F32), None),
            (shape(1, dim, dtype=F32), None),
        ],
        vmem=VMEM_BYTES,
        flops=2 * rows * dim * width,
    )


def attend_back_body(
    p, do, q, raw, before, own, gain, cosine, sine, dq_out, before_out, own_out, gain_out, acc
):
    head, part = pl.program_id(0), pl.program_id(1)
    first = (head == 0) & (part == 0)
    last = (head == pl.num_programs(0) - 1) & (part == pl.num_programs(1) - 1)
    rows = before.shape[0]
    dp = jnp.concatenate(
        [
            contract(do[...], before[:, HD:], ((1,), (1,))),
            contract(do[...], own[:, HD:], ((1,), (1,))),
        ],
        axis=1,
    )
    probs = p[...].astype(F32)
    weighted = probs * dp
    ds = (weighted - probs * jnp.sum(weighted, axis=1, keepdims=True)).astype(LOW)
    dq = contract(ds[:, :rows], before[:, :HD], ((1,), (0,)))
    dq += contract(ds[:, rows:], own[:, :HD], ((1,), (0,)))
    dk = contract(ds, q[...], ((0,), (0,))) * SCALE
    dv = contract(p[...], do[...], ((0,), (0,)))
    add_to(acc, jnp.concatenate([dk, dv], axis=1), first)
    back = turn_back(dq * SCALE, cosine[...], sine[...])
    dq_raw, gain_grad = rms_back(raw[...], gain[...], back)
    dq_out[...] = dq_raw.astype(LOW)
    add_to(gain_out, gain_grad, first)

    @pl.when(last)
    def _():
        before_out[...] = acc[:rows].astype(LOW)
        own_out[...] = acc[rows:]


def attend_back(p, do, q, raw, before, own, gain, cosine, sine):
    rows, width = q.shape
    heads = width // HD
    block = row_tile(rows, 512)
    blocks = rows // block
    head_block = ((block, HD), lambda h, i: (i, h))
    table = ((block, HD // 2), lambda h, i: (i, 0))
    return run(
        attend_back_body,
        "attend_back",
        (heads, blocks),
        [
            (p, ((block, 2 * rows), lambda h, i: (h * blocks + i, 0))),
            (do, head_block),
            (q, head_block),
            (raw, head_block),
            (before, None),
            (own, None),
            (gain, None),
            (cosine, table),
            (sine, table),
        ],
        [
            (shape(rows, width), head_block),
            (shape(rows, 2 * HD), None),
            (shape(rows, 2 * HD, dtype=F32), None),
            (shape(1, HD, dtype=F32), None),
        ],
        scratch=[pltpu.VMEM((2 * rows, 2 * HD), F32)],
        vmem=VMEM_BYTES,
        flops=16 * rows * rows * width,
    )


def input_back_body(
    dq, dkv_own, dkv_other, raw, cosine, sine, x, dh, key_gain, in_gain,
    own_w, first_w, second_w, key_w, value_w,
    grad_out, dkv_out, key_gain_out, in_gain_out,
):
    first = pl.program_id(0) == 0
    dkv = dkv_own[...] + dkv_other[...].astype(F32)
    back = turn_back(dkv[:, :HD], cosine[...], sine[...])
    dk, key_grad = rms_back(raw[...], key_gain[...], back)
    dk = dk.astype(LOW)
    dv = dkv[:, HD:].astype(LOW)
    dkv_out[:, :HD] = dk
    dkv_out[:, HD:] = dv
    add_to(key_gain_out, key_grad, first)
    dxn = contract(dk, key_w[...], ((1,), (1,))) + contract(dv, value_w[...], ((1,), (1,)))
    at = 0
    for weight in (own_w, first_w, second_w):
        width = weight.shape[1]
        dxn += contract(dq[:, at : at + width], weight[...], ((1,), (1,)))
        at += width
    dx, in_grad = rms_back(x[...].astype(F32), in_gain[...], dxn)
    grad_out[...] = (dh[...].astype(F32) + dx).astype(LOW)
    add_to(in_gain_out, in_grad, first)


def input_back(dq, dkv_own, dkv_other, raw, cosine, sine, x, dh, key_gain, in_gain, weights):
    rows, dim = x.shape
    width = dq.shape[1]
    tile = row_tile(rows, 256)
    by_row = lambda size: ((tile, size), lambda i: (i, 0))
    return run(
        input_back_body,
        "input_back",
        (rows // tile,),
        [(v, by_row(v.shape[1])) for v in (dq, dkv_own, dkv_other, raw, cosine, sine, x, dh)]
        + [(v, None) for v in (key_gain, in_gain, *weights)],
        [
            (shape(rows, dim), by_row(dim)),
            (shape(rows, 2 * HD), by_row(2 * HD)),
            (shape(1, HD, dtype=F32), None),
            (shape(1, dim, dtype=F32), None),
        ],
        vmem=VMEM_BYTES,
        flops=2 * rows * dim * (width + 2 * HD),
    )


def swap_head(value):
    return lax.ppermute(value, "head", [(0, 1), (1, 0)])


def pair(axis_size, bit):
    return [(i, i ^ (1 << bit)) for i in range(axis_size)]


def tie(*values):
    return lax.optimization_barrier(values)


def sum_parts(parts, choice, columns, dtype):
    total = None
    for array, own, at in parts:
        rows = array.shape[-2]
        value = lax.dynamic_slice(
            array.reshape((2,) * len(own) + array.shape[-2:]),
            [choice.get(b, 0) for b in own] + [0, at],
            [1 if b in choice else 2 for b in own] + [rows, columns],
        )
        value = value.reshape((2,) * sum(b not in choice for b in own) + (rows, columns))
        value = value.astype(F32)
        total = value if total is None else total + value
    return total.astype(dtype)


class Scatter:
    def __init__(self, size, index, order, bits, parts, columns, out=None, low=LOW):
        self.size, self.index, self.order, self.low = size, index, list(order), low
        self.bits, self.parts, self.columns, self.out = list(bits), list(parts), columns, out
        self.gone, self.loaded, self.flying, self.cuts = [], out is not None, False, None
        if out is None:
            self.load()
        else:
            self.drop()

    def value(self, bit):
        return (self.index >> bit) & 1

    def drop(self):
        bit = self.order[0]
        if bit == "head":
            self.columns //= 2
        else:
            self.bits.remove(bit)
            self.gone.append(bit)

    def load(self):
        if not self.order:
            return
        bit = self.order[0]
        choice = {b: self.value(b) for b in self.gone}
        parts, columns = self.parts, self.columns
        if bit == "head":
            columns //= 2
            parts = [(p, own, at + columns) for p, own, at in parts]
        else:
            choice[bit] = 1 - self.value(bit)
        self.out = sum_parts(parts, choice, columns, self.low)
        self.loaded = True
        self.drop()

    def go(self):
        bit = self.order.pop(0)
        if bit == "head":
            self.got = swap_head(self.out)
        else:
            self.got = lax.ppermute(self.out, "dp", pair(self.size, bit))
        self.loaded, self.flying = False, True
        return self

    def take(self):
        self.parts = self.parts + [(self.got, list(self.bits), 0)]
        self.flying = False
        return self

    def land(self):
        self.take().load()
        return self

    def finish(self):
        if self.flying:
            self.take()
        while self.order:
            if not self.loaded:
                self.load()
            self.go().take()
        choice = {b: self.value(b) for b in self.gone}
        return sum_parts(self.parts, choice, self.columns, F32)


class Joint:
    def __init__(self, items):
        self.items, self.cuts = items, None
        self.join()

    def join(self):
        self.order = self.items[0].order
        if self.order:
            self.out = jnp.concatenate([s.out for s in self.items], axis=-1)

    def load(self):
        for s in self.items:
            if not s.loaded:
                s.load()
        self.join()

    def go(self):
        bit = self.order[0]
        self.got = lax.ppermute(self.out, "dp", pair(self.items[0].size, bit))
        for s in self.items:
            s.order.pop(0)
            s.loaded = False
        return self

    def take(self):
        at = 0
        for s in self.items:
            s.parts = s.parts + [(self.got, list(s.bits), at)]
            at += s.columns
        return self


def load_body(*refs):
    count = (len(refs) - 1) // 2
    sems = refs[-1]
    copies = [
        pltpu.make_async_copy(source, target, sems.at[i])
        for i, (source, target) in enumerate(zip(refs[:count], refs[count : 2 * count]))
    ]
    for copy in copies:
        copy.start()
    for copy in copies:
        copy.wait()


def load_weights(weights):
    return pl.pallas_call(
        load_body,
        in_specs=[pl.BlockSpec(memory_space=pl.ANY)] * len(weights),
        out_specs=[pl.BlockSpec(memory_space=pltpu.VMEM)] * len(weights),
        out_shape=[pltpu.VMEM(w.shape, w.dtype) for w in weights],
        scratch_shapes=[pltpu.SemaphoreType.DMA((len(weights),))],
        compiler_params=pltpu.CompilerParams(vmem_limit_bytes=VMEM_BESIDE),
        name="load_weights",
    )(*weights)


def angle_tables(lengths, head_index, rows):
    ids = head_index * rows + jnp.arange(rows, dtype=jnp.int32)
    begin = jnp.zeros_like(ids)
    end = jnp.int32(0)
    for s in range(lengths.shape[0]):
        end = end + lengths[s]
        begin = jnp.where(ids >= end, end, begin)
    frequency = np.power(ROPE_BASE, -2.0 * np.arange(HD // 2) / HD).astype(np.float32)
    grid = (ids - begin).astype(F32)[:, None] * frequency[None, :]
    return jnp.cos(grid), jnp.sin(grid)


def on_device(
    layer_input,
    seq_lengths,
    input_gain,
    query_weight,
    key_weight,
    value_weight,
    query_gain,
    key_gain,
    output_weight,
    post_attn_gain,
    pre_ffn_gain,
    gate_weight,
    up_weight,
    down_weight,
    post_ffn_gain,
    out_cotangent,
):
    rows = layer_input.shape[0]
    dp_size = lax.axis_size("dp")
    bit_count = dp_size.bit_length() - 1
    dp_index = lax.axis_index("dp")
    head_index = lax.axis_index("head")
    core = dp_index & 1
    core_pairs = pair(dp_size, 0)
    width = query_weight.shape[1]
    in_gain, q_gain, k_gain, post_gain, pre_gain, end_gain = (
        g.reshape(1, -1)
        for g in (input_gain, query_gain, key_gain, post_attn_gain, pre_ffn_gain, post_ffn_gain)
    )

    query_mine = lax.dynamic_slice_in_dim(query_weight, core * HD, HD, axis=1)
    output_mine = lax.dynamic_slice_in_dim(output_weight, core * HD, HD, axis=1)
    query_mine, output_mine, layer_input, seq_lengths = tie(
        query_mine, output_mine, layer_input, seq_lengths
    )
    query_first = swap_head(query_mine)

    cosine, sine = angle_tables(seq_lengths[0], head_index, rows)
    meta = jnp.concatenate([head_index.reshape(1).astype(jnp.int32), seq_lengths[0]])
    xn, kv_own, k_raw = project_keys(
        layer_input, in_gain, key_weight, value_weight, k_gain, cosine, sine
    )
    kv_before = lax.ppermute(kv_own, "head", [(0, 1)])
    query_first, kv_own, *weights = tie(
        query_first, kv_own, gate_weight, up_weight, down_weight
    )
    query_second = lax.ppermute(query_first, "dp", core_pairs)
    weights = load_weights(weights)
    xn_in, kv_before, output_mine, *weights = tie(xn, kv_before, output_mine, *weights)
    output_first = swap_head(output_mine)
    weights = [pltpu.with_memory_space_constraint(w, pltpu.VMEM) for w in weights]
    query_w = (query_weight, query_first, query_second)

    q_low, q_raw = project_queries(xn_in, query_w, q_gain, cosine, sine)
    attn_out, probs = attend(meta, q_low, kv_before, kv_own)
    attn_out, output_first = tie(attn_out, output_first)
    output_second = lax.ppermute(output_first, "dp", core_pairs)
    output_w = (output_weight, output_first, output_second)
    attn_proj, state, *z_own = merge_heads(attn_out, output_w, layer_input, post_gain, pre_gain)

    half = rows // 2
    total = 2 * rows
    z_other = [swap_head(z) for z in z_own]
    *kept, f_own0 = ffn_forward(z_own[0], 0, half, weights, 0, total, None, F32)
    z_in, f_own0 = tie(z_other[0], f_own0)
    *kept, f_send0 = ffn_forward(z_in, 0, half, weights, 2, total, kept, LOW)
    z_in, f_send0 = tie(z_other[1], f_send0)
    *kept, f_send1 = ffn_forward(z_in, 0, half, weights, 3, total, kept, LOW)
    f_got0 = swap_head(f_send0)
    z_in, f_send1 = tie(z_own[1], f_send1)
    f_got1 = swap_head(f_send1)
    *kept, f_own1 = ffn_forward(z_in, 0, half, weights, 1, total, kept, F32)
    hid, act, slope = kept
    f_got0, f_own0, f_own1 = tie(f_got0, f_own0, f_own1)
    layer_output, df_own0, end_grad0 = ffn_end(
        f_own0, f_got0, state, out_cotangent, end_gain, 0, None
    )
    df_other0 = swap_head(df_own0)
    layer_output, df_own1, end_grad1 = ffn_end(
        f_own1, f_got1, state, out_cotangent, end_gain, 1, layer_output
    )
    df_other1 = swap_head(df_own1)
    df_own = [df_own0, df_own1]
    *made, own_zgrad = ffn_backward(df_own, act, slope, weights, 0, None, LOW, 1, True)
    df_other0, df_other1, own_zgrad = tie(df_other0, df_other1, own_zgrad)
    df_other = [df_other0, df_other1]
    units = hid.shape[1]
    order = list(range(bit_count))
    rest = order[1:]
    leading = rest[::-1]
    third = units // 3

    def start(pairs, first, last, route=order, **options):
        send, keep = weight_grad(pairs, core, dp_size, first, last, **options)
        columns = last - first
        return Scatter(
            dp_size, dp_index, route, order[::-1], [(keep, leading, 0)], columns, send
        )

    def cut(whole, at, columns, route=rest):
        parts = [(p, own, at) for p, own, _ in whole.parts]
        return Scatter(dp_size, dp_index, route, leading, parts, columns)

    def later(value, scatter):
        tied = tie(*[p for p, _, _ in scatter.parts], value)
        scatter.parts = [(p, own, at) for p, (_, own, at) in zip(tied, scatter.parts)]

    def phase(values, end=(), go=(), now=(), hold=()):
        count = len(values)
        done = list(end) + list(now) + list(hold)
        tied = list(tie(*values, *[s.got for s in done], *[s.out for s in go]))
        for s in go[::-1]:
            s.out = tied.pop()
        for s in done[::-1]:
            s.got = tied.pop()
            s.take()
        for s in go:
            s.go()
        for s in list(now) + [s for s in end if s.cuts is None]:
            s.load()
        if now:
            tied = list(tie(*tied, *[s.out for s in now]))
            for s in now[::-1]:
                s.out = tied.pop()
                s.go()
        return tied

    df_all = df_own + df_other
    down_a = start([(df_all, hid)], 0, 2 * third, vmem=VMEM_BESIDE)
    (hid,) = phase([hid], go=[down_a])
    down_b = start([(df_all, hid)], 2 * third, units, vmem=VMEM_BESIDE)
    down_a.cuts = down_b.cuts = 1
    (df_other0,) = phase([df_other0], end=[down_a], go=[down_b])
    d1 = cut(down_a, 0, 2 * third)
    (df_other0,) = phase([df_other0], go=[d1])
    *made, dz0, dz1 = ffn_backward(
        [df_other0, df_other1],
        act,
        slope,
        (gate_weight, up_weight, down_weight),
        1,
        made,
        LOW,
        2,
        False,
    )
    dgate, dup = made
    dz0, dz1, dgate = phase([dz0, dz1, dgate], end=[down_b, d1])
    d2 = cut(down_b, 0, third)
    dz0, dz1, dgate = phase([dz0, dz1, dgate], go=[d2])
    other0 = swap_head(dz0)
    z_both = z_own + z_other
    gate_s = start([(z_both, dgate)], 0, units)
    other0, dz1, dup = phase([other0, dz1, dup], end=[d2], go=[gate_s, d1])
    other1 = swap_head(dz1)
    up_s = start([(z_both, dup)], 0, units)
    gate_s.cuts = up_s.cuts = 1
    own_zgrad, other0, other1 = phase(
        [own_zgrad, other0, other1], end=[gate_s], go=[up_s, d2], hold=[d1]
    )
    g1 = cut(gate_s, 0, 2 * third)
    (own_zgrad,) = phase([own_zgrad], go=[g1])
    other_zgrad = [other0, other1]

    state_grad, attn_grad, heads_grad, pre_grad, post_grad = state_back(
        own_zgrad, other_zgrad, state, attn_proj, out_cotangent, pre_gain, post_gain, output_w
    )

    own_heads = width // HD

    def head_block(j, c):
        return jnp.where(j < own_heads, j, own_heads + ((j - own_heads) ^ c))

    def start_heads(left, right):
        route = [order[0], "head"] + rest
        return start([([left], right)], 0, 2 * width, route, tile=HD, columns_of=head_block)

    dq, kv_back_send, kv_grad, q_gain_grad = attend_back(
        probs, heads_grad, q_low, q_raw, kv_before, kv_own, q_gain, cosine, sine
    )
    attn_grad, dq = tie(attn_grad, dq)
    output_s = start_heads(attn_grad, attn_out)
    later(output_s.out, gate_s)
    later(output_s.out, d1)
    d1.load()
    g2 = cut(gate_s, 2 * third, third)
    dq, kv_back_send = phase(
        [dq, kv_back_send], end=[up_s, g1, d2], go=[g2, output_s, d1]
    )
    kv_back = lax.ppermute(kv_back_send, "head", [(1, 0)])
    query_s = start_heads(xn, dq)
    later(query_s.out, up_s)
    u1 = cut(up_s, 0, 2 * third)
    dq, kv_grad, kv_back = phase(
        [dq, kv_grad, kv_back], end=[g2, d1], go=[query_s, u1, g1, d2], now=[output_s]
    )
    input_grad, dkv, k_gain_grad, in_gain_grad = input_back(
        dq, kv_grad, kv_back, k_raw, cosine, sine, layer_input, state_grad, k_gain, in_gain,
        query_w + (key_weight, value_weight),
    )
    kv_s = start([([xn], dkv)], 0, 2 * HD)
    later(kv_s.out, up_s)
    u2 = cut(up_s, 2 * third, third)
    (wait,) = phase(
        [in_gain_grad], end=[u1, d2, output_s], go=[u2, kv_s, g2], now=[query_s, g1]
    )
    gains = [wait, post_grad, pre_grad, end_grad0 + end_grad1, q_gain_grad, k_gain_grad]
    gains = [g.reshape(dp_size, -1) for g in gains]
    widths = [g.shape[1] for g in gains]
    block = layer_input.shape[1] // dp_size
    packed = jnp.concatenate(gains, axis=1)
    packed = jnp.pad(packed, ((0, 0), (0, block * 128 - packed.shape[1])))
    packed = packed.reshape(dp_size // 2, 2, block, 128).astype(LOW)
    packed = jnp.concatenate([packed[:, 0], packed[:, 1]], axis=2)
    gains_s = Scatter(dp_size, dp_index, rest, leading, [(packed, leading, 0)], 256)
    wait, query_s.got, kv_s.got, u2.got, gains_s.out = tie(
        wait, query_s.got, kv_s.got, u2.got, gains_s.out
    )
    for s in (query_s, kv_s, u2):
        s.take().load()
    tail = Joint([output_s, query_s, kv_s, gains_s])
    up_both = Joint([u1, u2])
    (wait,) = phase([wait], end=[g1], go=[tail, up_both], now=[g2])
    (wait,) = phase([wait], end=[g2], now=[tail, up_both])
    (wait,) = phase([wait], end=[up_both], now=[tail])
    (wait,) = phase([wait], end=[tail])
    down_part = jnp.concatenate([d1.finish(), d2.finish()], axis=1)
    gate_part = jnp.concatenate([g1.finish(), g2.finish()], axis=1)
    up_part = jnp.concatenate([u1.finish(), u2.finish()], axis=1)
    output_part = output_s.finish()
    query_part = query_s.finish()
    packed = gains_s.finish()
    pick = lambda which: lax.dynamic_slice_in_dim(packed, which * 128, 128, axis=1)
    packed = pick(core) + lax.ppermute(pick(1 - core), "dp", core_pairs)
    kv_sum = jnp.concatenate([kv_s.finish(), packed], axis=1)
    kv_sum = kv_sum + swap_head(kv_sum.astype(LOW)).astype(F32)
    packed = kv_sum[:, 2 * HD :].reshape(-1)
    pieces = []
    at = 0
    for size in widths:
        pieces.append(packed[at : at + size])
        at += size
    return (
        layer_output,
        input_grad,
        pieces[0],
        query_part,
        kv_sum[:, :HD],
        kv_sum[:, HD : 2 * HD],
        pieces[4],
        pieces[5],
        output_part,
        pieces[1],
        pieces[2],
        gate_part,
        up_part,
        down_part,
        pieces[3],
    )


def solution(mesh):
    placed = (
        P(("dp", "head"), None),
        P("dp", None),
        P(),
        P(None, "head"),
        P(),
        P(),
        P(),
        P(),
        P(None, "head"),
        P(),
        P(),
        P(None, "head"),
        P(None, "head"),
        P(None, "head"),
        P(),
        P(("dp", "head"), None),
    )
    return jax.shard_map(
        on_device,
        mesh=mesh,
        in_specs=placed,
        out_specs=(
            P(("dp", "head"), None),
            P(("dp", "head"), None),
            P("dp"),
            P("dp", "head"),
            P("dp", None),
            P("dp", None),
            P("dp"),
            P("dp"),
            P("dp", "head"),
            P("dp"),
            P("dp"),
            P("dp", "head"),
            P("dp", "head"),
            P("dp", "head"),
            P("dp"),
        ),
        check_vma=False,
    )
```

```python
import jax
import jax.numpy as jnp
import numpy as np
from jax import lax
from jax.experimental import pallas as pl
from jax.experimental.pallas import tpu as pltpu
from jax.sharding import PartitionSpec as P

HD = 256
EPSILON = 1e-06
ROPE_BASE = 1000000.0
NEG_FILL = -1e30
LOW = jnp.bfloat16
F32 = jnp.float32
ROOT = 0.7978845608028654
CUBIC = 0.044715
SCALE = HD ** (-0.5)
VMEM_BESIDE = 30 << 20
VMEM_BYTES = 60 << 20


def shape(*dims, dtype=LOW):
    return jax.ShapeDtypeStruct(dims, dtype)


def contract(left, right, dims):
    return lax.dot_general(left, right, (dims, ((), ())), preferred_element_type=F32)


def rms_scale(values):
    return lax.rsqrt(jnp.mean(values * values, axis=-1, keepdims=True) + EPSILON)


def rms_back(values, gain, cotangent):
    scale = rms_scale(values)
    unit = values * scale
    scaled = cotangent * (1.0 + gain)
    back = scale * (scaled - unit * jnp.mean(scaled * unit, axis=-1, keepdims=True))
    return back, jnp.sum(cotangent * unit, axis=0, keepdims=True)


def turn(values, cosine, sine):
    half = HD // 2
    first, second = values[:, :half], values[:, half:]
    return jnp.concatenate([first * cosine - second * sine, second * cosine + first * sine], axis=1)


def turn_back(values, cosine, sine):
    return turn(values, cosine, -sine)


def add_to(ref, value, first):
    @pl.when(first)
    def _():
        ref[...] = value

    @pl.when(jnp.logical_not(first))
    def _():
        ref[...] += value


def run(body, name, grid, inputs, outputs, scratch=(), scalars=(), aliases=None, flops=0, vmem=VMEM_BESIDE, hbm=True):
    def spec(array, block):
        if block is None:
            dims = tuple(array.shape)
            return pl.BlockSpec(dims, lambda *_: (0,) * len(dims))
        if block == "any":
            return pl.BlockSpec(memory_space=pl.ANY)
        if block == "vmem":
            return pl.BlockSpec(memory_space=pltpu.VMEM)
        return pl.BlockSpec(*block)

    arrays = [a for a, _ in inputs]
    out_shape = [o for o, _ in outputs]
    if hbm:
        arrays = [
            a if b == "vmem" else pltpu.with_memory_space_constraint(a, pltpu.HBM)
            for a, b in inputs
        ]
    moved = sum(a.size * a.dtype.itemsize for a, _ in inputs)
    moved += sum(int(np.prod(o.shape)) * o.dtype.itemsize for o in out_shape)
    return pl.pallas_call(
        body,
        grid_spec=pltpu.PrefetchScalarGridSpec(
            num_scalar_prefetch=len(scalars),
            grid=grid,
            in_specs=[spec(a, b) for a, b in inputs],
            out_specs=[spec(o, b) for o, b in outputs],
            scratch_shapes=list(scratch),
        ),
        out_shape=[pltpu.HBM(o.shape, o.dtype) for o in out_shape] if hbm else out_shape,
        input_output_aliases={} if aliases is None else aliases,
        compiler_params=pltpu.CompilerParams(vmem_limit_bytes=vmem),
        cost_estimate=pl.CostEstimate(flops=flops, transcendentals=0, bytes_accessed=moved),
        name=name,
    )(*scalars, *arrays)


def column_tile(units):
    for tile in (1152, 1024, 768, 512, 384, 256, 128):
        if units % tile == 0:
            return tile
    return units


def row_tile(rows, most):
    tile = most
    while rows % tile:
        tile //= 2
    return tile


def keys_body(x, gain, key_w, value_w, key_gain, cosine, sine, xn_out, kv_out, raw_out):
    values = x[...].astype(F32)
    xn = (values * rms_scale(values) * (1.0 + gain[...])).astype(LOW)
    xn_out[...] = xn
    raw = contract(xn, key_w[...], ((1,), (0,)))
    raw_out[...] = raw
    unit = raw * rms_scale(raw) * (1.0 + key_gain[...])
    kv_out[:, :HD] = turn(unit, cosine[...], sine[...]).astype(LOW)
    kv_out[:, HD:] = contract(xn, value_w[...], ((1,), (0,))).astype(LOW)


def project_keys(x, gain, key_w, value_w, key_gain, cosine, sine):
    rows, dim = x.shape
    tile = row_tile(rows, 512)
    by_row = lambda width: ((tile, width), lambda i: (i, 0))
    return run(
        keys_body,
        "project_keys",
        (rows // tile,),
        [
            (x, by_row(dim)),
            (gain, None),
            (key_w, None),
            (value_w, None),
            (key_gain, None),
            (cosine, by_row(HD // 2)),
            (sine, by_row(HD // 2)),
        ],
        [
            (shape(rows, dim), by_row(dim)),
            (shape(rows, 2 * HD), by_row(2 * HD)),
            (shape(rows, HD, dtype=F32), by_row(HD)),
        ],
        flops=4 * rows * dim * HD,
    )


def queries_body(xn, own_w, first_w, second_w, gain, cosine, sine, q_out, raw_out):
    values = xn[...]
    start = 0
    for weight in (own_w, first_w, second_w):
        raw_all = contract(values, weight[...], ((1,), (0,)))
        for at in range(0, weight.shape[1], HD):
            raw = raw_all[:, at : at + HD]
            unit = raw * rms_scale(raw) * (1.0 + gain[...])
            raw_out[:, start : start + HD] = raw
            q_out[:, start : start + HD] = turn(unit, cosine[...], sine[...]).astype(LOW)
            start += HD


def project_queries(xn, heads_w, gain, cosine, sine):
    rows, dim = xn.shape
    width = sum(w.shape[1] for w in heads_w)
    tile = row_tile(rows, 512)
    by_row = lambda size: ((tile, size), lambda i: (i, 0))
    return run(
        queries_body,
        "project_queries",
        (rows // tile,),
        [(xn, by_row(dim))]
        + [(w, None) for w in heads_w]
        + [(gain, None), (cosine, by_row(HD // 2)), (sine, by_row(HD // 2))],
        [(shape(rows, width), by_row(width)), (shape(rows, width, dtype=F32), by_row(width))],
        flops=2 * rows * dim * width,
    )


def attend_body(slots, meta, q, before, own, o_out, p_out, bias):
    block, keys = bias.shape
    rows = keys // 2

    @pl.when(pl.program_id(1) == 0)
    def _():
        second = meta[0]
        first_row = second * rows + pl.program_id(0) * block
        query = first_row + lax.broadcasted_iota(jnp.int32, (block, keys), 0)
        column = lax.broadcasted_iota(jnp.int32, (block, keys), 1)
        is_own = column >= rows
        key = jnp.where(is_own, column + (second - 1) * rows, column)
        ends = jnp.int32(0)
        query_segment = jnp.zeros((block, keys), jnp.int32)
        key_segment = jnp.zeros((block, keys), jnp.int32)
        for s in range(slots):
            ends = ends + meta[1 + s]
            query_segment += (query >= ends).astype(jnp.int32)
            key_segment += (key >= ends).astype(jnp.int32)
        known = is_own | (column < second * rows)
        seen = (key < query) & (query_segment == key_segment) & (query_segment < slots) & known
        seen = seen | (is_own & (key == query))
        bias[...] = jnp.where(seen, 0.0, NEG_FILL)

    scaled = q[...] * LOW(SCALE)
    scores = jnp.concatenate(
        [
            contract(scaled, before[:, :HD], ((1,), (1,))),
            contract(scaled, own[:, :HD], ((1,), (1,))),
        ],
        axis=1,
    )
    scores = scores + bias[...]
    exps = jnp.exp(scores - jnp.max(scores, axis=1, keepdims=True))
    probs = (exps * (1.0 / jnp.sum(exps, axis=1, keepdims=True))).astype(LOW)
    p_out[...] = probs
    out = contract(probs[:, :rows], before[:, HD:], ((1,), (0,)))
    out += contract(probs[:, rows:], own[:, HD:], ((1,), (0,)))
    o_out[...] = out.astype(LOW)


def attend(meta, q, before, own):
    rows, width = q.shape
    heads = width // HD
    block = row_tile(rows, 512)
    blocks = rows // block
    slots = meta.shape[0] - 1
    head_block = ((block, HD), lambda i, h, m: (i, h))
    return run(
        lambda *refs: attend_body(slots, *refs),
        "attend",
        (blocks, heads),
        [(q, head_block), (before, None), (own, None)],
        [
            (shape(rows, width), head_block),
            (shape(heads * rows, 2 * rows), ((block, 2 * rows), lambda i, h, m: (h * blocks + i, 0))),
        ],
        scratch=[pltpu.VMEM((block, 2 * rows), F32)],
        scalars=[meta],
        flops=8 * rows * rows * width,
    )


def merge_body(o, own_w, first_w, second_w, x, post_gain, pre_gain, a_out, state_out, first_out, second_out):
    start = 0
    total = None
    for weight in (own_w, first_w, second_w):
        width = weight.shape[1]
        part = contract(o[:, start : start + width], weight[...], ((1,), (1,)))
        total = part if total is None else total + part
        start += width
    a_out[...] = total.astype(a_out.dtype)
    state = x[...].astype(F32) + total * rms_scale(total) * (1.0 + post_gain[...])
    state_out[...] = state.astype(state_out.dtype)
    z = (state * rms_scale(state) * (1.0 + pre_gain[...])).astype(LOW)
    early = pl.program_id(0) < pl.num_programs(0) // 2

    @pl.when(early)
    def _():
        first_out[...] = z

    @pl.when(jnp.logical_not(early))
    def _():
        second_out[...] = z


def merge_heads(o, heads_w, x, post_gain, pre_gain):
    rows, dim = x.shape
    width = o.shape[1]
    tile = row_tile(rows, 256)
    by_row = lambda size: ((tile, size), lambda i: (i, 0))
    half = rows // tile // 2
    return run(
        merge_body,
        "merge_heads",
        (rows // tile,),
        [(o, by_row(width))]
        + [(w, None) for w in heads_w]
        + [(x, by_row(dim)), (post_gain, None), (pre_gain, None)],
        [
            (shape(rows, dim), by_row(dim)),
            (shape(rows, dim), by_row(dim)),
            (shape(rows // 2, dim), ((tile, dim), lambda i: (jnp.minimum(i, half - 1), 0))),
            (shape(rows // 2, dim), ((tile, dim), lambda i: (jnp.maximum(i - half, 0), 0))),
        ],
        flops=2 * rows * dim * width,
    )


def ffn_forward_body(z, gate_w, up_w, down_w, *rest):
    hid_out, act_out, slope_out, f_out, acc = rest[-5:]
    step, last = pl.program_id(0), pl.num_programs(0) - 1
    tile = hid_out.shape[1]
    here = pl.ds(pl.multiple_of(step * tile, 128), tile)
    gate = contract(z[...], gate_w[:, here], ((1,), (0,)))
    up = contract(z[...], up_w[:, here], ((1,), (0,)))
    square = gate * gate
    tanh = jnp.tanh(ROOT * gate * (1.0 + CUBIC * square))
    half = 0.5 * (1.0 + tanh)
    act = gate * half
    slope = half + 0.5 * gate * (1.0 - tanh * tanh) * (ROOT * (1.0 + 3.0 * CUBIC * square))
    hid = (act * up).astype(LOW)
    hid_out[...] = hid
    act_out[...] = act.astype(LOW)
    slope_out[...] = (slope * up).astype(LOW)
    add_to(acc, contract(hid, down_w[:, here], ((1,), (1,))), step == 0)

    @pl.when(step == last)
    def _():
        f_out[...] = acc[...].astype(f_out.dtype)


def ffn_forward(z, z_block, rows, weights, block, total, kept, out_dtype):
    dim, units = weights[0].shape
    tile = column_tile(units)
    inner = ((rows, tile), lambda j: (block, j))
    extra = [] if kept is None else list(kept)
    return run(
        ffn_forward_body,
        "ffn_forward",
        (units // tile,),
        [(z, ((rows, dim), lambda j: (z_block, 0)))]
        + [(w, "vmem") for w in weights]
        + [(k, "any") for k in extra],
        [(shape(total, units), inner)] * 3 + [(shape(rows, dim, dtype=out_dtype), None)],
        scratch=[pltpu.VMEM((rows, dim), F32)],
        aliases={4 + i: i for i in range(len(extra))},
        flops=6 * rows * dim * units,
    )


def ffn_end_body(f_own, f_other, state, cotangent, gain, *rest):
    out, df_out, gain_out = rest[-3:]
    f = f_own[...] + f_other[...].astype(F32)
    out[...] = (state[...].astype(F32) + f * rms_scale(f) * (1.0 + gain[...])).astype(LOW)
    df, gain_grad = rms_back(f, gain[...], cotangent[...].astype(F32))
    df_out[...] = df.astype(LOW)
    add_to(gain_out, gain_grad, pl.program_id(0) == 0)


def ffn_end(f_own, f_other, state, cotangent, gain, chunk, out):
    rows, dim = f_own.shape
    tile = row_tile(rows, 128)
    steps = rows // tile
    here = ((tile, dim), lambda i: (i, 0))
    there = ((tile, dim), lambda i: (chunk * steps + i, 0))
    extra = [] if out is None else [out]
    return run(
        ffn_end_body,
        "ffn_end",
        (steps,),
        [(f_own, here), (f_other, here), (state, there), (cotangent, there), (gain, None)]
        + [(e, "any") for e in extra],
        [(shape(*state.shape), there), (shape(rows, dim), here), (shape(1, dim, dtype=F32), None)],
        aliases={5: 0} if extra else None,
    )


def ffn_backward_body(pieces, splits, *refs):
    dfs = refs[:pieces]
    act, slope, gate_w, up_w, down_w = refs[pieces : pieces + 5]
    *outs, acc, df = refs[pieces + 5 :]
    dgate_out, dup_out, *dz_outs = outs[-2 - splits :]
    step, last = pl.program_id(0), pl.num_programs(0) - 1

    @pl.when(step == 0)
    def _():
        at = 0
        for piece in dfs:
            df[at : at + piece.shape[0]] = piece[...]
            at += piece.shape[0]

    tile = dup_out.shape[1]
    if gate_w.shape[1] == tile:
        here = slice(None)
    else:
        here = pl.ds(pl.multiple_of(step * tile, 128), tile)
    dhid = contract(df[...], down_w[:, here], ((1,), (0,)))
    dup = (dhid * act[...].astype(F32)).astype(LOW)
    dgate = (dhid * slope[...].astype(F32)).astype(LOW)
    dup_out[...] = dup
    dgate_out[...] = dgate
    part = contract(dgate, gate_w[:, here], ((1,), (1,)))
    part += contract(dup, up_w[:, here], ((1,), (1,)))
    add_to(acc, part, step == 0)

    @pl.when(step == last)
    def _():
        at = 0
        for dz_out in dz_outs:
            size = dz_out.shape[0]
            dz_out[...] = acc[at : at + size].astype(dz_out.dtype)
            at += size


def ffn_backward(dfs, act, slope, weights, block, made, out_dtype, splits, resident):
    rows = sum(d.shape[0] for d in dfs)
    total, units = act.shape
    dim = dfs[0].shape[1]
    tile = column_tile(units)
    inner = ((rows, tile), lambda j: (block, j))
    weight = "vmem" if resident else ((dim, tile), lambda j: (0, j))
    extra = [] if made is None else list(made)
    return run(
        lambda *refs: ffn_backward_body(len(dfs), splits, *refs),
        "ffn_backward",
        (units // tile,),
        [(d, None) for d in dfs]
        + [(act, inner), (slope, inner)]
        + [(w, weight) for w in weights]
        + [(e, "any") for e in extra],
        [(shape(total, units), inner)] * 2
        + [(shape(rows // splits, dim, dtype=out_dtype), None)] * splits,
        scratch=[pltpu.VMEM((rows, dim), F32), pltpu.VMEM((rows, dim), LOW)],
        aliases={len(dfs) + 5 + i: i for i in range(len(extra))},
        flops=6 * rows * dim * units,
        vmem=VMEM_BESIDE if resident else VMEM_BYTES,
    )


def weight_grad_body(sides, core, *refs):
    *inputs, send, keep = refs
    groups, rows, _ = keep.shape
    first = core[0] == 0

    def write(lefts, right):
        at = 0
        total = None
        for left in lefts:
            size = left.shape[0]
            part = contract(left[...], right[at : at + size], ((0,), (0,)))
            total = part if total is None else total + part
            at += size
        for i in range(groups):
            even = total[2 * i * rows : (2 * i + 1) * rows].astype(LOW)
            odd = total[(2 * i + 1) * rows : (2 * i + 2) * rows].astype(LOW)
            send[i] = jnp.where(first, odd, even)
            keep[i] = jnp.where(first, even, odd)

    at = 0
    for side, count in enumerate(sides):
        lefts, right = inputs[at : at + count], inputs[at + count]
        at += count + 1
        if len(sides) == 1:
            write(lefts, right)
        else:
            mine = (pl.program_id(0) % len(sides)) == side
            pl.when(mine)(lambda lefts=lefts, right=right: write(lefts, right))


def weight_grad(
    pairs, core, axis_size, start, stop, tile=None, columns_of=None, vmem=VMEM_BYTES
):
    dim = pairs[0][0][0].shape[1]
    columns = stop - start
    rows = dim // axis_size
    groups = axis_size // 2
    tile = column_tile(columns) if tile is None else tile
    blocks = columns // tile
    if columns_of is None:
        columns_of = lambda j, c: j + start // tile
    if rows % 8:
        full = []
        for j in range(blocks):
            lefts, right = pairs[j % len(pairs)]
            left = jnp.concatenate(lefts, axis=0)
            at = columns_of(j, core) * tile
            here = lax.dynamic_slice_in_dim(right, at, tile, axis=1)
            full.append(contract(left, here, ((0,), (0,))).astype(LOW))
        full = jnp.concatenate(full, axis=1).reshape(groups, 2, rows, columns)
        return (
            lax.dynamic_index_in_dim(full, 1 - core, axis=1, keepdims=False),
            lax.dynamic_index_in_dim(full, core, axis=1, keepdims=False),
        )
    inputs = []
    for lefts, right in pairs:
        inputs += [(left, None) for left in lefts]
        inputs.append((right, ((right.shape[0], tile), lambda j, c: (0, columns_of(j, c[0])))))
    out = (shape(groups, rows, columns), ((groups, rows, tile), lambda j, c: (0, 0, j)))
    sides = [len(lefts) for lefts, _ in pairs]
    return run(
        lambda *refs: weight_grad_body(sides, *refs),
        "weight_grad",
        (blocks,),
        inputs,
        [out, out],
        scalars=[core.reshape(1)],
        flops=2 * pairs[0][1].shape[0] * dim * columns,
        vmem=vmem,
    )


def state_back_body(
    dz_own, dz_first, dz_second, state, a, cotangent, pre_gain, post_gain, own_w, first_w, second_w,
    dh_out, da_out, do_out, pre_out, post_out,
):
    first = pl.program_id(0) == 0
    early = pl.program_id(0) < pl.num_programs(0) // 2
    dz = dz_own[...].astype(F32) + jnp.where(early, dz_first[...], dz_second[...]).astype(F32)
    back, pre_grad = rms_back(state[...].astype(F32), pre_gain[...], dz)
    dh = cotangent[...].astype(F32) + back
    dh_out[...] = dh.astype(dh_out.dtype)
    da, post_grad = rms_back(a[...].astype(F32), post_gain[...], dh)
    da = da.astype(LOW)
    da_out[...] = da
    add_to(pre_out, pre_grad, first)
    add_to(post_out, post_grad, first)
    at = 0
    for weight in (own_w, first_w, second_w):
        width = weight.shape[1]
        do_out[:, at : at + width] = contract(da, weight[...], ((1,), (0,))).astype(LOW)
        at += width


def state_back(dz_own, dz_other, state, a, cotangent, pre_gain, post_gain, heads_w):
    rows, dim = state.shape
    width = sum(w.shape[1] for w in heads_w)
    tile = row_tile(rows, 256)
    steps = rows // tile
    by_row = lambda size: ((tile, size), lambda i: (i, 0))
    return run(
        state_back_body,
        "state_back",
        (rows // tile,),
        [
            (dz_own, by_row(dim)),
            (dz_other[0], ((tile, dim), lambda i: (jnp.minimum(i, steps // 2 - 1), 0))),
            (dz_other[1], ((tile, dim), lambda i: (jnp.maximum(i - steps // 2, 0), 0))),
        ]
        + [(v, by_row(dim)) for v in (state, a, cotangent)]
        + [(v, None) for v in (pre_gain, post_gain, *heads_w)],
        [
            (shape(rows, dim), by_row(dim)),
            (shape(rows, dim), by_row(dim)),
            (shape(rows, width), by_row(width)),
            (shape(1, dim, dtype=F32), None),
            (shape(1, dim, dtype=F32), None),
        ],
        vmem=VMEM_BYTES,
        flops=2 * rows * dim * width,
    )


def attend_back_body(
    p, do, q, raw, before, own, gain, cosine, sine, dq_out, before_out, own_out, gain_out, acc
):
    head, part = pl.program_id(0), pl.program_id(1)
    first = (head == 0) & (part == 0)
    last = (head == pl.num_programs(0) - 1) & (part == pl.num_programs(1) - 1)
    rows = before.shape[0]
    dp = jnp.concatenate(
        [
            contract(do[...], before[:, HD:], ((1,), (1,))),
            contract(do[...], own[:, HD:], ((1,), (1,))),
        ],
        axis=1,
    )
    probs = p[...].astype(F32)
    weighted = probs * dp
    ds = (weighted - probs * jnp.sum(weighted, axis=1, keepdims=True)).astype(LOW)
    dq = contract(ds[:, :rows], before[:, :HD], ((1,), (0,)))
    dq += contract(ds[:, rows:], own[:, :HD], ((1,), (0,)))
    dk = contract(ds, q[...], ((0,), (0,))) * SCALE
    dv = contract(p[...], do[...], ((0,), (0,)))
    add_to(acc, jnp.concatenate([dk, dv], axis=1), first)
    back = turn_back(dq * SCALE, cosine[...], sine[...])
    dq_raw, gain_grad = rms_back(raw[...], gain[...], back)
    dq_out[...] = dq_raw.astype(LOW)
    add_to(gain_out, gain_grad, first)

    @pl.when(last)
    def _():
        before_out[...] = acc[:rows].astype(LOW)
        own_out[...] = acc[rows:]


def attend_back(p, do, q, raw, before, own, gain, cosine, sine):
    rows, width = q.shape
    heads = width // HD
    block = row_tile(rows, 512)
    blocks = rows // block
    head_block = ((block, HD), lambda h, i: (i, h))
    table = ((block, HD // 2), lambda h, i: (i, 0))
    return run(
        attend_back_body,
        "attend_back",
        (heads, blocks),
        [
            (p, ((block, 2 * rows), lambda h, i: (h * blocks + i, 0))),
            (do, head_block),
            (q, head_block),
            (raw, head_block),
            (before, None),
            (own, None),
            (gain, None),
            (cosine, table),
            (sine, table),
        ],
        [
            (shape(rows, width), head_block),
            (shape(rows, 2 * HD), None),
            (shape(rows, 2 * HD, dtype=F32), None),
            (shape(1, HD, dtype=F32), None),
        ],
        scratch=[pltpu.VMEM((2 * rows, 2 * HD), F32)],
        vmem=VMEM_BYTES,
        flops=16 * rows * rows * width,
    )


def input_back_body(
    dq, dkv_own, dkv_other, raw, cosine, sine, x, dh, key_gain, in_gain,
    own_w, first_w, second_w, key_w, value_w,
    grad_out, dkv_out, key_gain_out, in_gain_out,
):
    first = pl.program_id(0) == 0
    dkv = dkv_own[...] + dkv_other[...].astype(F32)
    back = turn_back(dkv[:, :HD], cosine[...], sine[...])
    dk, key_grad = rms_back(raw[...], key_gain[...], back)
    dk = dk.astype(LOW)
    dv = dkv[:, HD:].astype(LOW)
    dkv_out[:, :HD] = dk
    dkv_out[:, HD:] = dv
    add_to(key_gain_out, key_grad, first)
    dxn = contract(dk, key_w[...], ((1,), (1,))) + contract(dv, value_w[...], ((1,), (1,)))
    at = 0
    for weight in (own_w, first_w, second_w):
        width = weight.shape[1]
        dxn += contract(dq[:, at : at + width], weight[...], ((1,), (1,)))
        at += width
    dx, in_grad = rms_back(x[...].astype(F32), in_gain[...], dxn)
    grad_out[...] = (dh[...].astype(F32) + dx).astype(LOW)
    add_to(in_gain_out, in_grad, first)


def input_back(dq, dkv_own, dkv_other, raw, cosine, sine, x, dh, key_gain, in_gain, weights):
    rows, dim = x.shape
    width = dq.shape[1]
    tile = row_tile(rows, 512)
    by_row = lambda size: ((tile, size), lambda i: (i, 0))
    return run(
        input_back_body,
        "input_back",
        (rows // tile,),
        [(v, by_row(v.shape[1])) for v in (dq, dkv_own, dkv_other, raw, cosine, sine, x, dh)]
        + [(v, None) for v in (key_gain, in_gain, *weights)],
        [
            (shape(rows, dim), by_row(dim)),
            (shape(rows, 2 * HD), by_row(2 * HD)),
            (shape(1, HD, dtype=F32), None),
            (shape(1, dim, dtype=F32), None),
        ],
        vmem=VMEM_BYTES,
        flops=2 * rows * dim * (width + 2 * HD),
    )


def swap_head(value):
    return lax.ppermute(value, "head", [(0, 1), (1, 0)])


def pair(axis_size, bit):
    return [(i, i ^ (1 << bit)) for i in range(axis_size)]


def tie(*values):
    return lax.optimization_barrier(values)


def sum_parts(parts, choice, columns, dtype):
    total = None
    for array, own, at in parts:
        rows = array.shape[-2]
        value = lax.dynamic_slice(
            array.reshape((2,) * len(own) + array.shape[-2:]),
            [choice.get(b, 0) for b in own] + [0, at],
            [1 if b in choice else 2 for b in own] + [rows, columns],
        )
        value = value.reshape((2,) * sum(b not in choice for b in own) + (rows, columns))
        value = value.astype(F32)
        total = value if total is None else total + value
    return total.astype(dtype)


class Scatter:
    def __init__(self, size, index, order, bits, parts, columns, out=None, low=LOW):
        self.size, self.index, self.order, self.low = size, index, list(order), low
        self.bits, self.parts, self.columns, self.out = list(bits), list(parts), columns, out
        self.gone, self.loaded, self.flying, self.cuts = [], out is not None, False, None
        if out is None:
            self.load()
        else:
            self.drop()

    def value(self, bit):
        return (self.index >> bit) & 1

    def drop(self):
        bit = self.order[0]
        if bit == "head":
            self.columns //= 2
        else:
            self.bits.remove(bit)
            self.gone.append(bit)

    def load(self):
        if not self.order:
            return
        bit = self.order[0]
        choice = {b: self.value(b) for b in self.gone}
        parts, columns = self.parts, self.columns
        if bit == "head":
            columns //= 2
            parts = [(p, own, at + columns) for p, own, at in parts]
        else:
            choice[bit] = 1 - self.value(bit)
        self.out = sum_parts(parts, choice, columns, self.low)
        self.loaded = True
        self.drop()

    def go(self):
        bit = self.order.pop(0)
        if bit == "head":
            self.got = swap_head(self.out)
        else:
            self.got = lax.ppermute(self.out, "dp", pair(self.size, bit))
        self.loaded, self.flying = False, True
        return self

    def take(self):
        self.parts = self.parts + [(self.got, list(self.bits), 0)]
        self.flying = False
        return self

    def land(self):
        self.take().load()
        return self

    def finish(self):
        if self.flying:
            self.take()
        while self.order:
            if not self.loaded:
                self.load()
            self.go().take()
        choice = {b: self.value(b) for b in self.gone}
        return sum_parts(self.parts, choice, self.columns, F32)


class Joint:
    def __init__(self, items):
        self.items, self.cuts = items, None
        self.join()

    def join(self):
        self.order = self.items[0].order
        if self.order:
            self.out = jnp.concatenate([s.out for s in self.items], axis=-1)

    def load(self):
        for s in self.items:
            if not s.loaded:
                s.load()
        self.join()

    def go(self):
        bit = self.order[0]
        self.got = lax.ppermute(self.out, "dp", pair(self.items[0].size, bit))
        for s in self.items:
            s.order.pop(0)
            s.loaded = False
        return self

    def take(self):
        at = 0
        for s in self.items:
            s.parts = s.parts + [(self.got, list(s.bits), at)]
            at += s.columns
        return self


def load_body(*refs):
    count = (len(refs) - 1) // 2
    sems = refs[-1]
    copies = [
        pltpu.make_async_copy(source, target, sems.at[i])
        for i, (source, target) in enumerate(zip(refs[:count], refs[count : 2 * count]))
    ]
    for copy in copies:
        copy.start()
    for copy in copies:
        copy.wait()


def load_weights(weights):
    return pl.pallas_call(
        load_body,
        in_specs=[pl.BlockSpec(memory_space=pl.ANY)] * len(weights),
        out_specs=[pl.BlockSpec(memory_space=pltpu.VMEM)] * len(weights),
        out_shape=[pltpu.VMEM(w.shape, w.dtype) for w in weights],
        scratch_shapes=[pltpu.SemaphoreType.DMA((len(weights),))],
        compiler_params=pltpu.CompilerParams(vmem_limit_bytes=VMEM_BESIDE),
        name="load_weights",
    )(*weights)


def angle_tables(lengths, head_index, rows):
    ids = head_index * rows + jnp.arange(rows, dtype=jnp.int32)
    begin = jnp.zeros_like(ids)
    end = jnp.int32(0)
    for s in range(lengths.shape[0]):
        end = end + lengths[s]
        begin = jnp.where(ids >= end, end, begin)
    frequency = np.power(ROPE_BASE, -2.0 * np.arange(HD // 2) / HD).astype(np.float32)
    grid = (ids - begin).astype(F32)[:, None] * frequency[None, :]
    return jnp.cos(grid), jnp.sin(grid)


def on_device(
    layer_input,
    seq_lengths,
    input_gain,
    query_weight,
    key_weight,
    value_weight,
    query_gain,
    key_gain,
    output_weight,
    post_attn_gain,
    pre_ffn_gain,
    gate_weight,
    up_weight,
    down_weight,
    post_ffn_gain,
    out_cotangent,
):
    rows = layer_input.shape[0]
    dp_size = lax.axis_size("dp")
    bit_count = dp_size.bit_length() - 1
    dp_index = lax.axis_index("dp")
    head_index = lax.axis_index("head")
    core = dp_index & 1
    core_pairs = pair(dp_size, 0)
    width = query_weight.shape[1]
    in_gain, q_gain, k_gain, post_gain, pre_gain, end_gain = (
        g.reshape(1, -1)
        for g in (input_gain, query_gain, key_gain, post_attn_gain, pre_ffn_gain, post_ffn_gain)
    )

    query_mine = lax.dynamic_slice_in_dim(query_weight, core * HD, HD, axis=1)
    output_mine = lax.dynamic_slice_in_dim(output_weight, core * HD, HD, axis=1)
    query_mine, output_mine, layer_input, seq_lengths = tie(
        query_mine, output_mine, layer_input, seq_lengths
    )
    query_first = swap_head(query_mine)

    cosine, sine = angle_tables(seq_lengths[0], head_index, rows)
    meta = jnp.concatenate([head_index.reshape(1).astype(jnp.int32), seq_lengths[0]])
    xn, kv_own, k_raw = project_keys(
        layer_input, in_gain, key_weight, value_weight, k_gain, cosine, sine
    )
    kv_before = lax.ppermute(kv_own, "head", [(0, 1)])
    query_first, kv_own, *weights = tie(
        query_first, kv_own, gate_weight, up_weight, down_weight
    )
    query_second = lax.ppermute(query_first, "dp", core_pairs)
    weights = load_weights(weights)
    xn_in, kv_before, output_mine, *weights = tie(xn, kv_before, output_mine, *weights)
    output_first = swap_head(output_mine)
    weights = [pltpu.with_memory_space_constraint(w, pltpu.VMEM) for w in weights]
    query_w = (query_weight, query_first, query_second)

    q_low, q_raw = project_queries(xn_in, query_w, q_gain, cosine, sine)
    attn_out, probs = attend(meta, q_low, kv_before, kv_own)
    attn_out, output_first = tie(attn_out, output_first)
    output_second = lax.ppermute(output_first, "dp", core_pairs)
    output_w = (output_weight, output_first, output_second)
    attn_proj, state, *z_own = merge_heads(attn_out, output_w, layer_input, post_gain, pre_gain)

    half = rows // 2
    total = 2 * rows
    z_other = [swap_head(z) for z in z_own]
    *kept, f_own0 = ffn_forward(z_own[0], 0, half, weights, 0, total, None, F32)
    z_in, f_own0 = tie(z_other[0], f_own0)
    *kept, f_send0 = ffn_forward(z_in, 0, half, weights, 2, total, kept, LOW)
    z_in, f_send0 = tie(z_other[1], f_send0)
    *kept, f_send1 = ffn_forward(z_in, 0, half, weights, 3, total, kept, LOW)
    f_got0 = swap_head(f_send0)
    z_in, f_send1 = tie(z_own[1], f_send1)
    f_got1 = swap_head(f_send1)
    *kept, f_own1 = ffn_forward(z_in, 0, half, weights, 1, total, kept, F32)
    hid, act, slope = kept
    f_got0, f_own0, f_own1 = tie(f_got0, f_own0, f_own1)
    layer_output, df_own0, end_grad0 = ffn_end(
        f_own0, f_got0, state, out_cotangent, end_gain, 0, None
    )
    df_other0 = swap_head(df_own0)
    layer_output, df_own1, end_grad1 = ffn_end(
        f_own1, f_got1, state, out_cotangent, end_gain, 1, layer_output
    )
    df_other1 = swap_head(df_own1)
    df_own = [df_own0, df_own1]
    *made, own_zgrad = ffn_backward(df_own, act, slope, weights, 0, None, LOW, 1, True)
    df_other0, df_other1, own_zgrad = tie(df_other0, df_other1, own_zgrad)
    df_other = [df_other0, df_other1]
    units = hid.shape[1]
    order = list(range(bit_count))
    rest = order[1:]
    leading = rest[::-1]
    third = units // 3

    def start(pairs, first, last, route=order, **options):
        send, keep = weight_grad(pairs, core, dp_size, first, last, **options)
        columns = last - first
        return Scatter(
            dp_size, dp_index, route, order[::-1], [(keep, leading, 0)], columns, send
        )

    def cut(whole, at, columns, route=rest):
        parts = [(p, own, at) for p, own, _ in whole.parts]
        return Scatter(dp_size, dp_index, route, leading, parts, columns)

    def later(value, scatter):
        tied = tie(*[p for p, _, _ in scatter.parts], value)
        scatter.parts = [(p, own, at) for p, (_, own, at) in zip(tied, scatter.parts)]

    def phase(values, end=(), go=(), now=(), hold=()):
        count = len(values)
        done = list(end) + list(now) + list(hold)
        tied = list(tie(*values, *[s.got for s in done], *[s.out for s in go]))
        for s in go[::-1]:
            s.out = tied.pop()
        for s in done[::-1]:
            s.got = tied.pop()
            s.take()
        for s in go:
            s.go()
        for s in list(now) + [s for s in end if s.cuts is None]:
            s.load()
        if now:
            tied = list(tie(*tied, *[s.out for s in now]))
            for s in now[::-1]:
                s.out = tied.pop()
                s.go()
        return tied

    df_all = df_own + df_other
    down_a = start([(df_all, hid)], 0, 2 * third, vmem=VMEM_BESIDE)
    (hid,) = phase([hid], go=[down_a])
    down_b = start([(df_all, hid)], 2 * third, units, vmem=VMEM_BESIDE)
    down_a.cuts = down_b.cuts = 1
    (df_other0,) = phase([df_other0], end=[down_a], go=[down_b])
    d1 = cut(down_a, 0, 2 * third)
    (df_other0,) = phase([df_other0], go=[d1])
    *made, dz0, dz1 = ffn_backward(
        [df_other0, df_other1],
        act,
        slope,
        (gate_weight, up_weight, down_weight),
        1,
        made,
        LOW,
        2,
        False,
    )
    dgate, dup = made
    dz0, dz1, dgate = phase([dz0, dz1, dgate], end=[down_b, d1])
    d2 = cut(down_b, 0, third)
    dz0, dz1, dgate = phase([dz0, dz1, dgate], go=[d2])
    other0 = swap_head(dz0)
    z_both = z_own + z_other
    gate_s = start([(z_both, dgate)], 0, units)
    other0, dz1, dup = phase([other0, dz1, dup], end=[d2], go=[gate_s, d1])
    other1 = swap_head(dz1)
    up_s = start([(z_both, dup)], 0, units)
    gate_s.cuts = up_s.cuts = 1
    own_zgrad, other0, other1 = phase(
        [own_zgrad, other0, other1], end=[gate_s], go=[up_s, d2], hold=[d1]
    )
    g1 = cut(gate_s, 0, 2 * third)
    (own_zgrad,) = phase([own_zgrad], go=[g1])
    other_zgrad = [other0, other1]

    state_grad, attn_grad, heads_grad, pre_grad, post_grad = state_back(
        own_zgrad, other_zgrad, state, attn_proj, out_cotangent, pre_gain, post_gain, output_w
    )

    own_heads = width // HD

    def head_block(j, c):
        return jnp.where(j < own_heads, j, own_heads + ((j - own_heads) ^ c))

    def start_heads(left, right):
        route = [order[0], "head"] + rest
        return start([([left], right)], 0, 2 * width, route, tile=HD, columns_of=head_block)

    dq, kv_back_send, kv_grad, q_gain_grad = attend_back(
        probs, heads_grad, q_low, q_raw, kv_before, kv_own, q_gain, cosine, sine
    )
    attn_grad, dq = tie(attn_grad, dq)
    output_s = start_heads(attn_grad, attn_out)
    later(output_s.out, gate_s)
    later(output_s.out, d1)
    d1.load()
    g2 = cut(gate_s, 2 * third, third)
    dq, kv_back_send = phase(
        [dq, kv_back_send], end=[up_s, g1, d2], go=[g2, output_s, d1]
    )
    kv_back = lax.ppermute(kv_back_send, "head", [(1, 0)])
    query_s = start_heads(xn, dq)
    later(query_s.out, up_s)
    u1 = cut(up_s, 0, 2 * third)
    dq, kv_grad, kv_back = phase(
        [dq, kv_grad, kv_back], end=[g2, d1], go=[query_s, u1, g1, d2], now=[output_s]
    )
    input_grad, dkv, k_gain_grad, in_gain_grad = input_back(
        dq, kv_grad, kv_back, k_raw, cosine, sine, layer_input, state_grad, k_gain, in_gain,
        query_w + (key_weight, value_weight),
    )
    kv_s = start([([xn], dkv)], 0, 2 * HD)
    later(kv_s.out, up_s)
    u2 = cut(up_s, 2 * third, third)
    (wait,) = phase(
        [in_gain_grad], end=[u1, d2, output_s], go=[u2, kv_s], now=[query_s, g1]
    )
    middle = Joint([g2, u1])
    (wait,) = phase([wait], go=[middle])
    gains = [wait, post_grad, pre_grad, end_grad0 + end_grad1, q_gain_grad, k_gain_grad]
    gains = [g.reshape(dp_size, -1) for g in gains]
    widths = [g.shape[1] for g in gains]
    block = layer_input.shape[1] // dp_size
    packed = jnp.concatenate(gains, axis=1)
    packed = jnp.pad(packed, ((0, 0), (0, block * 64 - packed.shape[1])))
    packed = packed.reshape(dp_size // 2, block, 128).astype(LOW)
    gains_s = Scatter(dp_size, dp_index, rest, leading, [(packed, leading, 0)], 128)
    wait, query_s.got, kv_s.got, u2.got, gains_s.out = tie(
        wait, query_s.got, kv_s.got, u2.got, gains_s.out
    )
    for s in (query_s, kv_s, u2):
        s.take().load()
    tail = Joint([output_s, query_s, kv_s, gains_s])
    (wait,) = phase([wait], end=[g1], go=[tail, u2], now=[middle])
    (wait,) = phase([wait], end=[middle], now=[tail, u2])
    (wait,) = phase([wait], end=[u2], now=[tail])
    (wait,) = phase([wait], end=[tail])
    down_part = jnp.concatenate([d1.finish(), d2.finish()], axis=1)
    gate_part = jnp.concatenate([g1.finish(), g2.finish()], axis=1)
    up_part = jnp.concatenate([u1.finish(), u2.finish()], axis=1)
    output_part = output_s.finish()
    query_part = query_s.finish()
    packed = gains_s.finish()
    pick = lambda which: lax.dynamic_slice_in_dim(packed, which * (block // 2), block // 2, axis=0)
    packed = pick(core) + lax.ppermute(pick(1 - core), "dp", core_pairs)
    packed = jnp.pad(packed, ((0, block - block // 2), (0, 0)))
    kv_sum = jnp.concatenate([kv_s.finish(), packed], axis=1)
    kv_sum = kv_sum + swap_head(kv_sum.astype(LOW)).astype(F32)
    packed = kv_sum[:, 2 * HD :].reshape(-1)
    pieces = []
    at = 0
    for size in widths:
        pieces.append(packed[at : at + size])
        at += size
    return (
        layer_output,
        input_grad,
        pieces[0],
        query_part,
        kv_sum[:, :HD],
        kv_sum[:, HD : 2 * HD],
        pieces[4],
        pieces[5],
        output_part,
        pieces[1],
        pieces[2],
        gate_part,
        up_part,
        down_part,
        pieces[3],
    )


def solution(mesh):
    placed = (
        P(("dp", "head"), None),
        P("dp", None),
        P(),
        P(None, "head"),
        P(),
        P(),
        P(),
        P(),
        P(None, "head"),
        P(),
        P(),
        P(None, "head"),
        P(None, "head"),
        P(None, "head"),
        P(),
        P(("dp", "head"), None),
    )
    return jax.shard_map(
        on_device,
        mesh=mesh,
        in_specs=placed,
        out_specs=(
            P(("dp", "head"), None),
            P(("dp", "head"), None),
            P("dp"),
            P("dp", "head"),
            P("dp", None),
            P("dp", None),
            P("dp"),
            P("dp"),
            P("dp", "head"),
            P("dp"),
            P("dp"),
            P("dp", "head"),
            P("dp", "head"),
            P("dp", "head"),
            P("dp"),
        ),
        check_vma=False,
    )
```

```python
import jax
import jax.numpy as jnp
import numpy as np
from jax import lax
from jax.experimental import pallas as pl
from jax.experimental.pallas import tpu as pltpu
from jax.sharding import PartitionSpec as P

HD = 256
EPSILON = 1e-06
ROPE_BASE = 1000000.0
NEG_FILL = -1e30
LOW = jnp.bfloat16
F32 = jnp.float32
ROOT = 0.7978845608028654
CUBIC = 0.044715
SCALE = HD ** (-0.5)
VMEM_BESIDE = 30 << 20
VMEM_BYTES = 60 << 20


def shape(*dims, dtype=LOW):
    return jax.ShapeDtypeStruct(dims, dtype)


def contract(left, right, dims):
    return lax.dot_general(left, right, (dims, ((), ())), preferred_element_type=F32)


def rms_scale(values):
    return lax.rsqrt(jnp.mean(values * values, axis=-1, keepdims=True) + EPSILON)


def rms_back(values, gain, cotangent):
    scale = rms_scale(values)
    unit = values * scale
    scaled = cotangent * (1.0 + gain)
    back = scale * (scaled - unit * jnp.mean(scaled * unit, axis=-1, keepdims=True))
    return back, jnp.sum(cotangent * unit, axis=0, keepdims=True)


def turn(values, cosine, sine):
    half = HD // 2
    first, second = values[:, :half], values[:, half:]
    return jnp.concatenate([first * cosine - second * sine, second * cosine + first * sine], axis=1)


def turn_back(values, cosine, sine):
    return turn(values, cosine, -sine)


def add_to(ref, value, first):
    @pl.when(first)
    def _():
        ref[...] = value

    @pl.when(jnp.logical_not(first))
    def _():
        ref[...] += value


def run(body, name, grid, inputs, outputs, scratch=(), scalars=(), aliases=None, flops=0, vmem=VMEM_BESIDE, hbm=True):
    def spec(array, block):
        if block is None:
            dims = tuple(array.shape)
            return pl.BlockSpec(dims, lambda *_: (0,) * len(dims))
        if block == "any":
            return pl.BlockSpec(memory_space=pl.ANY)
        if block == "vmem":
            return pl.BlockSpec(memory_space=pltpu.VMEM)
        return pl.BlockSpec(*block)

    arrays = [a for a, _ in inputs]
    out_shape = [o for o, _ in outputs]
    if hbm:
        arrays = [
            a if b == "vmem" else pltpu.with_memory_space_constraint(a, pltpu.HBM)
            for a, b in inputs
        ]
    moved = sum(a.size * a.dtype.itemsize for a, _ in inputs)
    moved += sum(int(np.prod(o.shape)) * o.dtype.itemsize for o in out_shape)
    return pl.pallas_call(
        body,
        grid_spec=pltpu.PrefetchScalarGridSpec(
            num_scalar_prefetch=len(scalars),
            grid=grid,
            in_specs=[spec(a, b) for a, b in inputs],
            out_specs=[spec(o, b) for o, b in outputs],
            scratch_shapes=list(scratch),
        ),
        out_shape=[pltpu.HBM(o.shape, o.dtype) for o in out_shape] if hbm else out_shape,
        input_output_aliases={} if aliases is None else aliases,
        compiler_params=pltpu.CompilerParams(vmem_limit_bytes=vmem),
        cost_estimate=pl.CostEstimate(flops=flops, transcendentals=0, bytes_accessed=moved),
        name=name,
    )(*scalars, *arrays)


def column_tile(units):
    for tile in (1152, 1024, 768, 512, 384, 256, 128):
        if units % tile == 0:
            return tile
    return units


def row_tile(rows, most):
    tile = most
    while rows % tile:
        tile //= 2
    return tile


def keys_body(x, gain, key_w, value_w, key_gain, cosine, sine, xn_out, kv_out, raw_out):
    values = x[...].astype(F32)
    xn = (values * rms_scale(values) * (1.0 + gain[...])).astype(LOW)
    xn_out[...] = xn
    raw = contract(xn, key_w[...], ((1,), (0,)))
    raw_out[...] = raw
    unit = raw * rms_scale(raw) * (1.0 + key_gain[...])
    kv_out[:, :HD] = turn(unit, cosine[...], sine[...]).astype(LOW)
    kv_out[:, HD:] = contract(xn, value_w[...], ((1,), (0,))).astype(LOW)


def project_keys(x, gain, key_w, value_w, key_gain, cosine, sine):
    rows, dim = x.shape
    tile = row_tile(rows, 256)
    by_row = lambda width: ((tile, width), lambda i: (i, 0))
    return run(
        keys_body,
        "project_keys",
        (rows // tile,),
        [
            (x, by_row(dim)),
            (gain, None),
            (key_w, None),
            (value_w, None),
            (key_gain, None),
            (cosine, by_row(HD // 2)),
            (sine, by_row(HD // 2)),
        ],
        [
            (shape(rows, dim), by_row(dim)),
            (shape(rows, 2 * HD), by_row(2 * HD)),
            (shape(rows, HD, dtype=F32), by_row(HD)),
        ],
        flops=4 * rows * dim * HD,
    )


def queries_body(xn, own_w, first_w, second_w, gain, cosine, sine, q_out, raw_out):
    values = xn[...]
    start = 0
    for weight in (own_w, first_w, second_w):
        raw_all = contract(values, weight[...], ((1,), (0,)))
        for at in range(0, weight.shape[1], HD):
            raw = raw_all[:, at : at + HD]
            unit = raw * rms_scale(raw) * (1.0 + gain[...])
            raw_out[:, start : start + HD] = raw
            q_out[:, start : start + HD] = turn(unit, cosine[...], sine[...]).astype(LOW)
            start += HD


def project_queries(xn, heads_w, gain, cosine, sine):
    rows, dim = xn.shape
    width = sum(w.shape[1] for w in heads_w)
    tile = row_tile(rows, 256)
    by_row = lambda size: ((tile, size), lambda i: (i, 0))
    return run(
        queries_body,
        "project_queries",
        (rows // tile,),
        [(xn, by_row(dim))]
        + [(w, None) for w in heads_w]
        + [(gain, None), (cosine, by_row(HD // 2)), (sine, by_row(HD // 2))],
        [(shape(rows, width), by_row(width)), (shape(rows, width, dtype=F32), by_row(width))],
        flops=2 * rows * dim * width,
    )


def attend_body(slots, meta, q, before, own, o_out, p_out, bias):
    block, keys = bias.shape
    rows = keys // 2

    @pl.when(pl.program_id(1) == 0)
    def _():
        second = meta[0]
        first_row = second * rows + pl.program_id(0) * block
        query = first_row + lax.broadcasted_iota(jnp.int32, (block, keys), 0)
        column = lax.broadcasted_iota(jnp.int32, (block, keys), 1)
        is_own = column >= rows
        key = jnp.where(is_own, column + (second - 1) * rows, column)
        ends = jnp.int32(0)
        query_segment = jnp.zeros((block, keys), jnp.int32)
        key_segment = jnp.zeros((block, keys), jnp.int32)
        for s in range(slots):
            ends = ends + meta[1 + s]
            query_segment += (query >= ends).astype(jnp.int32)
            key_segment += (key >= ends).astype(jnp.int32)
        known = is_own | (column < second * rows)
        seen = (key < query) & (query_segment == key_segment) & (query_segment < slots) & known
        seen = seen | (is_own & (key == query))
        bias[...] = jnp.where(seen, 0.0, NEG_FILL)

    scaled = q[...] * LOW(SCALE)
    scores = jnp.concatenate(
        [
            contract(scaled, before[:, :HD], ((1,), (1,))),
            contract(scaled, own[:, :HD], ((1,), (1,))),
        ],
        axis=1,
    )
    scores = scores + bias[...]
    exps = jnp.exp(scores - jnp.max(scores, axis=1, keepdims=True))
    probs = (exps * (1.0 / jnp.sum(exps, axis=1, keepdims=True))).astype(LOW)
    p_out[...] = probs
    out = contract(probs[:, :rows], before[:, HD:], ((1,), (0,)))
    out += contract(probs[:, rows:], own[:, HD:], ((1,), (0,)))
    o_out[...] = out.astype(LOW)


def attend(meta, q, before, own):
    rows, width = q.shape
    heads = width // HD
    block = row_tile(rows, 512)
    blocks = rows // block
    slots = meta.shape[0] - 1
    head_block = ((block, HD), lambda i, h, m: (i, h))
    return run(
        lambda *refs: attend_body(slots, *refs),
        "attend",
        (blocks, heads),
        [(q, head_block), (before, None), (own, None)],
        [
            (shape(rows, width), head_block),
            (shape(heads * rows, 2 * rows), ((block, 2 * rows), lambda i, h, m: (h * blocks + i, 0))),
        ],
        scratch=[pltpu.VMEM((block, 2 * rows), F32)],
        scalars=[meta],
        flops=8 * rows * rows * width,
    )


def merge_body(o, own_w, first_w, second_w, x, post_gain, pre_gain, a_out, state_out, first_out, second_out):
    start = 0
    total = None
    for weight in (own_w, first_w, second_w):
        width = weight.shape[1]
        part = contract(o[:, start : start + width], weight[...], ((1,), (1,)))
        total = part if total is None else total + part
        start += width
    a_out[...] = total.astype(a_out.dtype)
    state = x[...].astype(F32) + total * rms_scale(total) * (1.0 + post_gain[...])
    state_out[...] = state.astype(state_out.dtype)
    z = (state * rms_scale(state) * (1.0 + pre_gain[...])).astype(LOW)
    early = pl.program_id(0) < pl.num_programs(0) // 2

    @pl.when(early)
    def _():
        first_out[...] = z

    @pl.when(jnp.logical_not(early))
    def _():
        second_out[...] = z


def merge_heads(o, heads_w, x, post_gain, pre_gain):
    rows, dim = x.shape
    width = o.shape[1]
    tile = row_tile(rows, 256)
    by_row = lambda size: ((tile, size), lambda i: (i, 0))
    half = rows // tile // 2
    return run(
        merge_body,
        "merge_heads",
        (rows // tile,),
        [(o, by_row(width))]
        + [(w, None) for w in heads_w]
        + [(x, by_row(dim)), (post_gain, None), (pre_gain, None)],
        [
            (shape(rows, dim), by_row(dim)),
            (shape(rows, dim), by_row(dim)),
            (shape(rows // 2, dim), ((tile, dim), lambda i: (jnp.minimum(i, half - 1), 0))),
            (shape(rows // 2, dim), ((tile, dim), lambda i: (jnp.maximum(i - half, 0), 0))),
        ],
        flops=2 * rows * dim * width,
    )


def ffn_forward_body(z, gate_w, up_w, down_w, *rest):
    hid_out, act_out, slope_out, f_out, acc = rest[-5:]
    step, last = pl.program_id(0), pl.num_programs(0) - 1
    tile = hid_out.shape[1]
    here = pl.ds(pl.multiple_of(step * tile, 128), tile)
    gate = contract(z[...], gate_w[:, here], ((1,), (0,)))
    up = contract(z[...], up_w[:, here], ((1,), (0,)))
    square = gate * gate
    tanh = jnp.tanh(ROOT * gate * (1.0 + CUBIC * square))
    half = 0.5 * (1.0 + tanh)
    act = gate * half
    slope = half + 0.5 * gate * (1.0 - tanh * tanh) * (ROOT * (1.0 + 3.0 * CUBIC * square))
    hid = (act * up).astype(LOW)
    hid_out[...] = hid
    act_out[...] = act.astype(LOW)
    slope_out[...] = (slope * up).astype(LOW)
    add_to(acc, contract(hid, down_w[:, here], ((1,), (1,))), step == 0)

    @pl.when(step == last)
    def _():
        f_out[...] = acc[...].astype(f_out.dtype)


def ffn_forward(z, z_block, rows, weights, block, total, kept, out_dtype):
    dim, units = weights[0].shape
    tile = column_tile(units)
    inner = ((rows, tile), lambda j: (block, j))
    extra = [] if kept is None else list(kept)
    return run(
        ffn_forward_body,
        "ffn_forward",
        (units // tile,),
        [(z, ((rows, dim), lambda j: (z_block, 0)))]
        + [(w, "vmem") for w in weights]
        + [(k, "any") for k in extra],
        [(shape(total, units), inner)] * 3 + [(shape(rows, dim, dtype=out_dtype), None)],
        scratch=[pltpu.VMEM((rows, dim), F32)],
        aliases={4 + i: i for i in range(len(extra))},
        hbm=False,
        flops=6 * rows * dim * units,
    )


def ffn_end_body(f_own, f_other, state, cotangent, gain, *rest):
    out, df_out, gain_out = rest[-3:]
    f = f_own[...] + f_other[...].astype(F32)
    out[...] = (state[...].astype(F32) + f * rms_scale(f) * (1.0 + gain[...])).astype(LOW)
    df, gain_grad = rms_back(f, gain[...], cotangent[...].astype(F32))
    df_out[...] = df.astype(LOW)
    add_to(gain_out, gain_grad, pl.program_id(0) == 0)


def ffn_end(f_own, f_other, state, cotangent, gain, chunk, out):
    rows, dim = f_own.shape
    tile = row_tile(rows, 128)
    steps = rows // tile
    here = ((tile, dim), lambda i: (i, 0))
    there = ((tile, dim), lambda i: (chunk * steps + i, 0))
    extra = [] if out is None else [out]
    return run(
        ffn_end_body,
        "ffn_end",
        (steps,),
        [(f_own, here), (f_other, here), (state, there), (cotangent, there), (gain, None)]
        + [(e, "any") for e in extra],
        [(shape(*state.shape), there), (shape(rows, dim), here), (shape(1, dim, dtype=F32), None)],
        aliases={5: 0} if extra else None,
    )


def ffn_backward_body(pieces, splits, *refs):
    dfs = refs[:pieces]
    act, slope, gate_w, up_w, down_w = refs[pieces : pieces + 5]
    *outs, acc, df = refs[pieces + 5 :]
    dgate_out, dup_out, *dz_outs = outs[-2 - splits :]
    step, last = pl.program_id(0), pl.num_programs(0) - 1

    @pl.when(step == 0)
    def _():
        at = 0
        for piece in dfs:
            df[at : at + piece.shape[0]] = piece[...]
            at += piece.shape[0]

    tile = dup_out.shape[1]
    if gate_w.shape[1] == tile:
        here = slice(None)
    else:
        here = pl.ds(pl.multiple_of(step * tile, 128), tile)
    dhid = contract(df[...], down_w[:, here], ((1,), (0,)))
    dup = (dhid * act[...].astype(F32)).astype(LOW)
    dgate = (dhid * slope[...].astype(F32)).astype(LOW)
    dup_out[...] = dup
    dgate_out[...] = dgate
    part = contract(dgate, gate_w[:, here], ((1,), (1,)))
    part += contract(dup, up_w[:, here], ((1,), (1,)))
    add_to(acc, part, step == 0)

    @pl.when(step == last)
    def _():
        at = 0
        for dz_out in dz_outs:
            size = dz_out.shape[0]
            dz_out[...] = acc[at : at + size].astype(dz_out.dtype)
            at += size


def ffn_backward(dfs, act, slope, weights, block, made, out_dtype, splits, resident):
    rows = sum(d.shape[0] for d in dfs)
    total, units = act.shape
    dim = dfs[0].shape[1]
    tile = column_tile(units)
    inner = ((rows, tile), lambda j: (block, j))
    weight = "vmem" if resident else ((dim, tile), lambda j: (0, j))
    extra = [] if made is None else list(made)
    return run(
        lambda *refs: ffn_backward_body(len(dfs), splits, *refs),
        "ffn_backward",
        (units // tile,),
        [(d, None) for d in dfs]
        + [(act, inner), (slope, inner)]
        + [(w, weight) for w in weights]
        + [(e, "any") for e in extra],
        [(shape(total, units), inner)] * 2
        + [(shape(rows // splits, dim, dtype=out_dtype), None)] * splits,
        scratch=[pltpu.VMEM((rows, dim), F32), pltpu.VMEM((rows, dim), LOW)],
        aliases={len(dfs) + 5 + i: i for i in range(len(extra))},
        flops=6 * rows * dim * units,
        vmem=VMEM_BESIDE if resident else VMEM_BYTES,
    )


def weight_grad_body(sides, core, *refs):
    *inputs, send, keep = refs
    groups, rows, _ = keep.shape
    first = core[0] == 0

    def write(lefts, right):
        at = 0
        total = None
        for left in lefts:
            size = left.shape[0]
            part = contract(left[...], right[at : at + size], ((0,), (0,)))
            total = part if total is None else total + part
            at += size
        for i in range(groups):
            even = total[2 * i * rows : (2 * i + 1) * rows].astype(LOW)
            odd = total[(2 * i + 1) * rows : (2 * i + 2) * rows].astype(LOW)
            send[i] = jnp.where(first, odd, even)
            keep[i] = jnp.where(first, even, odd)

    at = 0
    for side, count in enumerate(sides):
        lefts, right = inputs[at : at + count], inputs[at + count]
        at += count + 1
        if len(sides) == 1:
            write(lefts, right)
        else:
            mine = (pl.program_id(0) % len(sides)) == side
            pl.when(mine)(lambda lefts=lefts, right=right: write(lefts, right))


def weight_grad(
    pairs, core, axis_size, start, stop, tile=None, columns_of=None, vmem=VMEM_BYTES
):
    dim = pairs[0][0][0].shape[1]
    columns = stop - start
    rows = dim // axis_size
    groups = axis_size // 2
    tile = column_tile(columns) if tile is None else tile
    blocks = columns // tile
    if columns_of is None:
        columns_of = lambda j, c: j + start // tile
    if rows % 8:
        full = []
        for j in range(blocks):
            lefts, right = pairs[j % len(pairs)]
            left = jnp.concatenate(lefts, axis=0)
            at = columns_of(j, core) * tile
            here = lax.dynamic_slice_in_dim(right, at, tile, axis=1)
            full.append(contract(left, here, ((0,), (0,))).astype(LOW))
        full = jnp.concatenate(full, axis=1).reshape(groups, 2, rows, columns)
        return (
            lax.dynamic_index_in_dim(full, 1 - core, axis=1, keepdims=False),
            lax.dynamic_index_in_dim(full, core, axis=1, keepdims=False),
        )
    inputs = []
    for lefts, right in pairs:
        inputs += [(left, None) for left in lefts]
        inputs.append((right, ((right.shape[0], tile), lambda j, c: (0, columns_of(j, c[0])))))
    out = (shape(groups, rows, columns), ((groups, rows, tile), lambda j, c: (0, 0, j)))
    sides = [len(lefts) for lefts, _ in pairs]
    return run(
        lambda *refs: weight_grad_body(sides, *refs),
        "weight_grad",
        (blocks,),
        inputs,
        [out, out],
        scalars=[core.reshape(1)],
        flops=2 * pairs[0][1].shape[0] * dim * columns,
        vmem=vmem,
    )


def state_back_body(
    dz_own, dz_first, dz_second, state, a, cotangent, pre_gain, post_gain, own_w, first_w, second_w,
    dh_out, da_out, do_out, pre_out, post_out,
):
    first = pl.program_id(0) == 0
    early = pl.program_id(0) < pl.num_programs(0) // 2
    dz = dz_own[...].astype(F32) + jnp.where(early, dz_first[...], dz_second[...]).astype(F32)
    back, pre_grad = rms_back(state[...].astype(F32), pre_gain[...], dz)
    dh = cotangent[...].astype(F32) + back
    dh_out[...] = dh.astype(dh_out.dtype)
    da, post_grad = rms_back(a[...].astype(F32), post_gain[...], dh)
    da = da.astype(LOW)
    da_out[...] = da
    add_to(pre_out, pre_grad, first)
    add_to(post_out, post_grad, first)
    at = 0
    for weight in (own_w, first_w, second_w):
        width = weight.shape[1]
        do_out[:, at : at + width] = contract(da, weight[...], ((1,), (0,))).astype(LOW)
        at += width


def state_back(dz_own, dz_other, state, a, cotangent, pre_gain, post_gain, heads_w):
    rows, dim = state.shape
    width = sum(w.shape[1] for w in heads_w)
    tile = row_tile(rows, 256)
    steps = rows // tile
    by_row = lambda size: ((tile, size), lambda i: (i, 0))
    return run(
        state_back_body,
        "state_back",
        (rows // tile,),
        [
            (dz_own, by_row(dim)),
            (dz_other[0], ((tile, dim), lambda i: (jnp.minimum(i, steps // 2 - 1), 0))),
            (dz_other[1], ((tile, dim), lambda i: (jnp.maximum(i - steps // 2, 0), 0))),
        ]
        + [(v, by_row(dim)) for v in (state, a, cotangent)]
        + [(v, None) for v in (pre_gain, post_gain, *heads_w)],
        [
            (shape(rows, dim), by_row(dim)),
            (shape(rows, dim), by_row(dim)),
            (shape(rows, width), by_row(width)),
            (shape(1, dim, dtype=F32), None),
            (shape(1, dim, dtype=F32), None),
        ],
        vmem=VMEM_BYTES,
        flops=2 * rows * dim * width,
    )


def attend_back_body(
    p, do, q, raw, before, own, gain, cosine, sine, dq_out, before_out, own_out, gain_out, acc
):
    head, part = pl.program_id(0), pl.program_id(1)
    first = (head == 0) & (part == 0)
    last = (head == pl.num_programs(0) - 1) & (part == pl.num_programs(1) - 1)
    rows = before.shape[0]
    dp = jnp.concatenate(
        [
            contract(do[...], before[:, HD:], ((1,), (1,))),
            contract(do[...], own[:, HD:], ((1,), (1,))),
        ],
        axis=1,
    )
    probs = p[...].astype(F32)
    weighted = probs * dp
    ds = (weighted - probs * jnp.sum(weighted, axis=1, keepdims=True)).astype(LOW)
    dq = contract(ds[:, :rows], before[:, :HD], ((1,), (0,)))
    dq += contract(ds[:, rows:], own[:, :HD], ((1,), (0,)))
    dk = contract(ds, q[...], ((0,), (0,))) * SCALE
    dv = contract(p[...], do[...], ((0,), (0,)))
    add_to(acc, jnp.concatenate([dk, dv], axis=1), first)
    back = turn_back(dq * SCALE, cosine[...], sine[...])
    dq_raw, gain_grad = rms_back(raw[...], gain[...], back)
    dq_out[...] = dq_raw.astype(LOW)
    add_to(gain_out, gain_grad, first)

    @pl.when(last)
    def _():
        before_out[...] = acc[:rows].astype(LOW)
        own_out[...] = acc[rows:]


def attend_back(p, do, q, raw, before, own, gain, cosine, sine):
    rows, width = q.shape
    heads = width // HD
    block = row_tile(rows, 512)
    blocks = rows // block
    head_block = ((block, HD), lambda h, i: (i, h))
    table = ((block, HD // 2), lambda h, i: (i, 0))
    return run(
        attend_back_body,
        "attend_back",
        (heads, blocks),
        [
            (p, ((block, 2 * rows), lambda h, i: (h * blocks + i, 0))),
            (do, head_block),
            (q, head_block),
            (raw, head_block),
            (before, None),
            (own, None),
            (gain, None),
            (cosine, table),
            (sine, table),
        ],
        [
            (shape(rows, width), head_block),
            (shape(rows, 2 * HD), None),
            (shape(rows, 2 * HD, dtype=F32), None),
            (shape(1, HD, dtype=F32), None),
        ],
        scratch=[pltpu.VMEM((2 * rows, 2 * HD), F32)],
        vmem=VMEM_BYTES,
        flops=16 * rows * rows * width,
    )


def input_back_body(
    dq, dkv_own, dkv_other, raw, cosine, sine, x, dh, key_gain, in_gain,
    own_w, first_w, second_w, key_w, value_w,
    grad_out, dkv_out, key_gain_out, in_gain_out,
):
    first = pl.program_id(0) == 0
    dkv = dkv_own[...] + dkv_other[...].astype(F32)
    back = turn_back(dkv[:, :HD], cosine[...], sine[...])
    dk, key_grad = rms_back(raw[...], key_gain[...], back)
    dk = dk.astype(LOW)
    dv = dkv[:, HD:].astype(LOW)
    dkv_out[:, :HD] = dk
    dkv_out[:, HD:] = dv
    add_to(key_gain_out, key_grad, first)
    dxn = contract(dk, key_w[...], ((1,), (1,))) + contract(dv, value_w[...], ((1,), (1,)))
    at = 0
    for weight in (own_w, first_w, second_w):
        width = weight.shape[1]
        dxn += contract(dq[:, at : at + width], weight[...], ((1,), (1,)))
        at += width
    dx, in_grad = rms_back(x[...].astype(F32), in_gain[...], dxn)
    grad_out[...] = (dh[...].astype(F32) + dx).astype(LOW)
    add_to(in_gain_out, in_grad, first)


def input_back(dq, dkv_own, dkv_other, raw, cosine, sine, x, dh, key_gain, in_gain, weights):
    rows, dim = x.shape
    width = dq.shape[1]
    tile = row_tile(rows, 256)
    by_row = lambda size: ((tile, size), lambda i: (i, 0))
    return run(
        input_back_body,
        "input_back",
        (rows // tile,),
        [(v, by_row(v.shape[1])) for v in (dq, dkv_own, dkv_other, raw, cosine, sine, x, dh)]
        + [(v, None) for v in (key_gain, in_gain, *weights)],
        [
            (shape(rows, dim), by_row(dim)),
            (shape(rows, 2 * HD), by_row(2 * HD)),
            (shape(1, HD, dtype=F32), None),
            (shape(1, dim, dtype=F32), None),
        ],
        vmem=VMEM_BYTES,
        flops=2 * rows * dim * (width + 2 * HD),
    )


def swap_head(value):
    return lax.ppermute(value, "head", [(0, 1), (1, 0)])


def pair(axis_size, bit):
    return [(i, i ^ (1 << bit)) for i in range(axis_size)]


def tie(*values):
    return lax.optimization_barrier(values)


def sum_parts(parts, choice, columns, dtype):
    total = None
    for array, own, at in parts:
        rows = array.shape[-2]
        value = lax.dynamic_slice(
            array.reshape((2,) * len(own) + array.shape[-2:]),
            [choice.get(b, 0) for b in own] + [0, at],
            [1 if b in choice else 2 for b in own] + [rows, columns],
        )
        value = value.reshape((2,) * sum(b not in choice for b in own) + (rows, columns))
        value = value.astype(F32)
        total = value if total is None else total + value
    return total.astype(dtype)


class Scatter:
    def __init__(self, size, index, order, bits, parts, columns, out=None, low=LOW):
        self.size, self.index, self.order, self.low = size, index, list(order), low
        self.bits, self.parts, self.columns, self.out = list(bits), list(parts), columns, out
        self.gone, self.loaded, self.flying, self.cuts = [], out is not None, False, None
        if out is None:
            self.load()
        else:
            self.drop()

    def value(self, bit):
        return (self.index >> bit) & 1

    def drop(self):
        bit = self.order[0]
        if bit == "head":
            self.columns //= 2
        else:
            self.bits.remove(bit)
            self.gone.append(bit)

    def load(self):
        if not self.order:
            return
        bit = self.order[0]
        choice = {b: self.value(b) for b in self.gone}
        parts, columns = self.parts, self.columns
        if bit == "head":
            columns //= 2
            parts = [(p, own, at + columns) for p, own, at in parts]
        else:
            choice[bit] = 1 - self.value(bit)
        self.out = sum_parts(parts, choice, columns, self.low)
        self.loaded = True
        self.drop()

    def go(self):
        bit = self.order.pop(0)
        if bit == "head":
            self.got = swap_head(self.out)
        else:
            self.got = lax.ppermute(self.out, "dp", pair(self.size, bit))
        self.loaded, self.flying = False, True
        return self

    def take(self):
        self.parts = self.parts + [(self.got, list(self.bits), 0)]
        self.flying = False
        return self

    def land(self):
        self.take().load()
        return self

    def finish(self):
        if self.flying:
            self.take()
        while self.order:
            if not self.loaded:
                self.load()
            self.go().take()
        choice = {b: self.value(b) for b in self.gone}
        return sum_parts(self.parts, choice, self.columns, F32)


class Joint:
    def __init__(self, items):
        self.items, self.cuts = items, None
        self.join()

    def join(self):
        self.order = self.items[0].order
        if self.order:
            self.out = jnp.concatenate([s.out for s in self.items], axis=-1)

    def load(self):
        for s in self.items:
            if not s.loaded:
                s.load()
        self.join()

    def go(self):
        bit = self.order[0]
        self.got = lax.ppermute(self.out, "dp", pair(self.items[0].size, bit))
        for s in self.items:
            s.order.pop(0)
            s.loaded = False
        return self

    def take(self):
        at = 0
        for s in self.items:
            s.parts = s.parts + [(self.got, list(s.bits), at)]
            at += s.columns
        return self


def load_body(*refs):
    count = (len(refs) - 1) // 2
    sems = refs[-1]
    copies = [
        pltpu.make_async_copy(source, target, sems.at[i])
        for i, (source, target) in enumerate(zip(refs[:count], refs[count : 2 * count]))
    ]
    for copy in copies:
        copy.start()
    for copy in copies:
        copy.wait()


def load_weights(weights):
    return pl.pallas_call(
        load_body,
        in_specs=[pl.BlockSpec(memory_space=pl.ANY)] * len(weights),
        out_specs=[pl.BlockSpec(memory_space=pltpu.VMEM)] * len(weights),
        out_shape=[pltpu.VMEM(w.shape, w.dtype) for w in weights],
        scratch_shapes=[pltpu.SemaphoreType.DMA((len(weights),))],
        compiler_params=pltpu.CompilerParams(vmem_limit_bytes=VMEM_BESIDE),
        name="load_weights",
    )(*weights)


def angle_tables(lengths, head_index, rows):
    ids = head_index * rows + jnp.arange(rows, dtype=jnp.int32)
    begin = jnp.zeros_like(ids)
    end = jnp.int32(0)
    for s in range(lengths.shape[0]):
        end = end + lengths[s]
        begin = jnp.where(ids >= end, end, begin)
    frequency = np.power(ROPE_BASE, -2.0 * np.arange(HD // 2) / HD).astype(np.float32)
    grid = (ids - begin).astype(F32)[:, None] * frequency[None, :]
    return jnp.cos(grid), jnp.sin(grid)


def on_device(
    layer_input,
    seq_lengths,
    input_gain,
    query_weight,
    key_weight,
    value_weight,
    query_gain,
    key_gain,
    output_weight,
    post_attn_gain,
    pre_ffn_gain,
    gate_weight,
    up_weight,
    down_weight,
    post_ffn_gain,
    out_cotangent,
):
    rows = layer_input.shape[0]
    dp_size = lax.axis_size("dp")
    bit_count = dp_size.bit_length() - 1
    dp_index = lax.axis_index("dp")
    head_index = lax.axis_index("head")
    core = dp_index & 1
    core_pairs = pair(dp_size, 0)
    width = query_weight.shape[1]
    in_gain, q_gain, k_gain, post_gain, pre_gain, end_gain = (
        g.reshape(1, -1)
        for g in (input_gain, query_gain, key_gain, post_attn_gain, pre_ffn_gain, post_ffn_gain)
    )

    query_mine = lax.dynamic_slice_in_dim(query_weight, core * HD, HD, axis=1)
    output_mine = lax.dynamic_slice_in_dim(output_weight, core * HD, HD, axis=1)
    query_mine, output_mine, layer_input, seq_lengths = tie(
        query_mine, output_mine, layer_input, seq_lengths
    )
    query_first = swap_head(query_mine)

    cosine, sine = angle_tables(seq_lengths[0], head_index, rows)
    meta = jnp.concatenate([head_index.reshape(1).astype(jnp.int32), seq_lengths[0]])
    xn, kv_own, k_raw = project_keys(
        layer_input, in_gain, key_weight, value_weight, k_gain, cosine, sine
    )
    kv_before = lax.ppermute(kv_own, "head", [(0, 1)])
    query_first, kv_own, *weights = tie(
        query_first, kv_own, gate_weight, up_weight, down_weight
    )
    query_second = lax.ppermute(query_first, "dp", core_pairs)
    weights = load_weights(weights)
    xn_in, kv_before, output_mine, *weights = tie(xn, kv_before, output_mine, *weights)
    output_first = swap_head(output_mine)
    weights = [pltpu.with_memory_space_constraint(w, pltpu.VMEM) for w in weights]
    query_w = (query_weight, query_first, query_second)

    q_low, q_raw = project_queries(xn_in, query_w, q_gain, cosine, sine)
    attn_out, probs = attend(meta, q_low, kv_before, kv_own)
    attn_out, output_first = tie(attn_out, output_first)
    output_second = lax.ppermute(output_first, "dp", core_pairs)
    output_w = (output_weight, output_first, output_second)
    attn_proj, state, *z_own = merge_heads(attn_out, output_w, layer_input, post_gain, pre_gain)

    half = rows // 2
    total = 2 * rows
    z_other = [swap_head(z) for z in z_own]
    *kept, f_own0 = ffn_forward(z_own[0], 0, half, weights, 0, total, None, F32)
    z_in, f_own0 = tie(z_other[0], f_own0)
    *kept, f_send0 = ffn_forward(z_in, 0, half, weights, 2, total, kept, LOW)
    z_in, f_send0 = tie(z_other[1], f_send0)
    *kept, f_send1 = ffn_forward(z_in, 0, half, weights, 3, total, kept, LOW)
    f_got0 = swap_head(f_send0)
    z_in, f_send1 = tie(z_own[1], f_send1)
    f_got1 = swap_head(f_send1)
    *kept, f_own1 = ffn_forward(z_in, 0, half, weights, 1, total, kept, F32)
    hid, act, slope = kept
    f_got0, f_own0, f_own1 = tie(f_got0, f_own0, f_own1)
    layer_output, df_own0, end_grad0 = ffn_end(
        f_own0, f_got0, state, out_cotangent, end_gain, 0, None
    )
    df_other0 = swap_head(df_own0)
    layer_output, df_own1, end_grad1 = ffn_end(
        f_own1, f_got1, state, out_cotangent, end_gain, 1, layer_output
    )
    df_other1 = swap_head(df_own1)
    df_own = [df_own0, df_own1]
    *made, own_zgrad = ffn_backward(df_own, act, slope, weights, 0, None, LOW, 1, True)
    df_other0, df_other1, own_zgrad = tie(df_other0, df_other1, own_zgrad)
    df_other = [df_other0, df_other1]
    units = hid.shape[1]
    order = list(range(bit_count))
    rest = order[1:]
    leading = rest[::-1]
    third = units // 3

    def start(pairs, first, last, route=order, **options):
        send, keep = weight_grad(pairs, core, dp_size, first, last, **options)
        columns = last - first
        return Scatter(
            dp_size, dp_index, route, order[::-1], [(keep, leading, 0)], columns, send
        )

    def cut(whole, at, columns, route=rest):
        parts = [(p, own, at) for p, own, _ in whole.parts]
        return Scatter(dp_size, dp_index, route, leading, parts, columns)

    def later(value, scatter):
        tied = tie(*[p for p, _, _ in scatter.parts], value)
        scatter.parts = [(p, own, at) for p, (_, own, at) in zip(tied, scatter.parts)]

    def phase(values, end=(), go=(), now=(), hold=()):
        count = len(values)
        done = list(end) + list(now) + list(hold)
        tied = list(tie(*values, *[s.got for s in done], *[s.out for s in go]))
        for s in go[::-1]:
            s.out = tied.pop()
        for s in done[::-1]:
            s.got = tied.pop()
            s.take()
        for s in go:
            s.go()
        for s in list(now) + [s for s in end if s.cuts is None]:
            s.load()
        if now:
            tied = list(tie(*tied, *[s.out for s in now]))
            for s in now[::-1]:
                s.out = tied.pop()
                s.go()
        return tied

    df_all = df_own + df_other
    down_a = start([(df_all, hid)], 0, 2 * third, vmem=VMEM_BESIDE)
    (hid,) = phase([hid], go=[down_a])
    down_b = start([(df_all, hid)], 2 * third, units, vmem=VMEM_BESIDE)
    down_a.cuts = down_b.cuts = 1
    (df_other0,) = phase([df_other0], end=[down_a], go=[down_b])
    d1 = cut(down_a, 0, 2 * third)
    (df_other0,) = phase([df_other0], go=[d1])
    *made, dz0, dz1 = ffn_backward(
        [df_other0, df_other1],
        act,
        slope,
        (gate_weight, up_weight, down_weight),
        1,
        made,
        LOW,
        2,
        False,
    )
    dgate, dup = made
    dz0, dz1, dgate = phase([dz0, dz1, dgate], end=[down_b, d1])
    d2 = cut(down_b, 0, third)
    dz0, dz1, dgate = phase([dz0, dz1, dgate], go=[d2])
    other0 = swap_head(dz0)
    z_both = z_own + z_other
    gate_s = start([(z_both, dgate)], 0, units)
    other0, dz1, dup = phase([other0, dz1, dup], end=[d2], go=[gate_s, d1])
    other1 = swap_head(dz1)
    up_s = start([(z_both, dup)], 0, units)
    gate_s.cuts = up_s.cuts = 1
    own_zgrad, other0, other1 = phase(
        [own_zgrad, other0, other1], end=[gate_s], go=[up_s, d2], hold=[d1]
    )
    g1 = cut(gate_s, 0, 2 * third)
    (own_zgrad,) = phase([own_zgrad], go=[g1])
    other_zgrad = [other0, other1]

    state_grad, attn_grad, heads_grad, pre_grad, post_grad = state_back(
        own_zgrad, other_zgrad, state, attn_proj, out_cotangent, pre_gain, post_gain, output_w
    )

    own_heads = width // HD

    def head_block(j, c):
        return jnp.where(j < own_heads, j, own_heads + ((j - own_heads) ^ c))

    def start_heads(left, right):
        route = [order[0], "head"] + rest
        return start([([left], right)], 0, 2 * width, route, tile=HD, columns_of=head_block)

    dq, kv_back_send, kv_grad, q_gain_grad = attend_back(
        probs, heads_grad, q_low, q_raw, kv_before, kv_own, q_gain, cosine, sine
    )
    attn_grad, dq = tie(attn_grad, dq)
    output_s = start_heads(attn_grad, attn_out)
    later(output_s.out, gate_s)
    later(output_s.out, d1)
    d1.load()
    g2 = cut(gate_s, 2 * third, third)
    dq, kv_back_send = phase(
        [dq, kv_back_send], end=[up_s, g1, d2], go=[g2, output_s, d1]
    )
    kv_back = lax.ppermute(kv_back_send, "head", [(1, 0)])
    query_s = start_heads(xn, dq)
    later(query_s.out, up_s)
    u1 = cut(up_s, 0, 2 * third)
    dq, kv_grad, kv_back = phase(
        [dq, kv_grad, kv_back], end=[g2, d1], go=[query_s, u1, g1, d2], now=[output_s]
    )
    input_grad, dkv, k_gain_grad, in_gain_grad = input_back(
        dq, kv_grad, kv_back, k_raw, cosine, sine, layer_input, state_grad, k_gain, in_gain,
        query_w + (key_weight, value_weight),
    )
    kv_s = start([([xn], dkv)], 0, 2 * HD)
    later(kv_s.out, up_s)
    u2 = cut(up_s, 2 * third, third)
    (wait,) = phase(
        [in_gain_grad], end=[u1, d2, output_s], go=[u2, kv_s], now=[query_s, g1]
    )
    middle = Joint([g2, u1])
    (wait,) = phase([wait], go=[middle])
    gains = [wait, post_grad, pre_grad, end_grad0 + end_grad1, q_gain_grad, k_gain_grad]
    gains = [g.reshape(dp_size, -1) for g in gains]
    widths = [g.shape[1] for g in gains]
    block = layer_input.shape[1] // dp_size
    packed = jnp.concatenate(gains, axis=1)
    packed = jnp.pad(packed, ((0, 0), (0, block * 64 - packed.shape[1])))
    packed = packed.reshape(dp_size // 2, block, 128).astype(LOW)
    gains_s = Scatter(dp_size, dp_index, rest, leading, [(packed, leading, 0)], 128)
    wait, query_s.got, kv_s.got, u2.got, gains_s.out = tie(
        wait, query_s.got, kv_s.got, u2.got, gains_s.out
    )
    for s in (query_s, kv_s, u2):
        s.take().load()
    tail = Joint([output_s, query_s, kv_s, gains_s])
    (wait,) = phase([wait], end=[g1], go=[tail, u2], now=[middle])
    (wait,) = phase([wait], end=[middle], now=[tail, u2])
    (wait,) = phase([wait], end=[u2], now=[tail])
    (wait,) = phase([wait], end=[tail])
    down_part = jnp.concatenate([d1.finish(), d2.finish()], axis=1)
    gate_part = jnp.concatenate([g1.finish(), g2.finish()], axis=1)
    up_part = jnp.concatenate([u1.finish(), u2.finish()], axis=1)
    output_part = output_s.finish()
    query_part = query_s.finish()
    packed = gains_s.finish()
    pick = lambda which: lax.dynamic_slice_in_dim(packed, which * (block // 2), block // 2, axis=0)
    packed = pick(core) + lax.ppermute(pick(1 - core), "dp", core_pairs)
    packed = jnp.pad(packed, ((0, block - block // 2), (0, 0)))
    kv_sum = jnp.concatenate([kv_s.finish(), packed], axis=1)
    kv_sum = kv_sum + swap_head(kv_sum.astype(LOW)).astype(F32)
    packed = kv_sum[:, 2 * HD :].reshape(-1)
    pieces = []
    at = 0
    for size in widths:
        pieces.append(packed[at : at + size])
        at += size
    return (
        layer_output,
        input_grad,
        pieces[0],
        query_part,
        kv_sum[:, :HD],
        kv_sum[:, HD : 2 * HD],
        pieces[4],
        pieces[5],
        output_part,
        pieces[1],
        pieces[2],
        gate_part,
        up_part,
        down_part,
        pieces[3],
    )


def solution(mesh):
    placed = (
        P(("dp", "head"), None),
        P("dp", None),
        P(),
        P(None, "head"),
        P(),
        P(),
        P(),
        P(),
        P(None, "head"),
        P(),
        P(),
        P(None, "head"),
        P(None, "head"),
        P(None, "head"),
        P(),
        P(("dp", "head"), None),
    )
    return jax.shard_map(
        on_device,
        mesh=mesh,
        in_specs=placed,
        out_specs=(
            P(("dp", "head"), None),
            P(("dp", "head"), None),
            P("dp"),
            P("dp", "head"),
            P("dp", None),
            P("dp", None),
            P("dp"),
            P("dp"),
            P("dp", "head"),
            P("dp"),
            P("dp"),
            P("dp", "head"),
            P("dp", "head"),
            P("dp", "head"),
            P("dp"),
        ),
        check_vma=False,
    )
```

```python
import jax
import jax.numpy as jnp
import numpy as np
from jax import lax
from jax.experimental import pallas as pl
from jax.experimental.pallas import tpu as pltpu
from jax.sharding import PartitionSpec as P

HD = 256
EPSILON = 1e-06
ROPE_BASE = 1000000.0
NEG_FILL = -1e30
LOW = jnp.bfloat16
F32 = jnp.float32
ROOT = 0.7978845608028654
CUBIC = 0.044715
SCALE = HD ** (-0.5)
VMEM_BESIDE = 30 << 20
VMEM_BYTES = 60 << 20


def shape(*dims, dtype=LOW):
    return jax.ShapeDtypeStruct(dims, dtype)


def contract(left, right, dims):
    return lax.dot_general(left, right, (dims, ((), ())), preferred_element_type=F32)


def rms_scale(values):
    return lax.rsqrt(jnp.mean(values * values, axis=-1, keepdims=True) + EPSILON)


def rms_back(values, gain, cotangent):
    scale = rms_scale(values)
    unit = values * scale
    scaled = cotangent * (1.0 + gain)
    back = scale * (scaled - unit * jnp.mean(scaled * unit, axis=-1, keepdims=True))
    return back, jnp.sum(cotangent * unit, axis=0, keepdims=True)


def turn(values, cosine, sine):
    half = HD // 2
    first, second = values[:, :half], values[:, half:]
    return jnp.concatenate([first * cosine - second * sine, second * cosine + first * sine], axis=1)


def turn_back(values, cosine, sine):
    return turn(values, cosine, -sine)


def add_to(ref, value, first):
    @pl.when(first)
    def _():
        ref[...] = value

    @pl.when(jnp.logical_not(first))
    def _():
        ref[...] += value


def run(body, name, grid, inputs, outputs, scratch=(), scalars=(), aliases=None, flops=0, vmem=VMEM_BESIDE, hbm=True):
    def spec(array, block):
        if block is None:
            dims = tuple(array.shape)
            return pl.BlockSpec(dims, lambda *_: (0,) * len(dims))
        if block == "any":
            return pl.BlockSpec(memory_space=pl.ANY)
        if block == "vmem":
            return pl.BlockSpec(memory_space=pltpu.VMEM)
        return pl.BlockSpec(*block)

    arrays = [a for a, _ in inputs]
    out_shape = [o for o, _ in outputs]
    if hbm:
        arrays = [
            a if b == "vmem" else pltpu.with_memory_space_constraint(a, pltpu.HBM)
            for a, b in inputs
        ]
    moved = sum(a.size * a.dtype.itemsize for a, _ in inputs)
    moved += sum(int(np.prod(o.shape)) * o.dtype.itemsize for o in out_shape)
    return pl.pallas_call(
        body,
        grid_spec=pltpu.PrefetchScalarGridSpec(
            num_scalar_prefetch=len(scalars),
            grid=grid,
            in_specs=[spec(a, b) for a, b in inputs],
            out_specs=[spec(o, b) for o, b in outputs],
            scratch_shapes=list(scratch),
        ),
        out_shape=[pltpu.HBM(o.shape, o.dtype) for o in out_shape] if hbm else out_shape,
        input_output_aliases={} if aliases is None else aliases,
        compiler_params=pltpu.CompilerParams(vmem_limit_bytes=vmem),
        cost_estimate=pl.CostEstimate(flops=flops, transcendentals=0, bytes_accessed=moved),
        name=name,
    )(*scalars, *arrays)


def column_tile(units):
    for tile in (1152, 1024, 768, 512, 384, 256, 128):
        if units % tile == 0:
            return tile
    return units


def row_tile(rows, most):
    tile = most
    while rows % tile:
        tile //= 2
    return tile


def keys_body(x, gain, key_w, value_w, key_gain, cosine, sine, xn_out, kv_out, raw_out):
    values = x[...].astype(F32)
    xn = (values * rms_scale(values) * (1.0 + gain[...])).astype(LOW)
    xn_out[...] = xn
    raw = contract(xn, key_w[...], ((1,), (0,)))
    raw_out[...] = raw
    unit = raw * rms_scale(raw) * (1.0 + key_gain[...])
    kv_out[:, :HD] = turn(unit, cosine[...], sine[...]).astype(LOW)
    kv_out[:, HD:] = contract(xn, value_w[...], ((1,), (0,))).astype(LOW)


def project_keys(x, gain, key_w, value_w, key_gain, cosine, sine):
    rows, dim = x.shape
    tile = row_tile(rows, 256)
    by_row = lambda width: ((tile, width), lambda i: (i, 0))
    return run(
        keys_body,
        "project_keys",
        (rows // tile,),
        [
            (x, by_row(dim)),
            (gain, None),
            (key_w, None),
            (value_w, None),
            (key_gain, None),
            (cosine, by_row(HD // 2)),
            (sine, by_row(HD // 2)),
        ],
        [
            (shape(rows, dim), by_row(dim)),
            (shape(rows, 2 * HD), by_row(2 * HD)),
            (shape(rows, HD, dtype=F32), by_row(HD)),
        ],
        flops=4 * rows * dim * HD,
    )


def queries_body(xn, own_w, first_w, second_w, gain, cosine, sine, q_out, raw_out):
    values = xn[...]
    start = 0
    for weight in (own_w, first_w, second_w):
        raw_all = contract(values, weight[...], ((1,), (0,)))
        for at in range(0, weight.shape[1], HD):
            raw = raw_all[:, at : at + HD]
            unit = raw * rms_scale(raw) * (1.0 + gain[...])
            raw_out[:, start : start + HD] = raw
            q_out[:, start : start + HD] = turn(unit, cosine[...], sine[...]).astype(LOW)
            start += HD


def project_queries(xn, heads_w, gain, cosine, sine):
    rows, dim = xn.shape
    width = sum(w.shape[1] for w in heads_w)
    tile = row_tile(rows, 256)
    by_row = lambda size: ((tile, size), lambda i: (i, 0))
    return run(
        queries_body,
        "project_queries",
        (rows // tile,),
        [(xn, by_row(dim))]
        + [(w, None) for w in heads_w]
        + [(gain, None), (cosine, by_row(HD // 2)), (sine, by_row(HD // 2))],
        [(shape(rows, width), by_row(width)), (shape(rows, width, dtype=F32), by_row(width))],
        flops=2 * rows * dim * width,
    )


def attend_body(slots, meta, q, before, own, o_out, p_out, bias):
    block, keys = bias.shape
    rows = keys // 2

    @pl.when(pl.program_id(1) == 0)
    def _():
        second = meta[0]
        first_row = second * rows + pl.program_id(0) * block
        query = first_row + lax.broadcasted_iota(jnp.int32, (block, keys), 0)
        column = lax.broadcasted_iota(jnp.int32, (block, keys), 1)
        is_own = column >= rows
        key = jnp.where(is_own, column + (second - 1) * rows, column)
        ends = jnp.int32(0)
        query_segment = jnp.zeros((block, keys), jnp.int32)
        key_segment = jnp.zeros((block, keys), jnp.int32)
        for s in range(slots):
            ends = ends + meta[1 + s]
            query_segment += (query >= ends).astype(jnp.int32)
            key_segment += (key >= ends).astype(jnp.int32)
        known = is_own | (column < second * rows)
        seen = (key < query) & (query_segment == key_segment) & (query_segment < slots) & known
        seen = seen | (is_own & (key == query))
        bias[...] = jnp.where(seen, 0.0, NEG_FILL)

    scaled = q[...] * LOW(SCALE)
    scores = jnp.concatenate(
        [
            contract(scaled, before[:, :HD], ((1,), (1,))),
            contract(scaled, own[:, :HD], ((1,), (1,))),
        ],
        axis=1,
    )
    scores = scores + bias[...]
    exps = jnp.exp(scores - jnp.max(scores, axis=1, keepdims=True))
    probs = (exps * (1.0 / jnp.sum(exps, axis=1, keepdims=True))).astype(LOW)
    p_out[...] = probs
    out = contract(probs[:, :rows], before[:, HD:], ((1,), (0,)))
    out += contract(probs[:, rows:], own[:, HD:], ((1,), (0,)))
    o_out[...] = out.astype(LOW)


def attend(meta, q, before, own):
    rows, width = q.shape
    heads = width // HD
    block = row_tile(rows, 512)
    blocks = rows // block
    slots = meta.shape[0] - 1
    head_block = ((block, HD), lambda i, h, m: (i, h))
    return run(
        lambda *refs: attend_body(slots, *refs),
        "attend",
        (blocks, heads),
        [(q, head_block), (before, None), (own, None)],
        [
            (shape(rows, width), head_block),
            (shape(heads * rows, 2 * rows), ((block, 2 * rows), lambda i, h, m: (h * blocks + i, 0))),
        ],
        scratch=[pltpu.VMEM((block, 2 * rows), F32)],
        scalars=[meta],
        flops=8 * rows * rows * width,
    )


def merge_body(o, own_w, first_w, second_w, x, post_gain, pre_gain, a_out, state_out, first_out, second_out):
    start = 0
    total = None
    for weight in (own_w, first_w, second_w):
        width = weight.shape[1]
        part = contract(o[:, start : start + width], weight[...], ((1,), (1,)))
        total = part if total is None else total + part
        start += width
    a_out[...] = total.astype(a_out.dtype)
    state = x[...].astype(F32) + total * rms_scale(total) * (1.0 + post_gain[...])
    state_out[...] = state.astype(state_out.dtype)
    z = (state * rms_scale(state) * (1.0 + pre_gain[...])).astype(LOW)
    early = pl.program_id(0) < pl.num_programs(0) // 2

    @pl.when(early)
    def _():
        first_out[...] = z

    @pl.when(jnp.logical_not(early))
    def _():
        second_out[...] = z


def merge_heads(o, heads_w, x, post_gain, pre_gain):
    rows, dim = x.shape
    width = o.shape[1]
    tile = row_tile(rows, 256)
    by_row = lambda size: ((tile, size), lambda i: (i, 0))
    half = rows // tile // 2
    return run(
        merge_body,
        "merge_heads",
        (rows // tile,),
        [(o, by_row(width))]
        + [(w, None) for w in heads_w]
        + [(x, by_row(dim)), (post_gain, None), (pre_gain, None)],
        [
            (shape(rows, dim), by_row(dim)),
            (shape(rows, dim), by_row(dim)),
            (shape(rows // 2, dim), ((tile, dim), lambda i: (jnp.minimum(i, half - 1), 0))),
            (shape(rows // 2, dim), ((tile, dim), lambda i: (jnp.maximum(i - half, 0), 0))),
        ],
        flops=2 * rows * dim * width,
    )


def ffn_forward_body(z, gate_w, up_w, down_w, *rest):
    hid_out, act_out, slope_out, f_out, acc = rest[-5:]
    step, last = pl.program_id(0), pl.num_programs(0) - 1
    tile = hid_out.shape[1]
    here = pl.ds(pl.multiple_of(step * tile, 128), tile)
    gate = contract(z[...], gate_w[:, here], ((1,), (0,)))
    up = contract(z[...], up_w[:, here], ((1,), (0,)))
    square = gate * gate
    tanh = jnp.tanh(ROOT * gate * (1.0 + CUBIC * square))
    half = 0.5 * (1.0 + tanh)
    act = gate * half
    slope = half + 0.5 * gate * (1.0 - tanh * tanh) * (ROOT * (1.0 + 3.0 * CUBIC * square))
    hid = (act * up).astype(LOW)
    hid_out[...] = hid
    act_out[...] = act.astype(LOW)
    slope_out[...] = (slope * up).astype(LOW)
    add_to(acc, contract(hid, down_w[:, here], ((1,), (1,))), step == 0)

    @pl.when(step == last)
    def _():
        f_out[...] = acc[...].astype(f_out.dtype)


def ffn_forward(z, z_block, rows, weights, block, total, kept, out_dtype):
    dim, units = weights[0].shape
    tile = column_tile(units)
    inner = ((rows, tile), lambda j: (block, j))
    extra = [] if kept is None else list(kept)
    return run(
        ffn_forward_body,
        "ffn_forward",
        (units // tile,),
        [(z, ((rows, dim), lambda j: (z_block, 0)))]
        + [(w, "vmem") for w in weights]
        + [(k, "any") for k in extra],
        [(shape(total, units), inner)] * 3 + [(shape(rows, dim, dtype=out_dtype), None)],
        scratch=[pltpu.VMEM((rows, dim), F32)],
        aliases={4 + i: i for i in range(len(extra))},
        hbm=False,
        flops=6 * rows * dim * units,
    )


def ffn_end_body(f_own, f_other, state, cotangent, gain, *rest):
    out, df_out, gain_out = rest[-3:]
    f = f_own[...] + f_other[...].astype(F32)
    out[...] = (state[...].astype(F32) + f * rms_scale(f) * (1.0 + gain[...])).astype(LOW)
    df, gain_grad = rms_back(f, gain[...], cotangent[...].astype(F32))
    df_out[...] = df.astype(LOW)
    add_to(gain_out, gain_grad, pl.program_id(0) == 0)


def ffn_end(f_own, f_other, state, cotangent, gain, chunk, out):
    rows, dim = f_own.shape
    tile = row_tile(rows, 128)
    steps = rows // tile
    here = ((tile, dim), lambda i: (i, 0))
    there = ((tile, dim), lambda i: (chunk * steps + i, 0))
    extra = [] if out is None else [out]
    return run(
        ffn_end_body,
        "ffn_end",
        (steps,),
        [(f_own, here), (f_other, here), (state, there), (cotangent, there), (gain, None)]
        + [(e, "any") for e in extra],
        [(shape(*state.shape), there), (shape(rows, dim), here), (shape(1, dim, dtype=F32), None)],
        hbm=False,
        aliases={5: 0} if extra else None,
    )


def ffn_backward_body(pieces, splits, *refs):
    dfs = refs[:pieces]
    act, slope, gate_w, up_w, down_w = refs[pieces : pieces + 5]
    *outs, acc, df = refs[pieces + 5 :]
    dgate_out, dup_out, *dz_outs = outs[-2 - splits :]
    step, last = pl.program_id(0), pl.num_programs(0) - 1

    @pl.when(step == 0)
    def _():
        at = 0
        for piece in dfs:
            df[at : at + piece.shape[0]] = piece[...]
            at += piece.shape[0]

    tile = dup_out.shape[1]
    if gate_w.shape[1] == tile:
        here = slice(None)
    else:
        here = pl.ds(pl.multiple_of(step * tile, 128), tile)
    dhid = contract(df[...], down_w[:, here], ((1,), (0,)))
    dup = (dhid * act[...].astype(F32)).astype(LOW)
    dgate = (dhid * slope[...].astype(F32)).astype(LOW)
    dup_out[...] = dup
    dgate_out[...] = dgate
    part = contract(dgate, gate_w[:, here], ((1,), (1,)))
    part += contract(dup, up_w[:, here], ((1,), (1,)))
    add_to(acc, part, step == 0)

    @pl.when(step == last)
    def _():
        at = 0
        for dz_out in dz_outs:
            size = dz_out.shape[0]
            dz_out[...] = acc[at : at + size].astype(dz_out.dtype)
            at += size


def ffn_backward(dfs, act, slope, weights, block, made, out_dtype, splits, resident):
    rows = sum(d.shape[0] for d in dfs)
    total, units = act.shape
    dim = dfs[0].shape[1]
    tile = column_tile(units)
    inner = ((rows, tile), lambda j: (block, j))
    weight = "vmem" if resident else ((dim, tile), lambda j: (0, j))
    extra = [] if made is None else list(made)
    return run(
        lambda *refs: ffn_backward_body(len(dfs), splits, *refs),
        "ffn_backward",
        (units // tile,),
        [(d, None) for d in dfs]
        + [(act, inner), (slope, inner)]
        + [(w, weight) for w in weights]
        + [(e, "any") for e in extra],
        [(shape(total, units), inner)] * 2
        + [(shape(rows // splits, dim, dtype=out_dtype), None)] * splits,
        scratch=[pltpu.VMEM((rows, dim), F32), pltpu.VMEM((rows, dim), LOW)],
        aliases={len(dfs) + 5 + i: i for i in range(len(extra))},
        flops=6 * rows * dim * units,
        vmem=VMEM_BESIDE if resident else VMEM_BYTES,
    )


def weight_grad_body(sides, core, *refs):
    *inputs, send, keep = refs
    groups, rows, _ = keep.shape
    first = core[0] == 0

    def write(lefts, right):
        at = 0
        total = None
        for left in lefts:
            size = left.shape[0]
            part = contract(left[...], right[at : at + size], ((0,), (0,)))
            total = part if total is None else total + part
            at += size
        for i in range(groups):
            even = total[2 * i * rows : (2 * i + 1) * rows].astype(LOW)
            odd = total[(2 * i + 1) * rows : (2 * i + 2) * rows].astype(LOW)
            send[i] = jnp.where(first, odd, even)
            keep[i] = jnp.where(first, even, odd)

    at = 0
    for side, count in enumerate(sides):
        lefts, right = inputs[at : at + count], inputs[at + count]
        at += count + 1
        if len(sides) == 1:
            write(lefts, right)
        else:
            mine = (pl.program_id(0) % len(sides)) == side
            pl.when(mine)(lambda lefts=lefts, right=right: write(lefts, right))


def weight_grad(
    pairs, core, axis_size, start, stop, tile=None, columns_of=None, vmem=VMEM_BYTES
):
    dim = pairs[0][0][0].shape[1]
    columns = stop - start
    rows = dim // axis_size
    groups = axis_size // 2
    tile = column_tile(columns) if tile is None else tile
    blocks = columns // tile
    if columns_of is None:
        columns_of = lambda j, c: j + start // tile
    if rows % 8:
        full = []
        for j in range(blocks):
            lefts, right = pairs[j % len(pairs)]
            left = jnp.concatenate(lefts, axis=0)
            at = columns_of(j, core) * tile
            here = lax.dynamic_slice_in_dim(right, at, tile, axis=1)
            full.append(contract(left, here, ((0,), (0,))).astype(LOW))
        full = jnp.concatenate(full, axis=1).reshape(groups, 2, rows, columns)
        return (
            lax.dynamic_index_in_dim(full, 1 - core, axis=1, keepdims=False),
            lax.dynamic_index_in_dim(full, core, axis=1, keepdims=False),
        )
    inputs = []
    for lefts, right in pairs:
        inputs += [(left, None) for left in lefts]
        inputs.append((right, ((right.shape[0], tile), lambda j, c: (0, columns_of(j, c[0])))))
    out = (shape(groups, rows, columns), ((groups, rows, tile), lambda j, c: (0, 0, j)))
    sides = [len(lefts) for lefts, _ in pairs]
    return run(
        lambda *refs: weight_grad_body(sides, *refs),
        "weight_grad",
        (blocks,),
        inputs,
        [out, out],
        scalars=[core.reshape(1)],
        flops=2 * pairs[0][1].shape[0] * dim * columns,
        vmem=vmem,
    )


def state_back_body(
    dz_own, dz_first, dz_second, state, a, cotangent, pre_gain, post_gain, own_w, first_w, second_w,
    dh_out, da_out, do_out, pre_out, post_out,
):
    first = pl.program_id(0) == 0
    early = pl.program_id(0) < pl.num_programs(0) // 2
    dz = dz_own[...].astype(F32) + jnp.where(early, dz_first[...], dz_second[...]).astype(F32)
    back, pre_grad = rms_back(state[...].astype(F32), pre_gain[...], dz)
    dh = cotangent[...].astype(F32) + back
    dh_out[...] = dh.astype(dh_out.dtype)
    da, post_grad = rms_back(a[...].astype(F32), post_gain[...], dh)
    da = da.astype(LOW)
    da_out[...] = da
    add_to(pre_out, pre_grad, first)
    add_to(post_out, post_grad, first)
    at = 0
    for weight in (own_w, first_w, second_w):
        width = weight.shape[1]
        do_out[:, at : at + width] = contract(da, weight[...], ((1,), (0,))).astype(LOW)
        at += width


def state_back(dz_own, dz_other, state, a, cotangent, pre_gain, post_gain, heads_w):
    rows, dim = state.shape
    width = sum(w.shape[1] for w in heads_w)
    tile = row_tile(rows, 256)
    steps = rows // tile
    by_row = lambda size: ((tile, size), lambda i: (i, 0))
    return run(
        state_back_body,
        "state_back",
        (rows // tile,),
        [
            (dz_own, by_row(dim)),
            (dz_other[0], ((tile, dim), lambda i: (jnp.minimum(i, steps // 2 - 1), 0))),
            (dz_other[1], ((tile, dim), lambda i: (jnp.maximum(i - steps // 2, 0), 0))),
        ]
        + [(v, by_row(dim)) for v in (state, a, cotangent)]
        + [(v, None) for v in (pre_gain, post_gain, *heads_w)],
        [
            (shape(rows, dim), by_row(dim)),
            (shape(rows, dim), by_row(dim)),
            (shape(rows, width), by_row(width)),
            (shape(1, dim, dtype=F32), None),
            (shape(1, dim, dtype=F32), None),
        ],
        vmem=VMEM_BYTES,
        flops=2 * rows * dim * width,
    )


def attend_back_body(
    p, do, q, raw, before, own, gain, cosine, sine, dq_out, before_out, own_out, gain_out, acc
):
    head, part = pl.program_id(0), pl.program_id(1)
    first = (head == 0) & (part == 0)
    last = (head == pl.num_programs(0) - 1) & (part == pl.num_programs(1) - 1)
    rows = before.shape[0]
    dp = jnp.concatenate(
        [
            contract(do[...], before[:, HD:], ((1,), (1,))),
            contract(do[...], own[:, HD:], ((1,), (1,))),
        ],
        axis=1,
    )
    probs = p[...].astype(F32)
    weighted = probs * dp
    ds = (weighted - probs * jnp.sum(weighted, axis=1, keepdims=True)).astype(LOW)
    dq = contract(ds[:, :rows], before[:, :HD], ((1,), (0,)))
    dq += contract(ds[:, rows:], own[:, :HD], ((1,), (0,)))
    dk = contract(ds, q[...], ((0,), (0,))) * SCALE
    dv = contract(p[...], do[...], ((0,), (0,)))
    add_to(acc, jnp.concatenate([dk, dv], axis=1), first)
    back = turn_back(dq * SCALE, cosine[...], sine[...])
    dq_raw, gain_grad = rms_back(raw[...], gain[...], back)
    dq_out[...] = dq_raw.astype(LOW)
    add_to(gain_out, gain_grad, first)

    @pl.when(last)
    def _():
        before_out[...] = acc[:rows].astype(LOW)
        own_out[...] = acc[rows:]


def attend_back(p, do, q, raw, before, own, gain, cosine, sine):
    rows, width = q.shape
    heads = width // HD
    block = row_tile(rows, 512)
    blocks = rows // block
    head_block = ((block, HD), lambda h, i: (i, h))
    table = ((block, HD // 2), lambda h, i: (i, 0))
    return run(
        attend_back_body,
        "attend_back",
        (heads, blocks),
        [
            (p, ((block, 2 * rows), lambda h, i: (h * blocks + i, 0))),
            (do, head_block),
            (q, head_block),
            (raw, head_block),
            (before, None),
            (own, None),
            (gain, None),
            (cosine, table),
            (sine, table),
        ],
        [
            (shape(rows, width), head_block),
            (shape(rows, 2 * HD), None),
            (shape(rows, 2 * HD, dtype=F32), None),
            (shape(1, HD, dtype=F32), None),
        ],
        scratch=[pltpu.VMEM((2 * rows, 2 * HD), F32)],
        vmem=VMEM_BYTES,
        flops=16 * rows * rows * width,
    )


def input_back_body(
    dq, dkv_own, dkv_other, raw, cosine, sine, x, dh, key_gain, in_gain,
    own_w, first_w, second_w, key_w, value_w,
    grad_out, dkv_out, key_gain_out, in_gain_out,
):
    first = pl.program_id(0) == 0
    dkv = dkv_own[...] + dkv_other[...].astype(F32)
    back = turn_back(dkv[:, :HD], cosine[...], sine[...])
    dk, key_grad = rms_back(raw[...], key_gain[...], back)
    dk = dk.astype(LOW)
    dv = dkv[:, HD:].astype(LOW)
    dkv_out[:, :HD] = dk
    dkv_out[:, HD:] = dv
    add_to(key_gain_out, key_grad, first)
    dxn = contract(dk, key_w[...], ((1,), (1,))) + contract(dv, value_w[...], ((1,), (1,)))
    at = 0
    for weight in (own_w, first_w, second_w):
        width = weight.shape[1]
        dxn += contract(dq[:, at : at + width], weight[...], ((1,), (1,)))
        at += width
    dx, in_grad = rms_back(x[...].astype(F32), in_gain[...], dxn)
    grad_out[...] = (dh[...].astype(F32) + dx).astype(LOW)
    add_to(in_gain_out, in_grad, first)


def input_back(dq, dkv_own, dkv_other, raw, cosine, sine, x, dh, key_gain, in_gain, weights):
    rows, dim = x.shape
    width = dq.shape[1]
    tile = row_tile(rows, 256)
    by_row = lambda size: ((tile, size), lambda i: (i, 0))
    return run(
        input_back_body,
        "input_back",
        (rows // tile,),
        [(v, by_row(v.shape[1])) for v in (dq, dkv_own, dkv_other, raw, cosine, sine, x, dh)]
        + [(v, None) for v in (key_gain, in_gain, *weights)],
        [
            (shape(rows, dim), by_row(dim)),
            (shape(rows, 2 * HD), by_row(2 * HD)),
            (shape(1, HD, dtype=F32), None),
            (shape(1, dim, dtype=F32), None),
        ],
        vmem=VMEM_BYTES,
        flops=2 * rows * dim * (width + 2 * HD),
    )


def swap_head(value):
    return lax.ppermute(value, "head", [(0, 1), (1, 0)])


def pair(axis_size, bit):
    return [(i, i ^ (1 << bit)) for i in range(axis_size)]


def tie(*values):
    return lax.optimization_barrier(values)


def sum_parts(parts, choice, columns, dtype):
    total = None
    for array, own, at in parts:
        rows = array.shape[-2]
        value = lax.dynamic_slice(
            array.reshape((2,) * len(own) + array.shape[-2:]),
            [choice.get(b, 0) for b in own] + [0, at],
            [1 if b in choice else 2 for b in own] + [rows, columns],
        )
        value = value.reshape((2,) * sum(b not in choice for b in own) + (rows, columns))
        value = value.astype(F32)
        total = value if total is None else total + value
    return total.astype(dtype)


class Scatter:
    def __init__(self, size, index, order, bits, parts, columns, out=None, low=LOW):
        self.size, self.index, self.order, self.low = size, index, list(order), low
        self.bits, self.parts, self.columns, self.out = list(bits), list(parts), columns, out
        self.gone, self.loaded, self.flying, self.cuts = [], out is not None, False, None
        if out is None:
            self.load()
        else:
            self.drop()

    def value(self, bit):
        return (self.index >> bit) & 1

    def drop(self):
        bit = self.order[0]
        if bit == "head":
            self.columns //= 2
        else:
            self.bits.remove(bit)
            self.gone.append(bit)

    def load(self):
        if not self.order:
            return
        bit = self.order[0]
        choice = {b: self.value(b) for b in self.gone}
        parts, columns = self.parts, self.columns
        if bit == "head":
            columns //= 2
            parts = [(p, own, at + columns) for p, own, at in parts]
        else:
            choice[bit] = 1 - self.value(bit)
        self.out = sum_parts(parts, choice, columns, self.low)
        self.loaded = True
        self.drop()

    def go(self):
        bit = self.order.pop(0)
        if bit == "head":
            self.got = swap_head(self.out)
        else:
            self.got = lax.ppermute(self.out, "dp", pair(self.size, bit))
        self.loaded, self.flying = False, True
        return self

    def take(self):
        self.parts = self.parts + [(self.got, list(self.bits), 0)]
        self.flying = False
        return self

    def land(self):
        self.take().load()
        return self

    def finish(self):
        if self.flying:
            self.take()
        while self.order:
            if not self.loaded:
                self.load()
            self.go().take()
        choice = {b: self.value(b) for b in self.gone}
        return sum_parts(self.parts, choice, self.columns, F32)


class Joint:
    def __init__(self, items):
        self.items, self.cuts = items, None
        self.join()

    def join(self):
        self.order = self.items[0].order
        if self.order:
            self.out = jnp.concatenate([s.out for s in self.items], axis=-1)

    def load(self):
        for s in self.items:
            if not s.loaded:
                s.load()
        self.join()

    def go(self):
        bit = self.order[0]
        self.got = lax.ppermute(self.out, "dp", pair(self.items[0].size, bit))
        for s in self.items:
            s.order.pop(0)
            s.loaded = False
        return self

    def take(self):
        at = 0
        for s in self.items:
            s.parts = s.parts + [(self.got, list(s.bits), at)]
            at += s.columns
        return self


def load_body(*refs):
    count = (len(refs) - 1) // 2
    sems = refs[-1]
    copies = [
        pltpu.make_async_copy(source, target, sems.at[i])
        for i, (source, target) in enumerate(zip(refs[:count], refs[count : 2 * count]))
    ]
    for copy in copies:
        copy.start()
    for copy in copies:
        copy.wait()


def load_weights(weights):
    return pl.pallas_call(
        load_body,
        in_specs=[pl.BlockSpec(memory_space=pl.ANY)] * len(weights),
        out_specs=[pl.BlockSpec(memory_space=pltpu.VMEM)] * len(weights),
        out_shape=[pltpu.VMEM(w.shape, w.dtype) for w in weights],
        scratch_shapes=[pltpu.SemaphoreType.DMA((len(weights),))],
        compiler_params=pltpu.CompilerParams(vmem_limit_bytes=VMEM_BESIDE),
        name="load_weights",
    )(*weights)


def angle_tables(lengths, head_index, rows):
    ids = head_index * rows + jnp.arange(rows, dtype=jnp.int32)
    begin = jnp.zeros_like(ids)
    end = jnp.int32(0)
    for s in range(lengths.shape[0]):
        end = end + lengths[s]
        begin = jnp.where(ids >= end, end, begin)
    frequency = np.power(ROPE_BASE, -2.0 * np.arange(HD // 2) / HD).astype(np.float32)
    grid = (ids - begin).astype(F32)[:, None] * frequency[None, :]
    return jnp.cos(grid), jnp.sin(grid)


def on_device(
    layer_input,
    seq_lengths,
    input_gain,
    query_weight,
    key_weight,
    value_weight,
    query_gain,
    key_gain,
    output_weight,
    post_attn_gain,
    pre_ffn_gain,
    gate_weight,
    up_weight,
    down_weight,
    post_ffn_gain,
    out_cotangent,
):
    rows = layer_input.shape[0]
    dp_size = lax.axis_size("dp")
    bit_count = dp_size.bit_length() - 1
    dp_index = lax.axis_index("dp")
    head_index = lax.axis_index("head")
    core = dp_index & 1
    core_pairs = pair(dp_size, 0)
    width = query_weight.shape[1]
    in_gain, q_gain, k_gain, post_gain, pre_gain, end_gain = (
        g.reshape(1, -1)
        for g in (input_gain, query_gain, key_gain, post_attn_gain, pre_ffn_gain, post_ffn_gain)
    )

    query_mine = lax.dynamic_slice_in_dim(query_weight, core * HD, HD, axis=1)
    output_mine = lax.dynamic_slice_in_dim(output_weight, core * HD, HD, axis=1)
    query_mine, output_mine, layer_input, seq_lengths = tie(
        query_mine, output_mine, layer_input, seq_lengths
    )
    query_first = swap_head(query_mine)

    cosine, sine = angle_tables(seq_lengths[0], head_index, rows)
    meta = jnp.concatenate([head_index.reshape(1).astype(jnp.int32), seq_lengths[0]])
    xn, kv_own, k_raw = project_keys(
        layer_input, in_gain, key_weight, value_weight, k_gain, cosine, sine
    )
    kv_before = lax.ppermute(kv_own, "head", [(0, 1)])
    query_first, kv_own, *weights = tie(
        query_first, kv_own, gate_weight, up_weight, down_weight
    )
    query_second = lax.ppermute(query_first, "dp", core_pairs)
    weights = load_weights(weights)
    xn_in, kv_before, output_mine, *weights = tie(xn, kv_before, output_mine, *weights)
    output_first = swap_head(output_mine)
    weights = [pltpu.with_memory_space_constraint(w, pltpu.VMEM) for w in weights]
    query_w = (query_weight, query_first, query_second)

    q_low, q_raw = project_queries(xn_in, query_w, q_gain, cosine, sine)
    attn_out, probs = attend(meta, q_low, kv_before, kv_own)
    attn_out, output_first = tie(attn_out, output_first)
    output_second = lax.ppermute(output_first, "dp", core_pairs)
    output_w = (output_weight, output_first, output_second)
    attn_proj, state, *z_own = merge_heads(attn_out, output_w, layer_input, post_gain, pre_gain)

    half = rows // 2
    total = 2 * rows
    z_other = [swap_head(z) for z in z_own]
    *kept, f_own0 = ffn_forward(z_own[0], 0, half, weights, 0, total, None, F32)
    z_in, f_own0 = tie(z_other[0], f_own0)
    *kept, f_send0 = ffn_forward(z_in, 0, half, weights, 2, total, kept, LOW)
    z_in, f_send0 = tie(z_other[1], f_send0)
    *kept, f_send1 = ffn_forward(z_in, 0, half, weights, 3, total, kept, LOW)
    f_got0 = swap_head(f_send0)
    z_in, f_send1 = tie(z_own[1], f_send1)
    f_got1 = swap_head(f_send1)
    *kept, f_own1 = ffn_forward(z_in, 0, half, weights, 1, total, kept, F32)
    hid, act, slope = kept
    f_got0, f_own0, f_own1 = tie(f_got0, f_own0, f_own1)
    layer_output, df_own0, end_grad0 = ffn_end(
        f_own0, f_got0, state, out_cotangent, end_gain, 0, None
    )
    df_other0 = swap_head(df_own0)
    layer_output, df_own1, end_grad1 = ffn_end(
        f_own1, f_got1, state, out_cotangent, end_gain, 1, layer_output
    )
    df_other1 = swap_head(df_own1)
    df_own = [df_own0, df_own1]
    *made, own_zgrad = ffn_backward(df_own, act, slope, weights, 0, None, LOW, 1, True)
    df_other0, df_other1, own_zgrad = tie(df_other0, df_other1, own_zgrad)
    df_other = [df_other0, df_other1]
    units = hid.shape[1]
    order = list(range(bit_count))
    rest = order[1:]
    leading = rest[::-1]
    third = units // 3

    def start(pairs, first, last, route=order, **options):
        send, keep = weight_grad(pairs, core, dp_size, first, last, **options)
        columns = last - first
        return Scatter(
            dp_size, dp_index, route, order[::-1], [(keep, leading, 0)], columns, send
        )

    def cut(whole, at, columns, route=rest):
        parts = [(p, own, at) for p, own, _ in whole.parts]
        return Scatter(dp_size, dp_index, route, leading, parts, columns)

    def later(value, scatter):
        tied = tie(*[p for p, _, _ in scatter.parts], value)
        scatter.parts = [(p, own, at) for p, (_, own, at) in zip(tied, scatter.parts)]

    def phase(values, end=(), go=(), now=(), hold=()):
        count = len(values)
        done = list(end) + list(now) + list(hold)
        tied = list(tie(*values, *[s.got for s in done], *[s.out for s in go]))
        for s in go[::-1]:
            s.out = tied.pop()
        for s in done[::-1]:
            s.got = tied.pop()
            s.take()
        for s in go:
            s.go()
        for s in list(now) + [s for s in end if s.cuts is None]:
            s.load()
        if now:
            tied = list(tie(*tied, *[s.out for s in now]))
            for s in now[::-1]:
                s.out = tied.pop()
                s.go()
        return tied

    df_all = df_own + df_other
    down_a = start([(df_all, hid)], 0, 2 * third, vmem=VMEM_BESIDE)
    (hid,) = phase([hid], go=[down_a])
    down_b = start([(df_all, hid)], 2 * third, units, vmem=VMEM_BESIDE)
    down_a.cuts = down_b.cuts = 1
    (df_other0,) = phase([df_other0], end=[down_a], go=[down_b])
    d1 = cut(down_a, 0, 2 * third)
    (df_other0,) = phase([df_other0], go=[d1])
    *made, dz0, dz1 = ffn_backward(
        [df_other0, df_other1],
        act,
        slope,
        (gate_weight, up_weight, down_weight),
        1,
        made,
        LOW,
        2,
        False,
    )
    dgate, dup = made
    dz0, dz1, dgate = phase([dz0, dz1, dgate], end=[down_b, d1])
    d2 = cut(down_b, 0, third)
    dz0, dz1, dgate = phase([dz0, dz1, dgate], go=[d2])
    other0 = swap_head(dz0)
    z_both = z_own + z_other
    gate_s = start([(z_both, dgate)], 0, units)
    other0, dz1, dup = phase([other0, dz1, dup], end=[d2], go=[gate_s, d1])
    other1 = swap_head(dz1)
    up_s = start([(z_both, dup)], 0, units)
    gate_s.cuts = up_s.cuts = 1
    own_zgrad, other0, other1 = phase(
        [own_zgrad, other0, other1], end=[gate_s], go=[up_s, d2], hold=[d1]
    )
    g1 = cut(gate_s, 0, 2 * third)
    (own_zgrad,) = phase([own_zgrad], go=[g1])
    other_zgrad = [other0, other1]

    state_grad, attn_grad, heads_grad, pre_grad, post_grad = state_back(
        own_zgrad, other_zgrad, state, attn_proj, out_cotangent, pre_gain, post_gain, output_w
    )

    own_heads = width // HD

    def head_block(j, c):
        return jnp.where(j < own_heads, j, own_heads + ((j - own_heads) ^ c))

    def start_heads(left, right):
        route = [order[0], "head"] + rest
        return start([([left], right)], 0, 2 * width, route, tile=HD, columns_of=head_block)

    dq, kv_back_send, kv_grad, q_gain_grad = attend_back(
        probs, heads_grad, q_low, q_raw, kv_before, kv_own, q_gain, cosine, sine
    )
    attn_grad, dq = tie(attn_grad, dq)
    output_s = start_heads(attn_grad, attn_out)
    later(output_s.out, gate_s)
    later(output_s.out, d1)
    d1.load()
    g2 = cut(gate_s, 2 * third, third)
    dq, kv_back_send = phase(
        [dq, kv_back_send], end=[up_s, g1, d2], go=[g2, output_s, d1]
    )
    kv_back = lax.ppermute(kv_back_send, "head", [(1, 0)])
    query_s = start_heads(xn, dq)
    later(query_s.out, up_s)
    u1 = cut(up_s, 0, 2 * third)
    dq, kv_grad, kv_back = phase(
        [dq, kv_grad, kv_back], end=[g2, d1], go=[query_s, u1, g1, d2], now=[output_s]
    )
    input_grad, dkv, k_gain_grad, in_gain_grad = input_back(
        dq, kv_grad, kv_back, k_raw, cosine, sine, layer_input, state_grad, k_gain, in_gain,
        query_w + (key_weight, value_weight),
    )
    kv_s = start([([xn], dkv)], 0, 2 * HD)
    later(kv_s.out, up_s)
    u2 = cut(up_s, 2 * third, third)
    (wait,) = phase(
        [in_gain_grad], end=[u1, d2, output_s], go=[u2, kv_s], now=[query_s, g1]
    )
    middle = Joint([g2, u1])
    (wait,) = phase([wait], go=[middle])
    gains = [wait, post_grad, pre_grad, end_grad0 + end_grad1, q_gain_grad, k_gain_grad]
    gains = [g.reshape(dp_size, -1) for g in gains]
    widths = [g.shape[1] for g in gains]
    block = layer_input.shape[1] // dp_size
    packed = jnp.concatenate(gains, axis=1)
    packed = jnp.pad(packed, ((0, 0), (0, block * 64 - packed.shape[1])))
    packed = packed.reshape(dp_size // 2, block, 128).astype(LOW)
    gains_s = Scatter(dp_size, dp_index, rest, leading, [(packed, leading, 0)], 128)
    wait, query_s.got, kv_s.got, u2.got, gains_s.out = tie(
        wait, query_s.got, kv_s.got, u2.got, gains_s.out
    )
    for s in (query_s, kv_s, u2):
        s.take().load()
    tail = Joint([output_s, query_s, kv_s, gains_s])
    (wait,) = phase([wait], end=[g1], go=[tail, u2], now=[middle])
    (wait,) = phase([wait], end=[middle], now=[tail, u2])
    (wait,) = phase([wait], end=[u2], now=[tail])
    (wait,) = phase([wait], end=[tail])
    down_part = jnp.concatenate([d1.finish(), d2.finish()], axis=1)
    gate_part = jnp.concatenate([g1.finish(), g2.finish()], axis=1)
    up_part = jnp.concatenate([u1.finish(), u2.finish()], axis=1)
    output_part = output_s.finish()
    query_part = query_s.finish()
    packed = gains_s.finish()
    pick = lambda which: lax.dynamic_slice_in_dim(packed, which * (block // 2), block // 2, axis=0)
    packed = pick(core) + lax.ppermute(pick(1 - core), "dp", core_pairs)
    packed = jnp.pad(packed, ((0, block - block // 2), (0, 0)))
    kv_sum = jnp.concatenate([kv_s.finish(), packed], axis=1)
    kv_sum = kv_sum + swap_head(kv_sum.astype(LOW)).astype(F32)
    packed = kv_sum[:, 2 * HD :].reshape(-1)
    pieces = []
    at = 0
    for size in widths:
        pieces.append(packed[at : at + size])
        at += size
    return (
        layer_output,
        input_grad,
        pieces[0],
        query_part,
        kv_sum[:, :HD],
        kv_sum[:, HD : 2 * HD],
        pieces[4],
        pieces[5],
        output_part,
        pieces[1],
        pieces[2],
        gate_part,
        up_part,
        down_part,
        pieces[3],
    )


def solution(mesh):
    placed = (
        P(("dp", "head"), None),
        P("dp", None),
        P(),
        P(None, "head"),
        P(),
        P(),
        P(),
        P(),
        P(None, "head"),
        P(),
        P(),
        P(None, "head"),
        P(None, "head"),
        P(None, "head"),
        P(),
        P(("dp", "head"), None),
    )
    return jax.shard_map(
        on_device,
        mesh=mesh,
        in_specs=placed,
        out_specs=(
            P(("dp", "head"), None),
            P(("dp", "head"), None),
            P("dp"),
            P("dp", "head"),
            P("dp", None),
            P("dp", None),
            P("dp"),
            P("dp"),
            P("dp", "head"),
            P("dp"),
            P("dp"),
            P("dp", "head"),
            P("dp", "head"),
            P("dp", "head"),
            P("dp"),
        ),
        check_vma=False,
    )
```
